32 devices in a mesh: seq: 8 (over z, y), tp: 4 (over x, core).
Axes of the slice: x: 2, y: 2, z: 4, core: 2. Of those that a mesh axis runs over, the one named last changes fastest.
Arguments:
- inputs: bfloat16 [8192, 1024], P(('seq', 'tp')), may hold values from -6 to 6
- ln_gains: float32 [5, 1024], replicated, may hold values from 0.5 to 1.5
- ffn1_in: bfloat16 [1024, 4096], P('seq', 'tp'), may hold values from -0.1875 to 0.1875
- ffn1_out: bfloat16 [4096, 1024], P(('tp', 'seq')), may hold values from -0.1875 to 0.1875
- qkv_weight: bfloat16 [1024, 3, 1024], P('seq', None, 'tp'), may hold values from -0.1875 to 0.1875
- attn_out: bfloat16 [1024, 1024], P(('tp', 'seq')), may hold values from -1.5 to 1.5
- conv_in: bfloat16 [1024, 2, 1024], P('seq', None, 'tp'), may hold values from -0.1875 to 0.1875
- conv_depth: float32 [5, 1024], P(None, 'tp'), may hold values from -2.5 to 2.5
- bn_gain: float32 [1024], P('tp'), may hold values from 0.5 to 1.5
- bn_bias: float32 [1024], P('tp'), may hold values from -3 to 3
- conv_out: bfloat16 [1024, 1024], P(('tp', 'seq')), may hold values from -0.25 to 0.25
- ffn2_in: bfloat16 [1024, 4096], P('seq', 'tp'), may hold values from -0.1875 to 0.1875
- ffn2_out: bfloat16 [4096, 1024], P(('tp', 'seq')), may hold values from -0.1875 to 0.1875
- segment_ids: int32 [8192], replicated, may hold values from 0 to 9, never falling along the last dimension, each value on 1 to 1536 neighbouring positions
- pad_mask: int32 [8192], replicated, may hold values 0 or 1
- out_grad: bfloat16 [8192, 1024], P(('seq', 'tp')), may hold values from -6 to 6
Outputs:
- output: bfloat16 [8192, 1024], P(('seq', 'tp'))
- input_grad: float32 [8192, 1024], P(('seq', 'tp'))
- grad_ln_gains: float32 [5, 1024], replicated
- grad_ffn1_in: float32 [1024, 4096], P('seq', 'tp')
- grad_ffn1_out: float32 [4096, 1024], P(('tp', 'seq'))
- grad_qkv_weight: float32 [1024, 3, 1024], P('seq', None, 'tp')
- grad_attn_out: float32 [1024, 1024], P(('tp', 'seq'))
- grad_conv_in: float32 [1024, 2, 1024], P('seq', None, 'tp')
- grad_conv_depth: float32 [5, 1024], P(None, 'tp')
- grad_bn_gain: float32 [1024], P('tp')
- grad_bn_bias: float32 [1024], P('tp')
- grad_conv_out: float32 [1024, 1024], P(('tp', 'seq'))
- grad_ffn2_in: float32 [1024, 4096], P('seq', 'tp')
- grad_ffn2_out: float32 [4096, 1024], P(('tp', 'seq'))
The draws below stay inside these ranges and needn't reach their ends.
Inputs may be any that keep to these rules, and one draw needn't show every extreme that they name: `segment_ids`: ids never fall along the frames; each utterance has 1 to 1536 frames, one exactly 1536.
All inputs are finite; a program needn't handle non-finite values.
Results may differ from the reference program's by a relative error of at most 0.034.
Values may be sent and summed in bfloat16 or wider, within the bound.
A program may use at most 192 MiB of HBM per device.

```python
import math
import jax
import jax.numpy as jnp
import numpy as np
from jax import lax

D = 1024
FF = 4096
HEADS = 8
HEAD_DIM = 128
KERNEL = 5
TOK_DEV = 1024
TOKENS = 8192
MAXLEN = 1536
SEGS = 10


def with_ends(drawn, own_key, low, top_value):
    longest = drawn.shape.index(max(drawn.shape))
    spots = []
    for shift in (0, 1):
        where = [jax.random.randint(jax.random.fold_in(own_key, axis), (), 0, length) for axis, length in enumerate(drawn.shape)]
        where[longest] = (where[longest] + shift) % drawn.shape[longest]
        spots.append(tuple(where))
    return drawn.at[spots[0]].set(low).at[spots[1]].set(top_value)


def level_of(stream_key, shape, cuts, smallest, high):
    level, own = 1.0, jax.random.fold_in(stream_key, 6)
    for axis_at, shards_of in cuts:
        draws = jnp.exp(jax.random.uniform(jax.random.fold_in(own, axis_at), (shards_of,), jnp.float32, smallest / len(cuts), high / len(cuts)))
        level = level * jnp.repeat(draws, shape[axis_at] // shards_of).reshape([-1 if axis == axis_at else 1 for axis in range(len(shape))])
    return level


def length_profile(number_of, total, limit, skew):
    portions = [(1 << 20) // math.isqrt(rank ** skew) + 1 for rank in range(2, number_of + 1)]
    rest, holding = total - limit - (number_of - 1), [1] * (number_of - 1)
    while rest > 0:
        free = [i for i in range(number_of - 1) if holding[i] < limit]
        pool, left = sum([portions[i] for i in free]), rest
        for i in free:
            addition = min(limit - holding[i], max(1, left * portions[i] // pool), rest)
            holding[i] = holding[i] + addition
            rest = rest - addition
    return np.array([limit] + holding)


def uneven(rng, amount, total, limit, skew):
    if amount == 2:
        one = jax.random.randint(rng, (), max(1, total - limit), min(limit, total - 1) + 1)
        return jnp.stack([one, total - one])
    lengths = jnp.asarray(length_profile(amount, total, limit, skew), jnp.int32)
    couples = (amount - 1) // 2
    donor, receiver = lengths[1:1 + 2 * couples:2], lengths[2:2 + 2 * couples:2]
    room = jnp.minimum(donor - 1, limit - receiver)
    moved = jax.random.randint(jax.random.fold_in(rng, 1), (couples,), 0, 1 << 20) % (room + 1)
    lengths = lengths.at[1:1 + 2 * couples:2].set(donor - moved).at[2:2 + 2 * couples:2].set(receiver + moved)
    return lengths[jax.random.permutation(jax.random.fold_in(rng, 2), amount)]


def gaussian(rng, shape, scale, reach, cuts=(), held_as=jnp.bfloat16):
    array = scale * jax.random.normal(rng, shape, jnp.float32)
    if cuts:
        array = array * level_of(rng, shape, cuts, -0.22, 0.18)
    return jnp.clip(array, -reach, reach).astype(held_as)


def setup_inputs(seed: int = 0) -> dict:
    streams_of = jax.random.split(jax.random.key(seed), 17)
    inputs = gaussian(streams_of[0], (TOKENS, D), 1.0, 6.0, ((0, 32),))
    ln_gains = jnp.clip(1.0 + 0.1 * jax.random.normal(streams_of[1], (5, D), jnp.float32), 0.5, 1.5)
    ffn1_in = gaussian(streams_of[2], (D, FF), D ** -0.5, 0.1875, ((0, 8), (1, 4)))
    ffn1_out = gaussian(streams_of[3], (FF, D), (FF // 4) ** -0.5, 0.1875, ((0, 32),))
    qkv_weight = gaussian(streams_of[4], (D, 3, D), D ** -0.5, 0.1875, ((0, 8), (2, 4)))
    attn_out = gaussian(streams_of[5], (D, D), (D // 64) ** -0.5, 1.5, ((0, 32),))
    conv_in = gaussian(streams_of[6], (D, 2, D), D ** -0.5, 0.1875, ((0, 8), (2, 4)))
    conv_depth = gaussian(streams_of[7], (KERNEL, D), KERNEL ** -0.5, 2.5, ((1, 4),), jnp.float32)
    bn_gain = jnp.clip(1.0 + 0.1 * jax.random.normal(streams_of[8], (D,), jnp.float32), 0.5, 1.5)
    bn_bias = gaussian(streams_of[9], (D,), 0.5, 3.0, ((0, 4),), jnp.float32)
    conv_out = gaussian(streams_of[10], (D, D), (D // 2) ** -0.5, 0.25, ((0, 32),))
    ffn2_in = gaussian(streams_of[11], (D, FF), D ** -0.5, 0.1875, ((0, 8), (1, 4)))
    ffn2_out = gaussian(streams_of[12], (FF, D), (FF // 4) ** -0.5, 0.1875, ((0, 32),))
    segment_ids = jnp.searchsorted(jnp.cumsum(uneven(streams_of[13], SEGS, TOKENS, MAXLEN, 2)), jnp.arange(TOKENS), side="right").astype(jnp.int32)
    pad_mask = with_ends((jax.random.randint(streams_of[14], (TOKENS,), 0, 8) < 7).astype(jnp.int32), jax.random.fold_in(streams_of[14], 1), 0, 1)
    out_grad = gaussian(streams_of[15], (TOKENS, D), 1.0, 6.0, ((0, 32),))
    return {"inputs": inputs, "ln_gains": ln_gains, "ffn1_in": ffn1_in, "ffn1_out": ffn1_out, "qkv_weight": qkv_weight, "attn_out": attn_out, "conv_in": conv_in, "conv_depth": conv_depth, "bn_gain": bn_gain, "bn_bias": bn_bias, "conv_out": conv_out, "ffn2_in": ffn2_in, "ffn2_out": ffn2_out, "segment_ids": segment_ids, "pad_mask": pad_mask, "out_grad": out_grad}


@jax.custom_vjp
def low(v):
    return lax.optimization_barrier(v.astype(jnp.bfloat16)).astype(jnp.float32)

@jax.custom_vjp
def low_back(v):
    return v

def low_keep(v):
    return (low(v), None)

def low_pass(kept, grad):
    return (grad,)

def back_keep(v):
    return (v, None)

def back_low(kept, grad):
    return (low(grad),)
low.defvjp(low_keep, low_pass)
low_back.defvjp(back_keep, back_low)
EPSILON = 1e-05
PRECISE = lax.Precision.HIGHEST

def matmul(left, right):
    return jnp.dot(left, right, precision=PRECISE, preferred_element_type=jnp.float32)

def norm_rows(values, gain_row):
    centred = values - lax.optimization_barrier(jnp.mean(values, axis=-1, keepdims=True))
    spread = lax.optimization_barrier(jnp.mean(centred * centred, axis=-1, keepdims=True))
    return centred * lax.rsqrt(spread + EPSILON) * gain_row

def swish(values):
    return values * jax.nn.sigmoid(values)

def feed_forward(values, gain_row, weight_in, weight_out):
    normed = low(norm_rows(values, gain_row))
    hidden = low_back(matmul(normed, weight_in))
    return low_back(matmul(low(swish(hidden)), weight_out))

def attention(values, gain_row, weight_qkv, weight_out, segment_ids, pad_mask):
    normed = low(norm_rows(values, gain_row))
    total = values.shape[0]
    width = values.shape[1]
    projected = matmul(normed, weight_qkv.reshape(width, 3 * width))
    queries = low_back(low(projected[:, :width]))
    keys = low_back(low(projected[:, width:2 * width]))
    vals = low_back(low(projected[:, 2 * width:]))
    height = min(512, TOK_DEV)
    window = height + 2 * MAXLEN
    keys_wide = jnp.pad(keys, ((MAXLEN, MAXLEN), (0, 0)))
    vals_wide = jnp.pad(vals, ((MAXLEN, MAXLEN), (0, 0)))
    seg_wide = jnp.pad(segment_ids, (MAXLEN, MAXLEN), constant_values=-1)
    real_wide = jnp.pad(pad_mask, (MAXLEN, MAXLEN))
    factor = 1.0 / math.sqrt(HEAD_DIM)

    def one_block(begin):
        query_rows = lax.dynamic_slice_in_dim(queries, begin, height, 0).reshape(height, HEADS, HEAD_DIM)
        key_rows = lax.dynamic_slice_in_dim(keys_wide, begin, window, 0).reshape(window, HEADS, HEAD_DIM)
        value_rows = lax.dynamic_slice_in_dim(vals_wide, begin, window, 0).reshape(window, HEADS, HEAD_DIM)
        query_seg = lax.dynamic_slice_in_dim(segment_ids, begin, height)
        key_seg = lax.dynamic_slice_in_dim(seg_wide, begin, window)
        key_real = lax.dynamic_slice_in_dim(real_wide, begin, window)
        query_place = begin + jnp.arange(height, dtype=jnp.int32)
        key_place = begin - MAXLEN + jnp.arange(window, dtype=jnp.int32)
        allowed = (query_seg[:, None] == key_seg[None, :]) & ((key_real[None, :] == 1) | (query_place[:, None] == key_place[None, :]))
        scores_raw = jnp.einsum('qhd,khd->hqk', query_rows, key_rows, precision=PRECISE)
        scores = jnp.where(allowed[None], low_back(scores_raw) * factor, -1e+30)
        highest = lax.optimization_barrier(jnp.max(scores, axis=-1, keepdims=True))
        weights = jnp.exp(scores - highest)
        probs = weights / lax.optimization_barrier(jnp.sum(weights, axis=-1, keepdims=True))
        mixed = jnp.einsum('hqk,khd->qhd', low(probs), value_rows, precision=PRECISE)
        return mixed.reshape(height, width)
    begins = jnp.arange(total // height, dtype=jnp.int32) * height
    blocks = lax.map(jax.checkpoint(one_block), begins)
    mixed = low_back(low(blocks.reshape(total, width)))
    return low_back(matmul(mixed, weight_out))

def convolve(values, gain_row, weight_pair, depth, bn_gain, bn_bias, weight_out, segment_ids, pad_mask):
    normed = low(norm_rows(values, gain_row))
    total = values.shape[0]
    width = values.shape[1]
    paired = matmul(normed, weight_pair.reshape(width, 2 * width))
    linear = low_back(paired[:, :width])
    gating = low_back(paired[:, width:])
    real = pad_mask.astype(jnp.float32)[:, None]
    gated = low(linear * jax.nn.sigmoid(gating) * real)
    half = KERNEL // 2
    gated_wide = jnp.pad(gated, ((half, half), (0, 0)))
    seg_wide = jnp.pad(segment_ids, (half, half), constant_values=-1)
    conv = jnp.zeros_like(gated)
    for tap_index in range(KERNEL):
        same_seg = (seg_wide[tap_index:tap_index + total] == segment_ids).astype(jnp.float32)[:, None]
        conv = conv + depth[tap_index] * gated_wide[tap_index:tap_index + total] * same_seg
    frames_real = jnp.sum(real)
    centre = lax.optimization_barrier(jnp.sum(real * conv, axis=0)) / frames_real
    deviation = conv - centre
    spread = lax.optimization_barrier(jnp.sum(real * deviation * deviation, axis=0)) / frames_real
    normal = deviation * lax.rsqrt(spread + EPSILON)
    batch = normal * bn_gain + bn_bias
    return low_back(matmul(low(swish(batch)), weight_out))

def layer(inputs, ln_gains, ffn1_in, ffn1_out, qkv_weight, attn_out, conv_in, conv_depth, bn_gain, bn_bias, conv_out, ffn2_in, ffn2_out, segment_ids, pad_mask):
    first = inputs + 0.5 * feed_forward(inputs, ln_gains[0], ffn1_in, ffn1_out)
    second = first + attention(first, ln_gains[1], qkv_weight, attn_out, segment_ids, pad_mask)
    third = second + convolve(second, ln_gains[2], conv_in, conv_depth, bn_gain, bn_bias, conv_out, segment_ids, pad_mask)
    fourth = third + 0.5 * feed_forward(third, ln_gains[3], ffn2_in, ffn2_out)
    return norm_rows(fourth, ln_gains[4])

def reference(inputs, ln_gains, ffn1_in, ffn1_out, qkv_weight, attn_out, conv_in, conv_depth, bn_gain, bn_bias, conv_out, ffn2_in, ffn2_out, segment_ids, pad_mask, out_grad):
    floats = tuple((item.astype(jnp.float32) for item in (inputs, ln_gains, ffn1_in, ffn1_out, qkv_weight, attn_out, conv_in, conv_depth, bn_gain, bn_bias, conv_out, ffn2_in, ffn2_out)))

    def forward(*params):
        return layer(*params, segment_ids, pad_mask)
    result, pullback = jax.vjp(forward, *floats)
    grads = pullback(out_grad.astype(jnp.float32))
    return (result.astype(jnp.bfloat16), grads[0], grads[1], grads[2], grads[3], grads[4], grads[5], grads[6], grads[7], grads[8], grads[9], grads[10], grads[11], grads[12])
```

```python
import math
from types import SimpleNamespace

import jax
import jax.numpy as jnp
from jax import lax
from jax.experimental import pallas as pl
from jax.experimental.pallas import tpu as pltpu
from jax.sharding import PartitionSpec as P

HEAD_DIM = 128
KERNEL = 5
MAXLEN = 1536
EPSILON = 1e-05
CHUNKS = 2
EDGE = 8
VMEM_LIMIT = 62 << 20
QUERY_BLOCK = 256
KEY_BLOCK = 512
SCORE_SCALE = 1.0 / math.sqrt(HEAD_DIM)
LOG2E = 1.4426950408889634
BF16 = jnp.bfloat16
F32 = jnp.float32
IN_VMEM = pl.BlockSpec(memory_space=pltpu.VMEM)
IN_PLACE = pl.BlockSpec(memory_space=pl.ANY)


def plain_product(left, right):
    return jnp.dot(left, right, preferred_element_type=F32)


def inner_product(left, right):
    return lax.dot_general(left, right, (((0,), (0,)), ((), ())), preferred_element_type=F32)


def across_product(left, right):
    return lax.dot_general(left, right, (((1,), (1,)), ((), ())), preferred_element_type=F32)


def swish(values):
    return values * jax.nn.sigmoid(values)


def standard_rows(values):
    centred = values - jnp.mean(values, axis=-1, keepdims=True)
    spread = jnp.mean(centred * centred, axis=-1, keepdims=True)
    inverse = lax.rsqrt(spread + EPSILON)
    return (centred * inverse, inverse)


def norm_rows(values, gain_row):
    return standard_rows(values)[0] * gain_row


def norm_back(values, gain_row, grads):
    normal, inverse = standard_rows(values)
    scaled = grads * gain_row
    result = inverse * (
        scaled
        - jnp.mean(scaled, axis=-1, keepdims=True)
        - normal * jnp.mean(scaled * normal, axis=-1, keepdims=True)
    )
    return (result, jnp.sum(grads * normal, axis=0, keepdims=True))


def flip(index, bit):
    return index + bit - 2 * bit * lax.rem(lax.div(index, bit), 2)


def span(begin, size):
    return pl.ds(pl.multiple_of(begin, size), size)


def static_span(begin, size):
    return pl.ds(begin, size)


def remote(source, target, send, receive, peer):
    return pltpu.make_async_remote_copy(
        src_ref=source,
        dst_ref=target,
        send_sem=send,
        recv_sem=receive,
        device_id=peer,
        device_id_type=pl.DeviceIdType.MESH,
    )


def tp_peers():
    me = lax.axis_index("tp")
    return [{"tp": flip(me, 1)}, {"tp": flip(me, 2)}]


def seq_peers():
    me, count = lax.axis_index("seq"), lax.axis_size("seq")
    return [{"seq": lax.rem(me + step, count)} for step in range(1, count)]


def greet(peers):
    barrier = pltpu.get_barrier_semaphore()
    for peer in peers:
        pl.semaphore_signal(barrier, inc=1, device_id=peer, device_id_type=pl.DeviceIdType.MESH)
    return lambda: pl.semaphore_wait(barrier, len(peers))


def owner(slot):
    me = lax.axis_index("tp")
    if slot & 1:
        me = flip(me, 1)
    if slot & 2:
        me = flip(me, 2)
    return me


def tiles(total, tile, body):
    def one(index, nothing):
        body(span(index * tile, tile))
        return nothing

    lax.fori_loop(0, total // tile, one, 0)


class Gather:
    def __init__(self, rows, send, receive):
        self.near, self.far = tp_peers()
        self.height = rows.shape[0] // 4
        self.piece = self.height // CHUNKS
        self.rows, self.send, self.receive = rows, send, receive

    def part(self, slot, chunk):
        return self.rows.at[pl.ds(slot * self.height + chunk * self.piece, self.piece), :]

    def hop(self, kind, chunk):
        source, target = ((0, 1), (0, 2), (2, 3))[kind]
        return remote(
            self.part(source, chunk),
            self.part(target, chunk),
            self.send.at[kind, chunk],
            self.receive.at[kind, chunk],
            self.far if kind == 1 else self.near,
        )

    def start(self, chunk):
        self.hop(1, chunk).start()
        self.hop(0, chunk).start()

    def wait_near(self):
        for chunk in range(CHUNKS):
            self.hop(0, chunk).wait_recv()

    def pass_on(self, chunk):
        self.hop(1, chunk).wait_recv()
        self.hop(2, chunk).start()

    def wait_last(self, chunk):
        self.hop(2, chunk).wait_recv()

    def finish(self):
        for chunk in range(CHUNKS):
            for kind in range(3):
                self.hop(kind, chunk).wait_send()


def gather_scratch():
    return dict(send=pltpu.SemaphoreType.DMA((3, CHUNKS)), receive=pltpu.SemaphoreType.DMA((3, CHUNKS)))


class Scatter:
    def __init__(self, own, passing, outgoing, incoming, send, receive):
        self.near, self.far = tp_peers()
        self.height = own.shape[0]
        self.piece = self.height // CHUNKS
        self.own, self.passing = own, passing
        self.outgoing, self.incoming, self.send, self.receive = outgoing, incoming, send, receive

    def rows(self, chunk):
        return pl.ds(chunk * self.piece, self.piece)

    def copy(self, kind, chunk):
        here = self.rows(chunk)
        return remote(
            self.outgoing.at[kind, here, :],
            self.incoming.at[kind, here, :],
            self.send.at[kind, chunk],
            self.receive.at[kind, chunk],
            self.far if kind == 2 else self.near,
        )

    def start(self, kind):
        for chunk in range(CHUNKS):
            self.copy(kind, chunk).start()

    def relay(self, chunk):
        here = self.rows(chunk)
        self.copy(1, chunk).wait_recv()
        self.outgoing[2, here, :] = (self.passing[here, :] + self.incoming[1, here, :].astype(F32)).astype(BF16)
        self.copy(2, chunk).start()

    def total(self, chunk):
        here = self.rows(chunk)
        self.copy(0, chunk).wait_recv()
        self.copy(2, chunk).wait_recv()
        return self.own[here, :] + self.incoming[0, here, :].astype(F32) + self.incoming[2, here, :].astype(F32)

    def spread(self, product, width, tile=512):
        height = self.height

        def far(cols):
            term = product((2, 3), cols)
            self.passing[:, cols] = term[:height]
            self.outgoing[1, :, cols] = term[height:].astype(BF16)

        tiles(width, tile, far)
        self.start(1)

        def near(cols):
            term = product((0, 1), cols)
            self.own[:, cols] = term[:height]
            self.outgoing[0, :, cols] = term[height:].astype(BF16)

        tiles(width, tile, near)
        for chunk in range(CHUNKS):
            self.relay(chunk)
        self.start(0)

    def finish(self):
        for kind in range(3):
            for chunk in range(CHUNKS):
                self.copy(kind, chunk).wait_send()


def scatter_scratch(height, width):
    return dict(
        own=pltpu.VMEM((height, width), F32),
        passing=pltpu.VMEM((height, width), F32),
        outgoing=pltpu.VMEM((3, height, width), BF16),
        incoming=pltpu.VMEM((3, height, width), BF16),
        send=pltpu.SemaphoreType.DMA((3, CHUNKS)),
        receive=pltpu.SemaphoreType.DMA((3, CHUNKS)),
    )


class Collect:
    def __init__(self, shard, full, send, receive, pair_send, pair_receive, local):
        self.me, self.count = lax.axis_index("seq"), lax.axis_size("seq")
        self.groups = self.count // 2
        self.pair = {"seq": flip(self.me, 1)}
        self.shard, self.full, self.height = shard, full, shard.shape[0]
        self.send, self.receive, self.pair_send, self.pair_receive = send, receive, pair_send, pair_receive
        self.local = pltpu.make_async_copy(shard, self.block(self.me), local.at[0])

    def block(self, index):
        return self.full.at[span(index * self.height, self.height), :]

    def out(self, step):
        peer = {"seq": lax.rem(self.me + 2 * step, self.count)}
        return remote(self.shard, self.block(self.me), self.send.at[step - 1], self.receive.at[step - 1], peer)

    def over(self, step):
        if step == 0:
            source, place = self.shard, self.me
        else:
            place = lax.rem(self.me + self.count - 2 * step, self.count)
            source = self.block(place)
        return remote(source, self.block(place), self.pair_send.at[step], self.pair_receive.at[step], self.pair)

    def begin(self):
        for step in range(1, self.groups):
            self.out(step).start()
        self.over(0).start()
        self.local.start()

    def middle(self):
        for step in range(1, self.groups):
            self.out(step).wait_recv()
            self.over(step).start()

    def end(self):
        self.local.wait()
        for step in range(self.groups):
            self.over(step).wait_recv()

    def finish(self):
        for step in range(self.groups):
            self.over(step).wait_send()
            if step:
                self.out(step).wait_send()


def collect_scratch():
    groups = lax.axis_size("seq") // 2
    return dict(
        send=pltpu.SemaphoreType.DMA((groups,)),
        receive=pltpu.SemaphoreType.DMA((groups,)),
        pair_send=pltpu.SemaphoreType.DMA((groups,)),
        pair_receive=pltpu.SemaphoreType.DMA((groups,)),
        local=pltpu.SemaphoreType.DMA((1,)),
    )


class Settle:
    def __init__(self, source, result, half, partner, others, load, send, receive, far_send, far_receive):
        self.me, self.count = lax.axis_index("seq"), lax.axis_size("seq")
        self.groups = self.count // 2
        self.other = flip(self.me, 1)
        self.source, self.result, self.half, self.partner, self.others = source, result, half, partner, others
        self.height = result.shape[0]
        self.load, self.send, self.receive = load, send, receive
        self.far_send, self.far_receive = far_send, far_receive

    def block(self, base, step):
        place = lax.rem(base + 2 * step, self.count)
        return self.source.at[span(place * self.height, self.height), :]

    def swap(self, step):
        return remote(
            self.block(self.other, step),
            self.partner.at[step],
            self.send.at[step],
            self.receive.at[step],
            {"seq": self.other},
        )

    def fetch(self, step):
        return pltpu.make_async_copy(self.block(self.me, step), self.half.at[step], self.load.at[step])

    def away(self, step):
        peer = {"seq": lax.rem(self.me + 2 * step, self.count)}
        return remote(
            self.half.at[step], self.others.at[step], self.far_send.at[step], self.far_receive.at[step], peer
        )

    def begin(self):
        for step in list(range(1, self.groups)) + [0]:
            self.swap(step).start()
            self.fetch(step).start()

    def middle(self):
        for step in range(1, self.groups):
            self.fetch(step).wait()
            self.swap(step).wait_recv()
            self.half[step] = (self.half[step].astype(F32) + self.partner[step].astype(F32)).astype(BF16)
            self.away(step).start()

    def end(self):
        self.fetch(0).wait()
        self.swap(0).wait_recv()
        total = self.half[0].astype(F32) + self.partner[0].astype(F32)
        for step in range(1, self.groups):
            self.away(step).wait_recv()
            total = total + self.others[step].astype(F32)
        self.result[...] = total

    def finish(self):
        for step in range(self.groups):
            self.swap(step).wait_send()
            if step:
                self.away(step).wait_send()


def settle_scratch(height, width):
    groups = lax.axis_size("seq") // 2
    return dict(
        half=pltpu.VMEM((groups, height, width), BF16),
        partner=pltpu.VMEM((groups, height, width), BF16),
        others=pltpu.VMEM((groups, height, width), BF16),
        load=pltpu.SemaphoreType.DMA((groups,)),
        send=pltpu.SemaphoreType.DMA((groups,)),
        receive=pltpu.SemaphoreType.DMA((groups,)),
        far_send=pltpu.SemaphoreType.DMA((groups,)),
        far_receive=pltpu.SemaphoreType.DMA((groups,)),
    )


class Swap:
    def __init__(self, blocks, send, receive):
        self.me, self.count = lax.axis_index("seq"), lax.axis_size("seq")
        self.blocks, self.send, self.receive = blocks, send, receive

    def copy(self, step):
        peer = {"seq": lax.rem(self.me + step, self.count)}
        return remote(self.blocks.at[0], self.blocks.at[step], self.send.at[step], self.receive.at[step], peer)

    def start(self):
        for step in range(1, self.count):
            self.copy(step).start()

    def wait(self):
        for step in range(1, self.count):
            self.copy(step).wait_recv()

    def finish(self):
        for step in range(1, self.count):
            self.copy(step).wait_send()


def swap_scratch(height, width):
    count = lax.axis_size("seq")
    return dict(
        blocks=pltpu.VMEM((count, height, width), F32),
        send=pltpu.SemaphoreType.DMA((count,)),
        receive=pltpu.SemaphoreType.DMA((count,)),
    )


class Edges:
    def __init__(self, padded, send, receive):
        self.me, self.count = lax.axis_index("seq"), lax.axis_size("seq")
        self.padded, self.send, self.receive = padded, send, receive
        self.frames = padded.shape[0] - 2 * EDGE

    def up(self):
        source = self.padded.at[pl.ds(self.frames, EDGE), :]
        target = self.padded.at[pl.ds(0, EDGE), :]
        peer = {"seq": lax.rem(self.me + 1, self.count)}
        return remote(source, target, self.send.at[0], self.receive.at[0], peer)

    def down(self):
        source = self.padded.at[pl.ds(EDGE, EDGE), :]
        target = self.padded.at[pl.ds(EDGE + self.frames, EDGE), :]
        peer = {"seq": lax.rem(self.me + self.count - 1, self.count)}
        return remote(source, target, self.send.at[1], self.receive.at[1], peer)

    def start(self):
        self.up().start()
        self.down().start()

    def wait(self):
        self.up().wait_recv()
        self.down().wait_recv()

    def finish(self):
        self.up().wait_send()
        self.down().wait_send()


def edges_scratch():
    return dict(send=pltpu.SemaphoreType.DMA((2,)), receive=pltpu.SemaphoreType.DMA((2,)))


def run_kernel(body, number, inputs, outputs, scratch, flops=1 << 33):
    flat, groups = [], []
    for name, item in scratch.items():
        parts = item if isinstance(item, dict) else {None: item}
        groups.append((name, list(parts)))
        flat.extend(parts.values())

    def kernel(*refs):
        given = dict(zip(list(inputs) + list(outputs), refs))
        rest = list(refs[len(given) :])
        for name, keys in groups:
            taken = {key: rest.pop(0) for key in keys}
            given[name] = taken[None] if None in taken else taken
        body(SimpleNamespace(**given))

    results = pl.pallas_call(
        kernel,
        out_shape=tuple(jax.ShapeDtypeStruct(shape, kind) for shape, kind, _ in outputs.values()),
        in_specs=[IN_VMEM if near else IN_PLACE for _, near in inputs.values()],
        out_specs=tuple(IN_VMEM if near else IN_PLACE for _, _, near in outputs.values()),
        scratch_shapes=flat,
        compiler_params=pltpu.CompilerParams(
            collective_id=number, has_side_effects=True, vmem_limit_bytes=VMEM_LIMIT
        ),
        cost_estimate=pl.CostEstimate(flops=flops, bytes_accessed=16 << 20, transcendentals=0),
    )(*[array for array, _ in inputs.values()])
    return SimpleNamespace(**dict(zip(outputs, results)))


def ffn_forward(gather, scatter, win, wout, hidden, active, wait_in, wait_out):
    rows, height, piece = gather.rows, gather.height, gather.piece
    width, inner = win.shape
    pair = pl.ds(0, 2 * height)
    gather.wait_near()
    wait_in()

    def first(cols):
        product = plain_product(rows[pair, :], win[:, cols])
        hidden[pair, cols] = product
        active[pair, cols] = swish(product).astype(BF16)

    tiles(inner, 512, first)
    gather.pass_on(0)
    wait_out()

    def second(cols):
        product = plain_product(active[pair, :], wout[:, cols])
        scatter.own[:, cols] = product[:height]
        scatter.outgoing[0, :, cols] = product[height:].astype(BF16)

    tiles(width, 512, second)
    scatter.start(0)
    for chunk in range(CHUNKS):
        if chunk > 0:
            gather.pass_on(chunk)
        gather.wait_last(chunk)
        low = pl.ds(2 * height + chunk * piece, piece)
        high = pl.ds(3 * height + chunk * piece, piece)
        here = scatter.rows(chunk)

        def third(cols):
            both = jnp.concatenate([rows[low, :], rows[high, :]], axis=0)
            product = plain_product(both, win[:, cols])
            hidden[low, cols] = product[:piece]
            hidden[high, cols] = product[piece:]
            alive = swish(product).astype(BF16)
            active[low, cols] = alive[:piece]
            active[high, cols] = alive[piece:]

        tiles(inner, 512, third)

        def fourth(cols):
            both = jnp.concatenate([active[low, :], active[high, :]], axis=0)
            product = plain_product(both, wout[:, cols])
            scatter.passing[here, cols] = product[:piece]
            scatter.outgoing[1, here, cols] = product[piece:].astype(BF16)

        tiles(width, 512, fourth)
        scatter.copy(1, chunk).start()
        scatter.relay(chunk)


def ffn_backward(gather, scatter, win, wout, hidden, active, slope, wait_out, wait_in):
    rows, height, piece = gather.rows, gather.height, gather.piece
    width, inner = win.shape
    pair = pl.ds(0, 2 * height)
    gather.wait_near()
    wait_out()

    def bend(product, before):
        logistic = jax.nn.sigmoid(before)
        return (
            (before * logistic).astype(BF16),
            (product * (logistic * (1.0 + before * (1.0 - logistic)))).astype(BF16),
        )

    def first(cols):
        alive, steep = bend(across_product(rows[pair, :], wout[cols, :]), hidden[pair, cols])
        if active is not None:
            active[pair, cols] = alive
        slope[pair, cols] = steep

    tiles(inner, 256, first)
    gather.pass_on(0)
    wait_in()

    def second(cols):
        product = across_product(slope[pair, :], win[cols, :])
        scatter.own[:, cols] = product[:height]
        scatter.outgoing[0, :, cols] = product[height:].astype(BF16)

    tiles(width, 512, second)
    scatter.start(0)
    for chunk in range(CHUNKS):
        if chunk > 0:
            gather.pass_on(chunk)
        gather.wait_last(chunk)
        low = pl.ds(2 * height + chunk * piece, piece)
        high = pl.ds(3 * height + chunk * piece, piece)
        here = scatter.rows(chunk)

        def third(cols):
            both = jnp.concatenate([rows[low, :], rows[high, :]], axis=0)
            before = jnp.concatenate([hidden[low, cols], hidden[high, cols]], axis=0)
            alive, steep = bend(across_product(both, wout[cols, :]), before)
            if active is not None:
                active[low, cols] = alive[:piece]
                active[high, cols] = alive[piece:]
            slope[low, cols] = steep[:piece]
            slope[high, cols] = steep[piece:]

        tiles(inner, 256, third)

        def fourth(cols):
            both = jnp.concatenate([slope[low, :], slope[high, :]], axis=0)
            product = across_product(both, win[cols, :])
            scatter.passing[here, cols] = product[:piece]
            scatter.outgoing[1, here, cols] = product[piece:].astype(BF16)

        tiles(width, 512, fourth)
        scatter.copy(1, chunk).start()
        scatter.relay(chunk)


def weight_products(result, left, right, tile=256):
    def one(cols):
        result[:, cols] = inner_product(left[...], right[:, cols]).astype(BF16)

    tiles(right.shape[1], tile, one)


def open_kernel(n):
    height, width = n.values.shape
    frames = 4 * height
    local = n.queries.shape[1]
    seq, count = lax.axis_index("seq"), lax.axis_size("seq")
    first_in = Collect(n.shard_in, n.win, **n.c_in)
    first_out = Collect(n.shard_out, n.wout, **n.c_out)
    project = Collect(n.shard_project, n.wproject, **n.c_project)
    later = [
        Collect(n.shard_attend, n.full_attend, **n.c_attend),
        Collect(n.shard_pair, n.full_pair, **n.c_pair),
        Collect(n.shard_conv, n.full_conv, **n.c_conv),
    ]
    gather = Gather(n.rows, **n.g1)
    scatter = Scatter(**n.s1)
    gather_two = Gather(n.rows_two, **n.g2)
    ready = greet(tp_peers() + seq_peers())
    n.rows[pl.ds(0, gather.piece), :] = norm_rows(
        n.values[pl.ds(0, gather.piece), :].astype(F32), n.gains[0:1, :]
    ).astype(BF16)
    ready()
    first_in.begin()
    first_out.begin()
    for chunk in range(CHUNKS):
        here = scatter.rows(chunk)
        if chunk > 0:
            n.rows[here, :] = norm_rows(n.values[here, :].astype(F32), n.gains[0:1, :]).astype(BF16)
        gather.start(chunk)
    first_in.middle()
    first_out.middle()
    project.begin()
    keeps = [
        pltpu.make_async_copy(n.win, n.full_in, n.keep.at[0]),
        pltpu.make_async_copy(n.wout, n.full_out, n.keep.at[1]),
        pltpu.make_async_copy(n.wproject, n.full_project, n.keep.at[2]),
    ]

    def wait_in():
        first_in.end()
        keeps[0].start()

    def wait_out():
        first_out.end()
        keeps[1].start()
        for task in later:
            task.begin()

    ffn_forward(gather, scatter, n.win, n.wout, n.hidden, n.active, wait_in, wait_out)
    project.middle()
    for chunk in range(CHUNKS):
        here = scatter.rows(chunk)
        n.first[here, :] = n.values[here, :].astype(F32) + 0.5 * scatter.total(chunk)
        n.rows_two[here, :] = norm_rows(n.first[here, :], n.gains[1:2, :]).astype(BF16)
        gather_two.start(chunk)
    for task in later:
        task.middle()
    project.end()
    keeps[2].start()
    gather_two.wait_near()

    def send_block(slot):
        place = owner(slot)
        source = n.pair_own.at[span(place * height, height), :]
        upper = lax.div(place, 2)

        def piece(kind):
            if kind == 0:
                peer, row = lax.rem(seq + 1, count), MAXLEN - frames + place * height
            elif kind == 1:
                peer, row = lax.rem(seq + count - 1, count), MAXLEN + frames + place * height
            else:
                peer = lax.rem(seq + count - 2 + 4 * upper, count)
                row = MAXLEN + place * height + 2 * frames * (1 - 2 * upper)
            target = n.window.at[span(row, height), :]
            return remote(source, target, n.halo_send.at[kind, slot], n.halo_receive.at[kind, slot], {"seq": peer})

        return [piece(kind) for kind in range(3)]

    def there(kind, slot, sending):
        upper = lax.div(owner(slot), 2)
        if kind == 2:
            shift = 4 * upper - 2
        else:
            shift = 1 - 2 * kind
        target = seq + shift if sending else seq - shift
        return (target >= 0) & (target < count)

    def project_rows(slots, low):
        for part in range(3):
            cols = pl.ds(part * local, local)
            product = plain_product(n.rows_two[low, :], n.wproject[:, cols]).astype(BF16)
            for index, slot in enumerate(slots):
                rows = product[index * height : (index + 1) * height]
                place = span(owner(slot) * height, height)
                if part == 0:
                    n.queries[place, :] = rows
                else:
                    n.pair_own[place, pl.ds((part - 1) * local, local)] = rows
        for slot in slots:
            for kind, copy in enumerate(send_block(slot)):

                @pl.when(there(kind, slot, True))
                def _():
                    copy.start()

    project_rows((0, 1), pl.ds(0, 2 * height))
    for chunk in range(CHUNKS):
        gather_two.pass_on(chunk)
    for chunk in range(CHUNKS):
        gather_two.wait_last(chunk)
    project_rows((2, 3), pl.ds(2 * height, 2 * height))
    own = pltpu.make_async_copy(n.pair_own, n.window.at[pl.ds(MAXLEN, frames), :], n.keep.at[3])
    own.start()
    for slot in range(4):
        for kind, copy in enumerate(send_block(slot)):

            @pl.when(there(kind, slot, False))
            def _():
                copy.wait_recv()

            @pl.when(there(kind, slot, True))
            def _():
                copy.wait_send()

    for task in later:
        task.end()
    for keep in keeps:
        keep.wait()
    own.wait()
    for item in [first_in, first_out, project, gather, scatter, gather_two] + later:
        item.finish()


def run_open(values, gains, shards):
    height, width = values.shape
    frames = 4 * height
    count = lax.axis_size("seq")
    inner, local = shards.ffn1_in.shape[1], shards.attend.shape[0] * count
    fulls = dict(
        full_in=shards.ffn1_in, full_out=shards.ffn1_out, full_project=shards.project,
        full_attend=shards.attend, full_pair=shards.pair, full_conv=shards.conv,
    )
    return run_kernel(
        open_kernel,
        0,
        dict(
            values=(values, True), gains=(gains, True), shard_in=(shards.ffn1_in, True),
            shard_out=(shards.ffn1_out, True), shard_project=(shards.project, True),
            shard_attend=(shards.attend, True), shard_pair=(shards.pair, True), shard_conv=(shards.conv, True),
        ),
        dict(
            first=((height, width), F32, True),
            rows=((frames, width), BF16, True),
            hidden=((frames, inner), F32, True),
            rows_two=((frames, width), BF16, True),
            queries=((frames, local), BF16, True),
            window=((frames + 2 * MAXLEN, 2 * local), BF16, False),
            **{name: ((item.shape[0] * count, item.shape[1]), BF16, False) for name, item in fulls.items()},
        ),
        dict(
            win=pltpu.VMEM((width, inner), BF16),
            wout=pltpu.VMEM((inner, width), BF16),
            wproject=pltpu.VMEM((width, 3 * local), BF16),
            active=pltpu.VMEM((frames, inner), BF16),
            pair_own=pltpu.VMEM((frames, 2 * local), BF16),
            c_in=collect_scratch(), c_out=collect_scratch(), c_project=collect_scratch(),
            c_attend=collect_scratch(), c_pair=collect_scratch(), c_conv=collect_scratch(),
            g1=gather_scratch(), s1=scatter_scratch(height, width), g2=gather_scratch(),
            halo_send=pltpu.SemaphoreType.DMA((3, 4)), halo_receive=pltpu.SemaphoreType.DMA((3, 4)),
            keep=pltpu.SemaphoreType.DMA((4,)),
        ),
    )


def slot_rows(slots, height):
    return pl.ds(slots[0] * height, 2 * height)


def in_order(swap):
    for place in range(swap.count):
        yield swap.blocks[lax.rem(swap.me + swap.count - place, swap.count)]


def conv_kernel(n):
    height, width = n.first.shape
    frames = 4 * height
    local = n.mixed.shape[1]
    fetches = [Collect(n.shard_in, n.full_in, **n.c_in), Collect(n.shard_out, n.full_out, **n.c_out)]
    scatter = Scatter(**n.s1)
    gather = Gather(n.rows, **n.g1)
    edges = Edges(n.gated, **n.edge)
    swap = Swap(**n.swap)
    scatter_two = Scatter(**n.s2)
    ready = greet(tp_peers() + seq_peers())
    for slot in range(4):
        n.mixed_low[pl.ds(slot * height, height), :] = n.mixed[span(owner(slot) * height, height), :].astype(BF16)
    ready()
    for task in fetches:
        task.begin()
    scatter.spread(
        lambda slots, cols: plain_product(n.mixed_low[slot_rows(slots, height), :], n.wattend[:, cols]), width
    )
    for chunk in range(CHUNKS):
        here = scatter.rows(chunk)
        n.second[here, :] = n.first[here, :] + scatter.total(chunk)
        n.rows[here, :] = norm_rows(n.second[here, :], n.gains[2:3, :]).astype(BF16)
        gather.start(chunk)
    gather.wait_near()

    def pair_rows(slots):
        product = plain_product(n.rows[slot_rows(slots, height), :], n.wpair[...])
        for index, slot in enumerate(slots):
            rows = product[index * height : (index + 1) * height]
            place = owner(slot) * height
            n.paired[span(place, height), :] = rows
            real = n.context[span(place, height), KERNEL : KERNEL + 1]
            gated = rows[:, :local] * jax.nn.sigmoid(rows[:, local:]) * real
            n.gated[pl.ds(pl.multiple_of(EDGE + place, EDGE), height), :] = gated.astype(BF16).astype(F32)

    pair_rows((0, 1))
    for chunk in range(CHUNKS):
        gather.pass_on(chunk)
    for chunk in range(CHUNKS):
        gather.wait_last(chunk)
    pair_rows((2, 3))
    edges.start()
    edges.wait()
    for task in fetches:
        task.middle()
    block = 128

    def convolve(index, carried):
        total, real_count = carried
        around = n.gated[pl.ds(pl.multiple_of(index * block, block), block + 2 * EDGE), :]
        marks = n.context[span(index * block, block), :]
        conv = jnp.zeros((block, local), F32)
        for tap in range(KERNEL):
            begin = EDGE - KERNEL // 2 + tap
            conv = conv + n.depth[tap : tap + 1, :] * around[begin : begin + block] * marks[:, tap : tap + 1]
        n.normal[span(index * block, block), :] = conv
        real = marks[:, KERNEL : KERNEL + 1]
        return (
            total + jnp.sum(real * conv, axis=0, keepdims=True),
            real_count + jnp.sum(jnp.broadcast_to(real, conv.shape), axis=0, keepdims=True),
        )

    none = jnp.zeros((1, local), F32)
    total, real_count = lax.fori_loop(0, frames // block, convolve, (none, none))
    middle = total / jnp.maximum(real_count, 1.0)

    def deviate(index, carried):
        conv = n.normal[span(index * block, block), :]
        real = n.context[span(index * block, block), KERNEL : KERNEL + 1]
        away = conv - middle
        return carried + jnp.sum(real * away * away, axis=0, keepdims=True)

    squares = lax.fori_loop(0, frames // block, deviate, none)
    swap.blocks[0, 0:1, :] = total
    swap.blocks[0, 1:2, :] = squares
    swap.blocks[0, 2:3, :] = real_count
    swap.start()
    swap.wait()
    total_all, real_all = none, none
    for item in in_order(swap):
        total_all = total_all + item[0:1]
        real_all = real_all + item[2:3]
    centre = total_all / real_all
    squares_all = none
    for item in in_order(swap):
        away = item[0:1] / jnp.maximum(item[2:3], 1.0) - centre
        squares_all = squares_all + item[1:2] + item[2:3] * away * away
    inverse = lax.rsqrt(squares_all / real_all + EPSILON)
    n.stats[0:1, :] = inverse
    n.stats[1:2, :] = real_all
    for slot in range(4):
        place = span(owner(slot) * height, height)
        normal = (n.normal[place, :] - centre) * inverse
        n.normal[place, :] = normal
        n.alive[pl.ds(slot * height, height), :] = swish(normal * n.bn_gain[...] + n.bn_bias[...]).astype(BF16)
    scatter_two.spread(
        lambda slots, cols: plain_product(n.alive[slot_rows(slots, height), :], n.wconv[:, cols]), width
    )
    for chunk in range(CHUNKS):
        here = scatter_two.rows(chunk)
        n.third[here, :] = n.second[here, :] + scatter_two.total(chunk)
    for task in fetches:
        task.end()
    for item in fetches + [scatter, gather, edges, swap, scatter_two]:
        item.finish()


def run_conv(mixed, first, gains, attend, context, depth, bn_gain, bn_bias, pair, conv, shard_in, shard_out):
    height, width = first.shape
    frames, local = mixed.shape
    count = lax.axis_size("seq")
    inner = shard_in.shape[1]
    return run_kernel(
        conv_kernel,
        1,
        dict(
            mixed=(mixed, True), first=(first, True), gains=(gains, True), wattend=(attend, True),
            context=(context, True), depth=(depth, True), bn_gain=(bn_gain, True), bn_bias=(bn_bias, True),
            wpair=(pair, True), wconv=(conv, True), shard_in=(shard_in, True), shard_out=(shard_out, True),
        ),
        dict(
            second=((height, width), F32, True),
            third=((height, width), F32, True),
            rows=((frames, width), BF16, True),
            mixed_low=((frames, local), BF16, True),
            paired=((frames, 2 * local), F32, True),
            gated=((frames + 2 * EDGE, local), F32, True),
            normal=((frames, local), F32, True),
            stats=((8, local), F32, True),
            alive=((frames, local), BF16, True),
            full_in=((shard_in.shape[0] * count, inner), BF16, False),
            full_out=((shard_out.shape[0] * count, width), BF16, False),
        ),
        dict(
            c_in=collect_scratch(), c_out=collect_scratch(),
            s1=scatter_scratch(height, width), g1=gather_scratch(), edge=edges_scratch(),
            swap=swap_scratch(8, local), s2=scatter_scratch(height, width),
        ),
    )


def turn_kernel(n):
    height, width = n.third.shape
    loads = [pltpu.make_async_copy(n.full_in, n.win, n.load.at[0]), pltpu.make_async_copy(n.full_out, n.wout, n.load.at[1])]
    for load in loads:
        load.start()
    gather, scatter = Gather(n.rows, **n.g1), Scatter(**n.s1)
    gather_two, scatter_two = Gather(n.grads, **n.g2), Scatter(**n.s2)
    ready = greet(tp_peers())
    for chunk in range(CHUNKS):
        here = scatter.rows(chunk)
        n.rows[here, :] = norm_rows(n.third[here, :], n.gains[3:4, :]).astype(BF16)
        if chunk == 0:
            ready()
        gather.start(chunk)
    ffn_forward(gather, scatter, n.win, n.wout, n.hidden, n.active, loads[0].wait, loads[1].wait)
    gain_four = jnp.zeros((1, width), F32)
    for chunk in range(CHUNKS):
        here = scatter.rows(chunk)
        fourth = n.third[here, :] + 0.5 * scatter.total(chunk)
        n.output[here, :] = norm_rows(fourth, n.gains[4:5, :]).astype(BF16)
        grad, gain = norm_back(fourth, n.gains[4:5, :], n.out_grad[here, :].astype(F32))
        gain_four = gain_four + gain
        n.grad_fourth[here, :] = grad
        n.grads[here, :] = (0.5 * grad).astype(BF16)
        gather_two.start(chunk)

    def nothing():
        return None

    ffn_backward(gather_two, scatter_two, n.win, n.wout, n.hidden, None, n.slope, nothing, nothing)
    weight_products(n.grad_out, n.active, n.grads)
    weight_products(n.grad_in, n.rows, n.slope)
    gain_three = jnp.zeros((1, width), F32)
    for chunk in range(CHUNKS):
        here = scatter.rows(chunk)
        grad, gain = norm_back(n.third[here, :], n.gains[3:4, :], scatter_two.total(chunk))
        gain_three = gain_three + gain
        n.grad_third[here, :] = n.grad_fourth[here, :] + grad
    n.gain_sums[0:1, :] = gain_three
    n.gain_sums[1:2, :] = gain_four
    for item in (gather, scatter, gather_two, scatter_two):
        item.finish()


def run_turn(third, gains, out_grad, full_in, full_out):
    height, width = third.shape
    frames = 4 * height
    inner = full_in.shape[1]
    return run_kernel(
        turn_kernel,
        2,
        dict(
            third=(third, True), gains=(gains, True), out_grad=(out_grad, True),
            full_in=(full_in, False), full_out=(full_out, False),
        ),
        dict(
            output=((height, width), BF16, True),
            grad_third=((height, width), F32, True),
            gain_sums=((8, width), F32, True),
            grad_in=((width, inner), BF16, True),
            grad_out=((inner, width), BF16, True),
        ),
        dict(
            win=pltpu.VMEM((width, inner), BF16), wout=pltpu.VMEM((inner, width), BF16),
            rows=pltpu.VMEM((frames, width), BF16), hidden=pltpu.VMEM((frames, inner), F32),
            active=pltpu.VMEM((frames, inner), BF16), slope=pltpu.VMEM((frames, inner), BF16),
            grads=pltpu.VMEM((frames, width), BF16), grad_fourth=pltpu.VMEM((height, width), F32),
            g1=gather_scratch(), s1=scatter_scratch(height, width),
            g2=gather_scratch(), s2=scatter_scratch(height, width),
            load=pltpu.SemaphoreType.DMA((2,)),
        ),
    )


def conv_back_kernel(n):
    height, width = n.grad_third.shape
    frames = 4 * height
    local = n.wconv.shape[0]
    settles = [Settle(n.grad_out, n.sum_out, **n.t_out), Settle(n.grad_in, n.sum_in, **n.t_in)]
    gather = Gather(n.grads, **n.g1)
    swap = Swap(**n.swap)
    edges = Edges(n.back, **n.edge)
    scatter = Scatter(**n.s1)
    gather_two = Gather(n.grads_two, **n.g2)
    ready = greet(tp_peers() + seq_peers())
    for chunk in range(CHUNKS):
        here = scatter.rows(chunk)
        n.grads[here, :] = n.grad_third[here, :].astype(BF16)
        if chunk == 0:
            ready()
        gather.start(chunk)
    for task in settles:
        task.begin()
    gather.wait_near()
    none = jnp.zeros((1, local), F32)
    sums = [none, none]

    def batch_rows(slots):
        product = across_product(n.grads[slot_rows(slots, height), :], n.wconv[...])
        for index, slot in enumerate(slots):
            place = span(owner(slot) * height, height)
            normal = n.normal[place, :]
            batch = normal * n.bn_gain[...] + n.bn_bias[...]
            logistic = jax.nn.sigmoid(batch)
            rows = product[index * height : (index + 1) * height]
            grad = rows * (logistic * (1.0 + batch * (1.0 - logistic)))
            n.grad_batch[place, :] = grad
            sums[0] = sums[0] + jnp.sum(grad * normal, axis=0, keepdims=True)
            sums[1] = sums[1] + jnp.sum(grad, axis=0, keepdims=True)

    batch_rows((0, 1))
    for chunk in range(CHUNKS):
        gather.pass_on(chunk)
    for chunk in range(CHUNKS):
        gather.wait_last(chunk)
    batch_rows((2, 3))
    swap.blocks[0, 0:1, :] = sums[0]
    swap.blocks[0, 1:2, :] = sums[1]
    swap.start()
    weight_products(n.grad_conv, n.alive, n.grads, 512)
    swap.wait()
    grad_gain, grad_bias = none, none
    for item in in_order(swap):
        grad_gain = grad_gain + item[0:1]
        grad_bias = grad_bias + item[1:2]
    n.bn_sums[0:1, :] = grad_gain
    n.bn_sums[1:2, :] = grad_bias
    gain, inverse, real_all = n.bn_gain[...], n.stats[0:1, :], n.stats[1:2, :]
    block = 128

    def deconvolve(index, nothing):
        here = span(index * block, block)
        real = n.context[here, KERNEL : KERNEL + 1]
        drift = real * (gain * grad_bias + n.normal[here, :] * gain * grad_gain) / real_all
        n.back[pl.ds(pl.multiple_of(EDGE + index * block, EDGE), block), :] = inverse * (
            n.grad_batch[here, :] * gain - drift
        )
        return nothing

    lax.fori_loop(0, frames // block, deconvolve, 0)
    edges.start()
    edges.wait()
    taps = [none] * KERNEL

    for slot in range(4):

        def part(index, carried):
            begin = owner(slot) * height + index * block
            here = span(begin, block)
            back = n.back[pl.ds(pl.multiple_of(begin, block), block + 2 * EDGE), :]
            gated = n.gated[pl.ds(pl.multiple_of(begin, block), block + 2 * EDGE), :]
            marks = n.context[here, :]
            own = back[EDGE : EDGE + block]
            grad = jnp.zeros((block, local), F32)
            result = []
            for tap in range(KERNEL):
                first = EDGE - KERNEL // 2 + tap
                mark = marks[:, tap : tap + 1]
                result.append(
                    carried[tap]
                    + jnp.sum(gated[first : first + block] * mark * own, axis=0, keepdims=True)
                )
                mirror = KERNEL - 1 - tap
                grad = grad + n.depth[mirror : mirror + 1, :] * back[first : first + block] * mark
            grad = grad * marks[:, KERNEL : KERNEL + 1]
            both = n.paired[here, :]
            logistic = jax.nn.sigmoid(both[:, local:])
            rows = span(slot * height + index * block, block)
            n.grad_paired[rows, pl.ds(0, local)] = (grad * logistic).astype(BF16)
            n.grad_paired[rows, pl.ds(local, local)] = (
                grad * both[:, :local] * logistic * (1.0 - logistic)
            ).astype(BF16)
            return tuple(result)

        taps = lax.fori_loop(0, height // block, part, tuple(taps))
    for tap in range(KERNEL):
        n.depth_sums[tap : tap + 1, :] = taps[tap]
    scatter.spread(
        lambda slots, cols: across_product(n.grad_paired[slot_rows(slots, height), :], n.wpair[cols, :]), width
    )
    weight_products(n.grad_pair, n.rows, n.grad_paired)
    gain_two = jnp.zeros((1, width), F32)
    for chunk in range(CHUNKS):
        here = scatter.rows(chunk)
        grad, gain = norm_back(n.second[here, :], n.gains[2:3, :], scatter.total(chunk))
        gain_two = gain_two + gain
        n.grad_second[here, :] = n.grad_third[here, :] + grad
        n.grads_two[here, :] = n.grad_second[here, :].astype(BF16)
        gather_two.start(chunk)
    n.gain_sums[0:1, :] = gain_two
    for task in settles:
        task.middle()
    gather_two.wait_near()

    def mixed_rows(slots):
        product = across_product(n.grads_two[slot_rows(slots, height), :], n.wattend[...]).astype(BF16)
        for index, slot in enumerate(slots):
            n.grad_mixed[span(owner(slot) * height, height), :] = product[index * height : (index + 1) * height]

    mixed_rows((0, 1))
    for chunk in range(CHUNKS):
        gather_two.pass_on(chunk)
    for chunk in range(CHUNKS):
        gather_two.wait_last(chunk)
    mixed_rows((2, 3))
    weight_products(n.grad_attend, n.mixed_low, n.grads_two, 512)
    for task in settles:
        task.end()
    for item in settles + [gather, swap, edges, scatter, gather_two]:
        item.finish()


def run_conv_back(grad_third, gains, kept, context, depth, bn_gain, bn_bias, attend, pair, conv, turn):
    height, width = grad_third.shape
    frames, local = kept.normal.shape
    count = lax.axis_size("seq")
    inner = turn.grad_in.shape[1]
    return run_kernel(
        conv_back_kernel,
        3,
        dict(
            grad_third=(grad_third, True), gains=(gains, True), second=(kept.second, True), rows=(kept.rows, True),
            paired=(kept.paired, True), gated=(kept.gated, True), normal=(kept.normal, True),
            stats=(kept.stats, True), alive=(kept.alive, True), mixed_low=(kept.mixed_low, True),
            context=(context, True), depth=(depth, True), bn_gain=(bn_gain, True), bn_bias=(bn_bias, True),
            wattend=(attend, True), wpair=(pair, True), wconv=(conv, True),
            grad_in=(turn.grad_in, False), grad_out=(turn.grad_out, False),
        ),
        dict(
            grad_second=((height, width), F32, True),
            grad_mixed=((frames, local), BF16, True),
            grad_pair=((width, 2 * local), BF16, True),
            grad_conv=((local, width), BF16, True),
            grad_attend=((local, width), BF16, True),
            depth_sums=((8, local), F32, True),
            bn_sums=((8, local), F32, True),
            gain_sums=((8, width), F32, True),
            sum_in=((width // count, inner), F32, True),
            sum_out=((inner // count, width), F32, True),
        ),
        dict(
            grads=pltpu.VMEM((frames, width), BF16), grads_two=pltpu.VMEM((frames, width), BF16),
            grad_batch=pltpu.VMEM((frames, local), F32), back=pltpu.VMEM((frames + 2 * EDGE, local), F32),
            grad_paired=pltpu.VMEM((frames, 2 * local), BF16),
            t_out=settle_scratch(inner // count, width), t_in=settle_scratch(width // count, inner),
            g1=gather_scratch(), swap=swap_scratch(8, local), edge=edges_scratch(),
            s1=scatter_scratch(height, width), g2=gather_scratch(),
        ),
    )


def close_kernel(n):
    height, width = n.grad_second.shape
    frames = 4 * height
    local = n.grad_query.shape[1]
    seq, count = lax.axis_index("seq"), lax.axis_size("seq")
    half = MAXLEN - frames
    loads = [
        pltpu.make_async_copy(n.full_out, n.wout, n.load.at[0]),
        pltpu.make_async_copy(n.full_hidden, n.hidden, n.load.at[1]),
        pltpu.make_async_copy(n.full_in, n.win, n.load.at[2]),
        pltpu.make_async_copy(n.grad_key.at[pl.ds(MAXLEN, frames), :], n.own_back.at[0], n.load.at[3]),
        pltpu.make_async_copy(n.grad_value.at[pl.ds(MAXLEN, frames), :], n.own_back.at[1], n.load.at[4]),
    ]
    for load in loads:
        load.start()
    earlier = [
        Settle(n.grad_pair, n.sum_pair, **n.t_pair),
        Settle(n.grad_conv, n.sum_conv, **n.t_conv),
        Settle(n.grad_attend, n.sum_attend, **n.t_attend),
    ]
    project = Settle(n.grad_project, n.sum_project, **n.t_project)
    last = [Settle(n.grad_out, n.sum_out, **n.t_out), Settle(n.grad_in, n.sum_in, **n.t_in)]
    scatter, gather, scatter_two = Scatter(**n.s1), Gather(n.grads, **n.g1), Scatter(**n.s2)
    swap = Swap(**n.swap)
    ready = greet(tp_peers() + seq_peers())
    shifts = (1, -1, 2, -2)
    sources = ((MAXLEN + frames, frames), (MAXLEN - frames, frames), (MAXLEN + 2 * frames, half), (0, half))
    targets = ((0, 0), (1, 0), (2, 0), (2, frames - half))

    def back(kind, which):
        begin, size = sources[kind]
        place, row = targets[kind]
        source = (n.grad_key, n.grad_value)[which].at[pl.ds(begin, size), :]
        target = n.others_back.at[which, place, pl.ds(row, size), :]
        peer = {"seq": lax.rem(seq + shifts[kind] + count, count)}
        return remote(source, target, n.back_send.at[which, kind], n.back_receive.at[which, kind], peer)

    def there(kind, sending):
        other = seq + shifts[kind] if sending else seq - shifts[kind]
        return (other >= 0) & (other < count)

    for kind in range(4):
        place, row = targets[kind]

        @pl.when(jnp.logical_not(there(kind, False)))
        def _():
            for which in range(2):
                size = sources[kind][1]
                n.others_back[which, place, pl.ds(row, size), :] = jnp.zeros((size, local), BF16)

    ready()
    for kind in range(4):

        @pl.when(there(kind, True))
        def _():
            for which in range(2):
                back(kind, which).start()

    for task in earlier:
        task.begin()
    for slot in range(4):
        n.grad_rows[pl.ds(slot * height, height), pl.ds(0, local)] = n.grad_query[span(owner(slot) * height, height), :]
    for task in earlier:
        task.middle()
    for kind in range(4):

        @pl.when(there(kind, False))
        def _():
            for which in range(2):
                back(kind, which).wait_recv()

    loads[3].wait()
    loads[4].wait()
    for slot in range(4):
        place = span(owner(slot) * height, height)
        for which in range(2):
            total = n.own_back[which, place, :].astype(F32)
            for other in range(3):
                total = total + n.others_back[which, other, place, :].astype(F32)
            n.grad_rows[pl.ds(slot * height, height), pl.ds((which + 1) * local, local)] = total.astype(BF16)
    scatter.spread(
        lambda slots, cols: across_product(n.grad_rows[slot_rows(slots, height), :], n.wproject[cols, :]), width
    )
    weight_products(n.grad_project, n.rows_two, n.grad_rows)
    project.begin()
    gain_one = jnp.zeros((1, width), F32)
    for chunk in range(CHUNKS):
        here = scatter.rows(chunk)
        grad, gain = norm_back(n.first[here, :], n.gains[1:2, :], scatter.total(chunk))
        gain_one = gain_one + gain
        n.grad_first[here, :] = n.grad_second[here, :] + grad
        n.grads[here, :] = (0.5 * n.grad_first[here, :]).astype(BF16)
        gather.start(chunk)

    def wait_out():
        loads[0].wait()
        loads[1].wait()

    ffn_backward(gather, scatter_two, n.win, n.wout, n.hidden, n.active, n.slope, wait_out, loads[2].wait)
    weight_products(n.grad_out, n.active, n.grads)
    last[0].begin()
    weight_products(n.grad_in, n.rows, n.slope)
    last[1].begin()
    project.middle()
    gain_zero = jnp.zeros((1, width), F32)
    for chunk in range(CHUNKS):
        here = scatter.rows(chunk)
        grad, gain = norm_back(n.values[here, :].astype(F32), n.gains[0:1, :], scatter_two.total(chunk))
        gain_zero = gain_zero + gain
        n.input_grad[here, :] = n.grad_first[here, :] + grad
    n.small[0, 0:1, :] = gain_zero
    n.small[0, 1:2, :] = gain_one
    n.small[0, 2:3, :] = n.gain_mid[0:1, :]
    n.small[0, 3:5, :] = n.gain_late[0:2, :]
    n.small[0, 5:8, :] = jnp.zeros((3, width), F32)
    near, far = tp_peers()
    hop = remote(n.small.at[0], n.small.at[1], n.small_sem.at[0], n.small_sem.at[1], near)
    hop.start()
    hop.wait_recv()
    n.small[2] = n.small[0] + n.small[1]
    hop_two = remote(n.small.at[2], n.small.at[3], n.small_sem.at[2], n.small_sem.at[3], far)
    hop_two.start()
    hop_two.wait_recv()
    swap.blocks[0, :, pl.ds(0, width)] = n.small[2] + n.small[3]
    swap.blocks[0, :, pl.ds(width, local)] = n.depth_sums[...]
    swap.start()
    for task in last:
        task.middle()
    for task in earlier:
        task.end()
    swap.wait()
    total = jnp.zeros((8, width + local), F32)
    for item in in_order(swap):
        total = total + item
    n.gain_total[...] = total[:, :width]
    n.depth_total[...] = total[:, width:]
    project.end()
    for task in last:
        task.end()
    for kind in range(4):

        @pl.when(there(kind, True))
        def _():
            for which in range(2):
                back(kind, which).wait_send()

    hop.wait_send()
    hop_two.wait_send()
    for item in earlier + [project] + last + [scatter, gather, scatter_two, swap]:
        item.finish()


def run_close(values, gains, opened, grad_second, grad_query, grad_key, grad_value, conv_back, gain_late):
    height, width = values.shape
    frames, local = grad_query.shape
    count = lax.axis_size("seq")
    inner = opened.full_in.shape[1]
    settled = dict(
        pair=(width, 2 * local), conv=(local, width), attend=(local, width),
        project=(width, 3 * local), out=(inner, width), **{"in": (width, inner)},
    )
    return run_kernel(
        close_kernel,
        4,
        dict(
            values=(values, True), gains=(gains, True), first=(opened.first, True), rows=(opened.rows, True),
            rows_two=(opened.rows_two, True), full_hidden=(opened.hidden, False),
            full_in=(opened.full_in, False), full_out=(opened.full_out, False),
            wproject=(opened.full_project, True), grad_second=(grad_second, True), grad_query=(grad_query, True),
            grad_key=(grad_key, False), grad_value=(grad_value, False), grad_pair=(conv_back.grad_pair, False),
            grad_conv=(conv_back.grad_conv, False), grad_attend=(conv_back.grad_attend, False),
            depth_sums=(conv_back.depth_sums, True), gain_mid=(conv_back.gain_sums, True), gain_late=(gain_late, True),
        ),
        dict(
            input_grad=((height, width), F32, True),
            gain_total=((8, width), F32, True),
            depth_total=((8, local), F32, True),
            **{f"sum_{name}": ((tall // count, wide), F32, True) for name, (tall, wide) in settled.items()},
        ),
        dict(
            win=pltpu.VMEM((width, inner), BF16), wout=pltpu.VMEM((inner, width), BF16),
            hidden=pltpu.VMEM((frames, inner), F32), active=pltpu.VMEM((frames, inner), BF16),
            slope=pltpu.VMEM((frames, inner), BF16), grads=pltpu.VMEM((frames, width), BF16),
            grad_first=pltpu.VMEM((height, width), F32),
            own_back=pltpu.VMEM((2, frames, local), BF16), others_back=pltpu.VMEM((2, 3, frames, local), BF16),
            grad_rows=pltpu.VMEM((frames, 3 * local), BF16),
            grad_project=pltpu.VMEM((width, 3 * local), BF16),
            grad_in=pltpu.VMEM((width, inner), BF16), grad_out=pltpu.VMEM((inner, width), BF16),
            **{f"t_{name}": settle_scratch(tall // count, wide) for name, (tall, wide) in settled.items()},
            g1=gather_scratch(), s1=scatter_scratch(height, width), s2=scatter_scratch(height, width),
            swap=swap_scratch(8, width + local),
            small=pltpu.VMEM((4, 8, width), F32), small_sem=pltpu.SemaphoreType.DMA((4,)),
            back_send=pltpu.SemaphoreType.DMA((2, 4)), back_receive=pltpu.SemaphoreType.DMA((2, 4)),
            load=pltpu.SemaphoreType.DMA((5,)),
        ),
    )


def attention_context(segment_ids, pad_mask, frames):
    anchor = lax.axis_index("seq") * frames
    window = frames + 2 * MAXLEN
    codes = jnp.where(pad_mask == 1, segment_ids, -1)
    codes_wide = jnp.pad(codes, (MAXLEN, MAXLEN), constant_values=-2)
    key_codes = lax.dynamic_slice_in_dim(codes_wide, anchor, window)
    query_seg = lax.dynamic_slice_in_dim(segment_ids, anchor, frames)
    blocks = query_seg.reshape(frames // QUERY_BLOCK, QUERY_BLOCK)
    low = jnp.sum((segment_ids[None, :] < blocks[:, :1]).astype(jnp.int32), axis=1)
    high = jnp.sum((segment_ids[None, :] <= blocks[:, -1:]).astype(jnp.int32), axis=1)
    first = (low - anchor + MAXLEN) // KEY_BLOCK
    last = (high - anchor + MAXLEN + KEY_BLOCK - 1) // KEY_BLOCK
    key_codes = jnp.broadcast_to(key_codes[:, None], (window, 128))
    return (first, last, query_seg[None, :], key_codes)


def allowed_block(codes, seg_row, key_begin, query_begin):
    wide = jnp.concatenate([codes] * (QUERY_BLOCK // 128), axis=1)
    place = lax.broadcasted_iota(jnp.int32, (KEY_BLOCK, QUERY_BLOCK), 0) - lax.broadcasted_iota(
        jnp.int32, (KEY_BLOCK, QUERY_BLOCK), 1
    )
    return (wide == seg_row) | (place == query_begin - key_begin)


def attend_kernel(first, last, query, keys, values, seg_row, codes, out, totals):
    step = pl.program_id(1)
    rows = query[...]
    segs = seg_row[...]

    def one(index, carried):
        highest, total, mixed = carried
        begin = pl.multiple_of(index * KEY_BLOCK, KEY_BLOCK)
        key_rows = keys[pl.ds(begin, KEY_BLOCK), :]
        value_rows = values[pl.ds(begin, KEY_BLOCK), :]
        scores = across_product(key_rows, rows) * (SCORE_SCALE * LOG2E)
        allowed = allowed_block(
            codes[pl.ds(begin, KEY_BLOCK), :], segs, begin, MAXLEN + step * QUERY_BLOCK
        )
        scores = jnp.where(allowed, scores, -1e30)
        top = jnp.maximum(highest, jnp.max(scores, axis=0, keepdims=True))
        fade = jnp.exp2(highest - top)
        weights = jnp.exp2(scores - top)
        total = total * fade + jnp.sum(weights, axis=0, keepdims=True)
        mixed = mixed * fade + inner_product(value_rows, weights.astype(jnp.bfloat16))
        return (top, total, mixed)

    start = (
        jnp.full((1, QUERY_BLOCK), -1e30, jnp.float32),
        jnp.zeros((1, QUERY_BLOCK), jnp.float32),
        jnp.zeros((HEAD_DIM, QUERY_BLOCK), jnp.float32),
    )
    highest, total, mixed = lax.fori_loop(first[step], last[step], one, start)
    out[...] = jnp.transpose(mixed / total)
    totals[...] = (highest + jnp.log2(total))[None]


def attend_back_kernel(
    first, last, query, keys, values, grad, mixed, totals, seg_row, codes, grad_query, key_out, value_out, grad_key, grad_value
):
    step = pl.program_id(1)

    @pl.when(step == 0)
    def _():
        grad_key[...] = jnp.zeros_like(grad_key)
        grad_value[...] = jnp.zeros_like(grad_value)

    rows = query[...]
    segs = seg_row[...]
    grads = grad[...]
    lse = totals[0]
    centre = jnp.sum(jnp.transpose(grads.astype(jnp.float32) * mixed[...]), axis=0, keepdims=True)

    def one(index, total):
        begin = pl.multiple_of(index * KEY_BLOCK, KEY_BLOCK)
        here = pl.ds(begin, KEY_BLOCK)
        key_rows = keys[here, :]
        scores = across_product(key_rows, rows) * (SCORE_SCALE * LOG2E)
        allowed = allowed_block(codes[here, :], segs, begin, MAXLEN + step * QUERY_BLOCK)
        probs = jnp.where(allowed, jnp.exp2(scores - lse), 0.0)
        grad_probs = across_product(values[here, :], grads)
        grad_scores = (probs * (grad_probs - centre) * SCORE_SCALE).astype(jnp.bfloat16)
        grad_value[here, :] += plain_product(probs.astype(jnp.bfloat16), grads)
        grad_key[here, :] += plain_product(grad_scores, rows)
        return total + inner_product(grad_scores, key_rows)

    grad_query[...] = lax.fori_loop(
        first[step], last[step], one, jnp.zeros((QUERY_BLOCK, HEAD_DIM), jnp.float32)
    ).astype(jnp.bfloat16)

    @pl.when(step == pl.num_programs(1) - 1)
    def _():
        key_out[...] = grad_key[...].astype(jnp.bfloat16)
        value_out[...] = grad_value[...].astype(jnp.bfloat16)


def attend(queries, both, context):
    first, last, seg_row, codes = context
    frames, local = queries.shape
    window = both.shape[0]
    grid = (local // HEAD_DIM, frames // QUERY_BLOCK)
    block = pl.BlockSpec((QUERY_BLOCK, HEAD_DIM), lambda h, i, *_: (i, h))
    whole = pl.BlockSpec((window, HEAD_DIM), lambda h, i, *_: (0, h))
    whole_values = pl.BlockSpec((window, HEAD_DIM), lambda h, i, *_: (0, grid[0] + h))
    seg_block = pl.BlockSpec((1, QUERY_BLOCK), lambda h, i, *_: (0, i))
    code_block = pl.BlockSpec((window, 128), lambda h, i, *_: (0, 0))
    row_block = pl.BlockSpec((1, 1, QUERY_BLOCK), lambda h, i, *_: (h, 0, i))
    return pl.pallas_call(
        attend_kernel,
        grid_spec=pltpu.PrefetchScalarGridSpec(
            num_scalar_prefetch=2,
            grid=grid,
            in_specs=[block, whole, whole_values, seg_block, code_block],
            out_specs=[block, row_block],
        ),
        out_shape=(
            jax.ShapeDtypeStruct((frames, local), jnp.float32),
            jax.ShapeDtypeStruct((grid[0], 1, frames), jnp.float32),
        ),
        cost_estimate=pl.CostEstimate(
            flops=4 * frames * MAXLEN * local, bytes_accessed=8 << 20, transcendentals=0
        ),
    )(first, last, queries, both, both, seg_row, codes)


def attend_back(queries, both, grads, mixed, totals, context):
    first, last, seg_row, codes = context
    frames, local = queries.shape
    window = both.shape[0]
    grid = (local // HEAD_DIM, frames // QUERY_BLOCK)
    block = pl.BlockSpec((QUERY_BLOCK, HEAD_DIM), lambda h, i, *_: (i, h))
    whole = pl.BlockSpec((window, HEAD_DIM), lambda h, i, *_: (0, h))
    whole_values = pl.BlockSpec((window, HEAD_DIM), lambda h, i, *_: (0, grid[0] + h))
    seg_block = pl.BlockSpec((1, QUERY_BLOCK), lambda h, i, *_: (0, i))
    code_block = pl.BlockSpec((window, 128), lambda h, i, *_: (0, 0))
    row_block = pl.BlockSpec((1, 1, QUERY_BLOCK), lambda h, i, *_: (h, 0, i))
    return pl.pallas_call(
        attend_back_kernel,
        grid_spec=pltpu.PrefetchScalarGridSpec(
            num_scalar_prefetch=2,
            grid=grid,
            in_specs=[block, whole, whole_values, block, block, row_block, seg_block, code_block],
            out_specs=[block, whole, whole],
            scratch_shapes=[pltpu.VMEM((window, HEAD_DIM), F32), pltpu.VMEM((window, HEAD_DIM), F32)],
        ),
        out_shape=(
            jax.ShapeDtypeStruct((frames, local), jnp.bfloat16),
            jax.ShapeDtypeStruct((window, local), jnp.bfloat16),
            jax.ShapeDtypeStruct((window, local), jnp.bfloat16),
        ),
        compiler_params=pltpu.CompilerParams(vmem_limit_bytes=48 << 20),
        cost_estimate=pl.CostEstimate(
            flops=10 * frames * MAXLEN * local, bytes_accessed=16 << 20, transcendentals=0
        ),
    )(first, last, queries, both, both, grads, mixed, totals, seg_row, codes)


def conv_context(segment_ids, pad_mask, frames):
    anchor = lax.axis_index("seq") * frames
    half = KERNEL // 2
    near = lax.dynamic_slice_in_dim(
        jnp.pad(segment_ids, (half, half), constant_values=-1), anchor, frames + 2 * half
    )
    own = lax.dynamic_slice_in_dim(segment_ids, anchor, frames)
    real = lax.dynamic_slice_in_dim(pad_mask, anchor, frames)
    columns = [near[tap : tap + frames] == own for tap in range(KERNEL)] + [real == 1]
    columns += [jnp.zeros_like(columns[0])] * (8 - len(columns))
    return jnp.stack(columns, axis=1).astype(F32)


def body(
    inputs,
    ln_gains,
    ffn1_in,
    ffn1_out,
    qkv_weight,
    attn_out,
    conv_in,
    conv_depth,
    bn_gain,
    bn_bias,
    conv_out,
    ffn2_in,
    ffn2_out,
    segment_ids,
    pad_mask,
    out_grad,
):
    frames = inputs.shape[0] * lax.axis_size("tp")
    attend_ctx = attention_context(segment_ids, pad_mask, frames)
    conv_ctx = conv_context(segment_ids, pad_mask, frames)
    gain_row, bias_row = bn_gain[None, :], bn_bias[None, :]
    shards = SimpleNamespace(
        ffn1_in=ffn1_in,
        ffn1_out=ffn1_out,
        project=qkv_weight.reshape(qkv_weight.shape[0], -1),
        attend=attn_out,
        pair=conv_in.reshape(conv_in.shape[0], -1),
        conv=conv_out,
    )
    opened = run_open(inputs, ln_gains, shards)
    mixed, totals = attend(opened.queries, opened.window, attend_ctx)
    conv = run_conv(
        mixed, opened.first, ln_gains, opened.full_attend, conv_ctx, conv_depth, gain_row, bias_row,
        opened.full_pair, opened.full_conv, ffn2_in, ffn2_out,
    )
    turn = run_turn(conv.third, ln_gains, out_grad, conv.full_in, conv.full_out)
    conv_back = run_conv_back(
        turn.grad_third, ln_gains, conv, conv_ctx, conv_depth, gain_row, bias_row,
        opened.full_attend, opened.full_pair, opened.full_conv, turn,
    )
    grad_query, grad_key, grad_value = attend_back(
        opened.queries, opened.window, conv_back.grad_mixed, mixed, totals, attend_ctx
    )
    closed = run_close(
        inputs, ln_gains, opened, conv_back.grad_second, grad_query, grad_key, grad_value, conv_back, turn.gain_sums
    )
    return (
        turn.output,
        closed.input_grad,
        closed.gain_total[:5],
        closed.sum_in,
        closed.sum_out,
        closed.sum_project.reshape(qkv_weight.shape),
        closed.sum_attend,
        closed.sum_pair.reshape(conv_in.shape),
        closed.depth_total[:KERNEL],
        conv_back.bn_sums[0],
        conv_back.bn_sums[1],
        closed.sum_conv,
        conv_back.sum_in,
        conv_back.sum_out,
    )


def solution(mesh):
    return jax.shard_map(
        body,
        mesh=mesh,
        in_specs=(
            P(("seq", "tp"), None),
            P(),
            P("seq", "tp"),
            P(("tp", "seq"), None),
            P("seq", None, "tp"),
            P(("tp", "seq"), None),
            P("seq", None, "tp"),
            P(None, "tp"),
            P("tp"),
            P("tp"),
            P(("tp", "seq"), None),
            P("seq", "tp"),
            P(("tp", "seq"), None),
            P(),
            P(),
            P(("seq", "tp"), None),
        ),
        out_specs=(
            P(("seq", "tp"), None),
            P(("seq", "tp"), None),
            P(),
            P("seq", "tp"),
            P(("tp", "seq"), None),
            P("seq", None, "tp"),
            P(("tp", "seq"), None),
            P("seq", None, "tp"),
            P(None, "tp"),
            P("tp"),
            P("tp"),
            P(("tp", "seq"), None),
            P("seq", "tp"),
            P(("tp", "seq"), None),
        ),
        check_vma=False,
    )
```

```python
import math
from types import SimpleNamespace

import jax
import jax.numpy as jnp
from jax import lax
from jax.experimental import pallas as pl
from jax.experimental.pallas import tpu as pltpu
from jax.sharding import PartitionSpec as P

HEAD_DIM = 128
KERNEL = 5
MAXLEN = 1536
EPSILON = 1e-05
CHUNKS = 2
EDGE = 8
VMEM_LIMIT = 62 << 20
QUERY_BLOCK = 256
KEY_BLOCK = 512
SCORE_SCALE = 1.0 / math.sqrt(HEAD_DIM)
LOG2E = 1.4426950408889634
BF16 = jnp.bfloat16
F32 = jnp.float32
IN_VMEM = pl.BlockSpec(memory_space=pltpu.VMEM)
IN_PLACE = pl.BlockSpec(memory_space=pl.ANY)


def plain_product(left, right):
    return jnp.dot(left, right, preferred_element_type=F32)


def inner_product(left, right):
    return lax.dot_general(left, right, (((0,), (0,)), ((), ())), preferred_element_type=F32)


def across_product(left, right):
    return lax.dot_general(left, right, (((1,), (1,)), ((), ())), preferred_element_type=F32)


def swish(values):
    return values * jax.nn.sigmoid(values)


def standard_rows(values):
    centred = values - jnp.mean(values, axis=-1, keepdims=True)
    spread = jnp.mean(centred * centred, axis=-1, keepdims=True)
    inverse = lax.rsqrt(spread + EPSILON)
    return (centred * inverse, inverse)


def norm_rows(values, gain_row):
    return standard_rows(values)[0] * gain_row


def norm_back(values, gain_row, grads):
    normal, inverse = standard_rows(values)
    scaled = grads * gain_row
    result = inverse * (
        scaled
        - jnp.mean(scaled, axis=-1, keepdims=True)
        - normal * jnp.mean(scaled * normal, axis=-1, keepdims=True)
    )
    return (result, jnp.sum(grads * normal, axis=0, keepdims=True))


def flip(index, bit):
    return index + bit - 2 * bit * lax.rem(lax.div(index, bit), 2)


def span(begin, size):
    return pl.ds(pl.multiple_of(begin, size), size)


def static_span(begin, size):
    return pl.ds(begin, size)


def remote(source, target, send, receive, peer):
    return pltpu.make_async_remote_copy(
        src_ref=source,
        dst_ref=target,
        send_sem=send,
        recv_sem=receive,
        device_id=peer,
        device_id_type=pl.DeviceIdType.MESH,
    )


def tp_peers():
    me = lax.axis_index("tp")
    return [{"tp": flip(me, 1)}, {"tp": flip(me, 2)}]


def seq_peers():
    me, count = lax.axis_index("seq"), lax.axis_size("seq")
    return [{"seq": lax.rem(me + step, count)} for step in range(1, count)]


def greet(peers):
    barrier = pltpu.get_barrier_semaphore()
    for peer in peers:
        pl.semaphore_signal(barrier, inc=1, device_id=peer, device_id_type=pl.DeviceIdType.MESH)
    return lambda: pl.semaphore_wait(barrier, len(peers))


def owner(slot):
    me = lax.axis_index("tp")
    if slot & 1:
        me = flip(me, 1)
    if slot & 2:
        me = flip(me, 2)
    return me


def tiles(total, tile, body):
    def one(index, nothing):
        body(span(index * tile, tile))
        return nothing

    lax.fori_loop(0, total // tile, one, 0)


class Gather:
    def __init__(self, rows, send, receive):
        self.near, self.far = tp_peers()
        self.height = rows.shape[0] // 4
        self.piece = self.height // CHUNKS
        self.rows, self.send, self.receive = rows, send, receive

    def part(self, slot, chunk):
        return self.rows.at[pl.ds(slot * self.height + chunk * self.piece, self.piece), :]

    def hop(self, kind, chunk):
        source, target = ((0, 1), (0, 2), (2, 3))[kind]
        return remote(
            self.part(source, chunk),
            self.part(target, chunk),
            self.send.at[kind, chunk],
            self.receive.at[kind, chunk],
            self.far if kind == 1 else self.near,
        )

    def start(self, chunk):
        self.hop(1, chunk).start()
        self.hop(0, chunk).start()

    def wait_near(self):
        for chunk in range(CHUNKS):
            self.hop(0, chunk).wait_recv()

    def pass_on(self, chunk):
        self.hop(1, chunk).wait_recv()
        self.hop(2, chunk).start()

    def wait_last(self, chunk):
        self.hop(2, chunk).wait_recv()

    def finish(self):
        for chunk in range(CHUNKS):
            for kind in range(3):
                self.hop(kind, chunk).wait_send()


def gather_scratch():
    return dict(send=pltpu.SemaphoreType.DMA((3, CHUNKS)), receive=pltpu.SemaphoreType.DMA((3, CHUNKS)))


class Scatter:
    def __init__(self, own, passing, outgoing, incoming, send, receive):
        self.near, self.far = tp_peers()
        self.height = own.shape[0]
        self.piece = self.height // CHUNKS
        self.own, self.passing = own, passing
        self.outgoing, self.incoming, self.send, self.receive = outgoing, incoming, send, receive

    def rows(self, chunk):
        return pl.ds(chunk * self.piece, self.piece)

    def copy(self, kind, chunk):
        here = self.rows(chunk)
        return remote(
            self.outgoing.at[kind, here, :],
            self.incoming.at[kind, here, :],
            self.send.at[kind, chunk],
            self.receive.at[kind, chunk],
            self.far if kind == 2 else self.near,
        )

    def start(self, kind):
        for chunk in range(CHUNKS):
            self.copy(kind, chunk).start()

    def relay(self, chunk):
        here = self.rows(chunk)
        self.copy(1, chunk).wait_recv()
        self.outgoing[2, here, :] = (self.passing[here, :] + self.incoming[1, here, :].astype(F32)).astype(BF16)
        self.copy(2, chunk).start()

    def total(self, chunk):
        here = self.rows(chunk)
        self.copy(0, chunk).wait_recv()
        self.copy(2, chunk).wait_recv()
        return self.own[here, :] + self.incoming[0, here, :].astype(F32) + self.incoming[2, here, :].astype(F32)

    def spread(self, product, width, tile=512):
        height = self.height

        def far(cols):
            term = product((2, 3), cols)
            self.passing[:, cols] = term[:height]
            self.outgoing[1, :, cols] = term[height:].astype(BF16)

        tiles(width, tile, far)
        self.start(1)

        def near(cols):
            term = product((0, 1), cols)
            self.own[:, cols] = term[:height]
            self.outgoing[0, :, cols] = term[height:].astype(BF16)

        tiles(width, tile, near)
        for chunk in range(CHUNKS):
            self.relay(chunk)
        self.start(0)

    def finish(self):
        for kind in range(3):
            for chunk in range(CHUNKS):
                self.copy(kind, chunk).wait_send()


def scatter_scratch(height, width):
    return dict(
        own=pltpu.VMEM((height, width), F32),
        passing=pltpu.VMEM((height, width), F32),
        outgoing=pltpu.VMEM((3, height, width), BF16),
        incoming=pltpu.VMEM((3, height, width), BF16),
        send=pltpu.SemaphoreType.DMA((3, CHUNKS)),
        receive=pltpu.SemaphoreType.DMA((3, CHUNKS)),
    )


class Collect:
    def __init__(self, shard, full, send, receive, pair_send, pair_receive, local):
        self.me, self.count = lax.axis_index("seq"), lax.axis_size("seq")
        self.groups = self.count // 2
        self.pair = {"seq": flip(self.me, 1)}
        self.shard, self.full, self.height = shard, full, shard.shape[0]
        self.send, self.receive, self.pair_send, self.pair_receive = send, receive, pair_send, pair_receive
        self.local = pltpu.make_async_copy(shard, self.block(self.me), local.at[0])

    def block(self, index):
        return self.full.at[span(index * self.height, self.height), :]

    def out(self, step):
        peer = {"seq": lax.rem(self.me + 2 * step, self.count)}
        return remote(self.shard, self.block(self.me), self.send.at[step - 1], self.receive.at[step - 1], peer)

    def over(self, step):
        if step == 0:
            source, place = self.shard, self.me
        else:
            place = lax.rem(self.me + self.count - 2 * step, self.count)
            source = self.block(place)
        return remote(source, self.block(place), self.pair_send.at[step], self.pair_receive.at[step], self.pair)

    def kick(self, step):
        if step == 0:
            self.over(0).start()
            self.local.start()
        else:
            self.out(step).start()

    def turn(self, step):
        if step:
            self.out(step).wait_recv()
            self.over(step).start()

    def end(self):
        self.local.wait()
        for step in range(self.groups):
            self.over(step).wait_recv()

    def finish(self):
        for step in range(self.groups):
            self.over(step).wait_send()
            if step:
                self.out(step).wait_send()


def collect_scratch():
    groups = lax.axis_size("seq") // 2
    return dict(
        send=pltpu.SemaphoreType.DMA((groups,)),
        receive=pltpu.SemaphoreType.DMA((groups,)),
        pair_send=pltpu.SemaphoreType.DMA((groups,)),
        pair_receive=pltpu.SemaphoreType.DMA((groups,)),
        local=pltpu.SemaphoreType.DMA((1,)),
    )


class Settle:
    def __init__(self, source, result, partner, others, send, receive, far_send, far_receive, half=None, load=None):
        self.me, self.count = lax.axis_index("seq"), lax.axis_size("seq")
        self.groups = self.count // 2
        self.other = flip(self.me, 1)
        self.source, self.result, self.half, self.partner, self.others = source, result, half, partner, others
        self.height = result.shape[0]
        self.load, self.send, self.receive = load, send, receive
        self.far_send, self.far_receive = far_send, far_receive

    def block(self, base, step):
        place = lax.rem(base + 2 * step, self.count)
        return self.source.at[span(place * self.height, self.height), :]

    def mine(self, step):
        return self.block(self.me, step) if self.half is None else self.half.at[step]

    def swap(self, step):
        return remote(
            self.block(self.other, step),
            self.partner.at[step],
            self.send.at[step],
            self.receive.at[step],
            {"seq": self.other},
        )

    def fetch(self, step):
        return pltpu.make_async_copy(self.block(self.me, step), self.half.at[step], self.load.at[step])

    def away(self, step):
        peer = {"seq": lax.rem(self.me + 2 * step, self.count)}
        return remote(
            self.mine(step), self.others.at[step], self.far_send.at[step], self.far_receive.at[step], peer
        )

    def kick(self, step):
        self.swap(step).start()
        if self.half is not None:
            self.fetch(step).start()

    def turn(self, step):
        if step:
            if self.half is not None:
                self.fetch(step).wait()
            self.swap(step).wait_recv()
            mine = self.mine(step)
            mine[...] = (mine[...].astype(F32) + self.partner[step].astype(F32)).astype(BF16)
            self.away(step).start()

    def end(self):
        if self.half is not None:
            self.fetch(0).wait()
        self.swap(0).wait_recv()
        total = self.mine(0)[...].astype(F32) + self.partner[0].astype(F32)
        for step in range(1, self.groups):
            self.away(step).wait_recv()
            total = total + self.others[step].astype(F32)
        self.result[...] = total

    def finish(self):
        for step in range(self.groups):
            self.swap(step).wait_send()
            if step:
                self.away(step).wait_send()


def settle_scratch(height, width, apart=False):
    groups = lax.axis_size("seq") // 2
    more = dict(half=pltpu.VMEM((groups, height, width), BF16), load=pltpu.SemaphoreType.DMA((groups,)))
    return dict(
        **(more if apart else {}),
        partner=pltpu.VMEM((groups, height, width), BF16),
        others=pltpu.VMEM((groups, height, width), BF16),
        send=pltpu.SemaphoreType.DMA((groups,)),
        receive=pltpu.SemaphoreType.DMA((groups,)),
        far_send=pltpu.SemaphoreType.DMA((groups,)),
        far_receive=pltpu.SemaphoreType.DMA((groups,)),
    )


class Plan:
    def __init__(self, points, tasks):
        self.points, self.tasks = points, tasks
        self.left = {(name, kind, step) for name in tasks for kind in "kt" for step in range(4)}

    def at(self, point):
        for word in self.points.get(point, "").split():
            name, kind, digit = word[:-2], word[-2], int(word[-1])
            self.left.remove((name, kind, digit))
            task = self.tasks[name]
            for step in range(digit, task.groups if digit == 3 else min(digit + 1, task.groups)):
                (task.kick if kind == "k" else task.turn)(step)

    def finish(self):
        assert all(kind == "t" and step == 0 for _, kind, step in self.left), "steps left"
        for task in self.tasks.values():
            task.finish()


class Swap:
    def __init__(self, blocks, send, receive):
        self.me, self.count = lax.axis_index("seq"), lax.axis_size("seq")
        self.blocks, self.send, self.receive = blocks, send, receive

    def copy(self, step):
        peer = {"seq": lax.rem(self.me + step, self.count)}
        return remote(self.blocks.at[0], self.blocks.at[step], self.send.at[step], self.receive.at[step], peer)

    def start(self):
        for step in range(1, self.count):
            self.copy(step).start()

    def wait(self):
        for step in range(1, self.count):
            self.copy(step).wait_recv()

    def finish(self):
        for step in range(1, self.count):
            self.copy(step).wait_send()


def swap_scratch(height, width):
    count = lax.axis_size("seq")
    return dict(
        blocks=pltpu.VMEM((count, height, width), F32),
        send=pltpu.SemaphoreType.DMA((count,)),
        receive=pltpu.SemaphoreType.DMA((count,)),
    )


class Edges:
    def __init__(self, padded, send, receive):
        self.me, self.count = lax.axis_index("seq"), lax.axis_size("seq")
        self.padded, self.send, self.receive = padded, send, receive
        self.frames = padded.shape[0] - 2 * EDGE

    def up(self):
        source = self.padded.at[pl.ds(self.frames, EDGE), :]
        target = self.padded.at[pl.ds(0, EDGE), :]
        peer = {"seq": lax.rem(self.me + 1, self.count)}
        return remote(source, target, self.send.at[0], self.receive.at[0], peer)

    def down(self):
        source = self.padded.at[pl.ds(EDGE, EDGE), :]
        target = self.padded.at[pl.ds(EDGE + self.frames, EDGE), :]
        peer = {"seq": lax.rem(self.me + self.count - 1, self.count)}
        return remote(source, target, self.send.at[1], self.receive.at[1], peer)

    def start(self):
        self.up().start()
        self.down().start()

    def wait(self):
        self.up().wait_recv()
        self.down().wait_recv()

    def finish(self):
        self.up().wait_send()
        self.down().wait_send()


def edges_scratch():
    return dict(send=pltpu.SemaphoreType.DMA((2,)), receive=pltpu.SemaphoreType.DMA((2,)))


def run_kernel(body, number, inputs, outputs, scratch, flops=1 << 33):
    flat, groups = [], []
    for name, item in scratch.items():
        parts = item if isinstance(item, dict) else {None: item}
        groups.append((name, list(parts)))
        flat.extend(parts.values())

    def kernel(*refs):
        given = dict(zip(list(inputs) + list(outputs), refs))
        rest = list(refs[len(given) :])
        for name, keys in groups:
            taken = {key: rest.pop(0) for key in keys}
            given[name] = taken[None] if None in taken else taken
        body(SimpleNamespace(**given))

    results = pl.pallas_call(
        kernel,
        out_shape=tuple(jax.ShapeDtypeStruct(shape, kind) for shape, kind, _ in outputs.values()),
        in_specs=[IN_VMEM if near else IN_PLACE for _, near in inputs.values()],
        out_specs=tuple(IN_VMEM if near else IN_PLACE for _, _, near in outputs.values()),
        scratch_shapes=flat,
        compiler_params=pltpu.CompilerParams(
            collective_id=number, has_side_effects=True, vmem_limit_bytes=VMEM_LIMIT
        ),
        cost_estimate=pl.CostEstimate(flops=flops, bytes_accessed=16 << 20, transcendentals=0),
    )(*[array for array, _ in inputs.values()])
    return SimpleNamespace(**dict(zip(outputs, results)))


def ffn_forward(gather, scatter, win, wout, hidden, active, wait_in, wait_out, late=False, at=lambda point: None):
    rows, height, piece = gather.rows, gather.height, gather.piece
    width, inner = win.shape
    pair = pl.ds(0, 2 * height)
    gather.wait_near()
    wait_in()

    def first(cols):
        product = plain_product(rows[pair, :], win[:, cols])
        hidden[pair, cols] = product
        active[pair, cols] = swish(product).astype(BF16)

    def second(cols):
        product = plain_product(active[pair, :], wout[:, cols])
        scatter.own[:, cols] = product[:height]
        scatter.outgoing[0, :, cols] = product[height:].astype(BF16)

    def far_rows(chunk):
        return (
            pl.ds(2 * height + chunk * piece, piece),
            pl.ds(3 * height + chunk * piece, piece),
            scatter.rows(chunk),
        )

    def inward(chunk):
        low, high, here = far_rows(chunk)

        def third(cols):
            both = jnp.concatenate([rows[low, :], rows[high, :]], axis=0)
            product = plain_product(both, win[:, cols])
            hidden[low, cols] = product[:piece]
            hidden[high, cols] = product[piece:]
            alive = swish(product).astype(BF16)
            active[low, cols] = alive[:piece]
            active[high, cols] = alive[piece:]

        gather.wait_last(chunk)
        tiles(inner, 512, third)

    def outward(chunk):
        low, high, here = far_rows(chunk)

        def fourth(cols):
            both = jnp.concatenate([active[low, :], active[high, :]], axis=0)
            product = plain_product(both, wout[:, cols])
            scatter.passing[here, cols] = product[:piece]
            scatter.outgoing[1, here, cols] = product[piece:].astype(BF16)

        tiles(width, 512, fourth)
        scatter.copy(1, chunk).start()
        scatter.relay(chunk)

    tiles(inner, 512, first)
    at("first")
    gather.pass_on(0)
    if late:
        for chunk in range(CHUNKS):
            if chunk > 0:
                gather.pass_on(chunk)
            inward(chunk)
            at(f"inward{chunk}")
        wait_out()
        for chunk in range(CHUNKS):
            outward(chunk)
            at(f"outward{chunk}")
    else:
        wait_out()
        tiles(width, 512, second)
        scatter.start(0)
        for chunk in range(CHUNKS):
            if chunk > 0:
                gather.pass_on(chunk)
            inward(chunk)
            outward(chunk)
    if late:
        tiles(width, 512, second)
        scatter.start(0)


def ffn_backward(gather, scatter, win, wout, hidden, active, slope, wait_out, wait_in, products=None, at=lambda point: None):
    rows, height, piece = gather.rows, gather.height, gather.piece
    width, inner = win.shape
    pair = pl.ds(0, 2 * height)
    gather.wait_near()
    wait_out()

    def bend(product, before):
        logistic = jax.nn.sigmoid(before)
        return (
            (before * logistic).astype(BF16),
            (product * (logistic * (1.0 + before * (1.0 - logistic)))).astype(BF16),
        )

    def first(cols):
        alive, steep = bend(across_product(rows[pair, :], wout[cols, :]), hidden[pair, cols])
        if active is not None:
            active[pair, cols] = alive
        slope[pair, cols] = steep

    def second(cols):
        product = across_product(slope[pair, :], win[cols, :])
        scatter.own[:, cols] = product[:height]
        scatter.outgoing[0, :, cols] = product[height:].astype(BF16)

    def far_rows(chunk):
        return (
            pl.ds(2 * height + chunk * piece, piece),
            pl.ds(3 * height + chunk * piece, piece),
            scatter.rows(chunk),
        )

    def inward(chunk):
        low, high, here = far_rows(chunk)

        def third(cols):
            both = jnp.concatenate([rows[low, :], rows[high, :]], axis=0)
            before = jnp.concatenate([hidden[low, cols], hidden[high, cols]], axis=0)
            alive, steep = bend(across_product(both, wout[cols, :]), before)
            if active is not None:
                active[low, cols] = alive[:piece]
                active[high, cols] = alive[piece:]
            slope[low, cols] = steep[:piece]
            slope[high, cols] = steep[piece:]

        gather.wait_last(chunk)
        tiles(inner, 256, third)

    def outward(chunk):
        low, high, here = far_rows(chunk)

        def fourth(cols):
            both = jnp.concatenate([slope[low, :], slope[high, :]], axis=0)
            product = across_product(both, win[cols, :])
            scatter.passing[here, cols] = product[:piece]
            scatter.outgoing[1, here, cols] = product[piece:].astype(BF16)

        tiles(width, 512, fourth)
        scatter.copy(1, chunk).start()
        scatter.relay(chunk)

    tiles(inner, 256, first)
    at("first")
    gather.pass_on(0)
    if products is not None:
        for chunk in range(CHUNKS):
            if chunk > 0:
                gather.pass_on(chunk)
            inward(chunk)
        products()
        wait_in()
        for chunk in range(CHUNKS):
            outward(chunk)
            at(f"outward{chunk}")
        tiles(width, 512, second)
        scatter.start(0)
        at("second")
    else:
        wait_in()
        tiles(width, 512, second)
        scatter.start(0)
        for chunk in range(CHUNKS):
            if chunk > 0:
                gather.pass_on(chunk)
            inward(chunk)
            outward(chunk)


def weight_products(result, left, right, tile=256):
    def one(cols):
        result[:, cols] = inner_product(left[...], right[:, cols]).astype(BF16)

    tiles(right.shape[1], tile, one)


OPEN_PLAN = dict(
    start="ik1 ik3 ik2 ik0 ok1 ok3 ok2 ok0",
    gather="it1 it3 it2 ot1",
    out="ot3 ot2 pk1 pk2 pk3 pk0",
    outward1="pt1 pt2",
    total0="pt3 ak1 ak2 ak3 ak0",
    near="at1 at2 at3",
)


def open_kernel(n):
    height, width = n.values.shape
    frames = 4 * height
    local = n.queries.shape[1]
    seq, count = lax.axis_index("seq"), lax.axis_size("seq")
    first_in = Collect(n.shard_in, n.win, **n.c_in)
    first_out = Collect(n.shard_out, n.wout, **n.c_out)
    project = Collect(n.shard_project, n.wproject, **n.c_project)
    attend_out = Collect(n.shard_attend, n.full_attend, **n.c_attend)
    plan = Plan(OPEN_PLAN, dict(i=first_in, o=first_out, p=project, a=attend_out))
    gather = Gather(n.rows, **n.g1)
    scatter = Scatter(**n.s1)
    gather_two = Gather(n.rows_two, **n.g2)
    ready = greet(tp_peers() + seq_peers())
    n.rows[pl.ds(0, gather.piece), :] = norm_rows(
        n.values[pl.ds(0, gather.piece), :].astype(F32), n.gains[0:1, :]
    ).astype(BF16)
    ready()
    plan.at("start")
    for chunk in range(CHUNKS):
        here = scatter.rows(chunk)
        if chunk > 0:
            n.rows[here, :] = norm_rows(n.values[here, :].astype(F32), n.gains[0:1, :]).astype(BF16)
        gather.start(chunk)
    plan.at("gather")
    keeps = [
        pltpu.make_async_copy(n.win, n.full_in, n.keep.at[0]),
        pltpu.make_async_copy(n.wout, n.full_out, n.keep.at[1]),
        pltpu.make_async_copy(n.wproject, n.full_project, n.keep.at[2]),
    ]

    def wait_in():
        first_in.end()
        keeps[0].start()

    def wait_out():
        plan.at("out")
        first_out.end()
        keeps[1].start()

    ffn_forward(gather, scatter, n.win, n.wout, n.hidden, n.active, wait_in, wait_out, late=True, at=plan.at)
    for chunk in range(CHUNKS):
        here = scatter.rows(chunk)
        n.first[here, :] = n.values[here, :].astype(F32) + 0.5 * scatter.total(chunk)
        n.rows_two[here, :] = norm_rows(n.first[here, :], n.gains[1:2, :]).astype(BF16)
        gather_two.start(chunk)
        plan.at(f"total{chunk}")
    project.end()
    keeps[2].start()
    gather_two.wait_near()

    def send_block(slot):
        place = owner(slot)
        source = n.pair_own.at[span(place * height, height), :]
        upper = lax.div(place, 2)

        def piece(kind):
            if kind == 0:
                peer, row = lax.rem(seq + 1, count), MAXLEN - frames + place * height
            elif kind == 1:
                peer, row = lax.rem(seq + count - 1, count), MAXLEN + frames + place * height
            else:
                peer = lax.rem(seq + count - 2 + 4 * upper, count)
                row = MAXLEN + place * height + 2 * frames * (1 - 2 * upper)
            target = n.window.at[span(row, height), :]
            return remote(source, target, n.halo_send.at[kind, slot], n.halo_receive.at[kind, slot], {"seq": peer})

        return [piece(kind) for kind in range(3)]

    def there(kind, slot, sending):
        upper = lax.div(owner(slot), 2)
        if kind == 2:
            shift = 4 * upper - 2
        else:
            shift = 1 - 2 * kind
        target = seq + shift if sending else seq - shift
        return (target >= 0) & (target < count)

    def project_rows(slots, low):
        for part in range(3):
            cols = pl.ds(part * local, local)
            product = plain_product(n.rows_two[low, :], n.wproject[:, cols]).astype(BF16)
            for index, slot in enumerate(slots):
                rows = product[index * height : (index + 1) * height]
                place = span(owner(slot) * height, height)
                if part == 0:
                    n.queries[place, :] = rows
                else:
                    n.pair_own[place, pl.ds((part - 1) * local, local)] = rows
        for slot in slots:
            for kind, copy in enumerate(send_block(slot)):

                @pl.when(there(kind, slot, True))
                def _():
                    copy.start()

    project_rows((0, 1), pl.ds(0, 2 * height))
    for chunk in range(CHUNKS):
        gather_two.pass_on(chunk)
    plan.at("near")
    for chunk in range(CHUNKS):
        gather_two.wait_last(chunk)
    project_rows((2, 3), pl.ds(2 * height, 2 * height))
    own = pltpu.make_async_copy(n.pair_own, n.window.at[pl.ds(MAXLEN, frames), :], n.keep.at[3])
    own.start()
    for slot in range(4):
        for kind, copy in enumerate(send_block(slot)):

            @pl.when(there(kind, slot, False))
            def _():
                copy.wait_recv()

            @pl.when(there(kind, slot, True))
            def _():
                copy.wait_send()

    attend_out.end()
    for keep in keeps:
        keep.wait()
    own.wait()
    plan.finish()
    for item in [gather, scatter, gather_two]:
        item.finish()


def run_open(values, gains, shards):
    height, width = values.shape
    frames = 4 * height
    count = lax.axis_size("seq")
    inner, local = shards.ffn1_in.shape[1], shards.attend.shape[0] * count
    fulls = dict(
        full_in=shards.ffn1_in, full_out=shards.ffn1_out, full_project=shards.project,
        full_attend=shards.attend,
    )
    return run_kernel(
        open_kernel,
        0,
        dict(
            values=(values, True), gains=(gains, True), shard_in=(shards.ffn1_in, True),
            shard_out=(shards.ffn1_out, True), shard_project=(shards.project, True),
            shard_attend=(shards.attend, True),
        ),
        dict(
            first=((height, width), F32, True),
            rows=((frames, width), BF16, True),
            hidden=((frames, inner), F32, True),
            rows_two=((frames, width), BF16, True),
            queries=((frames, local), BF16, True),
            window=((frames + 2 * MAXLEN, 2 * local), BF16, False),
            **{name: ((item.shape[0] * count, item.shape[1]), BF16, False) for name, item in fulls.items()},
        ),
        dict(
            win=pltpu.VMEM((width, inner), BF16),
            wout=pltpu.VMEM((inner, width), BF16),
            wproject=pltpu.VMEM((width, 3 * local), BF16),
            active=pltpu.VMEM((frames, inner), BF16),
            pair_own=pltpu.VMEM((frames, 2 * local), BF16),
            c_in=collect_scratch(), c_out=collect_scratch(), c_project=collect_scratch(),
            c_attend=collect_scratch(),
            g1=gather_scratch(), s1=scatter_scratch(height, width), g2=gather_scratch(),
            halo_send=pltpu.SemaphoreType.DMA((3, 4)), halo_receive=pltpu.SemaphoreType.DMA((3, 4)),
            keep=pltpu.SemaphoreType.DMA((4,)),
        ),
    )


def slot_rows(slots, height):
    return pl.ds(slots[0] * height, 2 * height)


def in_order(swap):
    for place in range(swap.count):
        yield swap.blocks[lax.rem(swap.me + swap.count - place, swap.count)]


def middle_kernel(n):
    height, width = n.first.shape
    frames = 4 * height
    local = n.mixed.shape[1]
    block = 128
    none = jnp.zeros((1, local), F32)
    pair_weight, conv_weight = Collect(n.shard_pair, n.wpair, **n.c_pair), Collect(n.shard_conv, n.wconv, **n.c_conv)
    in_weight, out_weight = Collect(n.shard_in, n.win, **n.c_in), Collect(n.shard_out, n.wout, **n.c_out)
    out_sum, in_sum = Settle(n.grad_out, n.sum_out, **n.t_out), Settle(n.grad_in, n.sum_in, **n.t_in)
    plan = Plan(
        MIDDLE_PLAN,
        dict(p=pair_weight, c=conv_weight, i=in_weight, o=out_weight, O=out_sum, I=in_sum),
    )
    scatter = Scatter(**n.s1)
    gathers = [
        Gather(n.rows_conv, **n.g1), Gather(n.rows, **n.g2), Gather(n.grads, **n.g3),
        Gather(n.grads_conv, **n.g4), Gather(n.grads, **n.g5),
    ]
    edges, edges_back = Edges(n.gated, **n.edge), Edges(n.back, **n.edge_back)
    swap, swap_back = Swap(**n.swap), Swap(**n.swap_back)
    chunks = [scatter.rows(chunk) for chunk in range(CHUNKS)]
    ready = greet(tp_peers() + seq_peers())
    for slot in range(4):
        n.mixed_low[pl.ds(slot * height, height), :] = n.mixed[span(owner(slot) * height, height), :].astype(BF16)
    ready()
    plan.at("start")
    scatter.spread(
        lambda slots, cols: plain_product(n.mixed_low[slot_rows(slots, height), :], n.wattend[:, cols]), width
    )
    gather = gathers[0]
    plan.at("spread")
    for chunk, here in enumerate(chunks):
        n.second[here, :] = n.first[here, :] + scatter.total(chunk)
        n.rows_conv[here, :] = norm_rows(n.second[here, :], n.gains[2:3, :]).astype(BF16)
        gather.start(chunk)
        plan.at(f"second{chunk}")
    scatter.finish()
    gather.wait_near()
    pair_weight.end()

    def pair_rows(slots):
        product = plain_product(n.rows_conv[slot_rows(slots, height), :], n.wpair[...])
        for index, slot in enumerate(slots):
            rows = product[index * height : (index + 1) * height]
            place = owner(slot) * height
            n.paired[span(place, height), :] = rows
            real = n.context[span(place, height), KERNEL : KERNEL + 1]
            gated = rows[:, :local] * jax.nn.sigmoid(rows[:, local:]) * real
            n.gated[pl.ds(pl.multiple_of(EDGE + place, EDGE), height), :] = gated.astype(BF16).astype(F32)

    pair_rows((0, 1))
    for chunk in range(CHUNKS):
        gather.pass_on(chunk)
    plan.at("passed")
    for chunk in range(CHUNKS):
        gather.wait_last(chunk)
    pair_rows((2, 3))
    edges.start()

    def convolve(index, carried):
        total, real_count = carried
        around = n.gated[pl.ds(pl.multiple_of(index * block, block), block + 2 * EDGE), :]
        marks = n.context[span(index * block, block), :]
        conv = jnp.zeros((block, local), F32)
        for tap in range(KERNEL):
            begin = EDGE - KERNEL // 2 + tap
            conv = conv + n.depth[tap : tap + 1, :] * around[begin : begin + block] * marks[:, tap : tap + 1]
        n.normal[span(index * block, block), :] = conv
        real = marks[:, KERNEL : KERNEL + 1]
        return (
            total + jnp.sum(real * conv, axis=0, keepdims=True),
            real_count + jnp.sum(jnp.broadcast_to(real, conv.shape), axis=0, keepdims=True),
        )

    last = frames // block - 1
    carried = lax.fori_loop(1, last, convolve, (none, none))
    edges.wait()
    plan.at("edges")
    total, real_count = convolve(last, convolve(0, carried))
    middle = total / jnp.maximum(real_count, 1.0)

    def deviate(index, carried):
        conv = n.normal[span(index * block, block), :]
        real = n.context[span(index * block, block), KERNEL : KERNEL + 1]
        away = conv - middle
        return carried + jnp.sum(real * away * away, axis=0, keepdims=True)

    squares = lax.fori_loop(0, frames // block, deviate, none)
    swap.blocks[0, 0:1, :] = total
    swap.blocks[0, 1:2, :] = squares
    swap.blocks[0, 2:3, :] = real_count
    swap.start()
    swap.wait()
    plan.at("swapped")
    total_all, real_all = none, none
    for item in in_order(swap):
        total_all = total_all + item[0:1]
        real_all = real_all + item[2:3]
    centre = total_all / real_all
    squares_all = none
    for item in in_order(swap):
        away = item[0:1] / jnp.maximum(item[2:3], 1.0) - centre
        squares_all = squares_all + item[1:2] + item[2:3] * away * away
    inverse = lax.rsqrt(squares_all / real_all + EPSILON)
    for slot in range(4):
        place = span(owner(slot) * height, height)
        normal = (n.normal[place, :] - centre) * inverse
        n.normal[place, :] = normal
        n.alive[pl.ds(slot * height, height), :] = swish(normal * n.bn_gain[...] + n.bn_bias[...]).astype(BF16)
    conv_weight.end()
    scatter.spread(
        lambda slots, cols: plain_product(n.alive[slot_rows(slots, height), :], n.wconv[:, cols]), width
    )
    plan.at("alive")
    gather = gathers[1]
    for chunk, here in enumerate(chunks):
        n.third[here, :] = n.second[here, :] + scatter.total(chunk)
        n.rows[here, :] = norm_rows(n.third[here, :], n.gains[3:4, :]).astype(BF16)
        gather.start(chunk)
        plan.at(f"third{chunk}")
    scatter.finish()
    ffn_forward(gather, scatter, n.win, n.wout, n.hidden, n.active, in_weight.end, out_weight.end, True, plan.at)
    gather = gathers[2]
    gain_four = jnp.zeros((1, width), F32)
    for chunk, here in enumerate(chunks):
        fourth = n.third[here, :] + 0.5 * scatter.total(chunk)
        n.output[here, :] = norm_rows(fourth, n.gains[4:5, :]).astype(BF16)
        grad, gain = norm_back(fourth, n.gains[4:5, :], n.out_grad[here, :].astype(F32))
        gain_four = gain_four + gain
        n.grad_row[here, :] = grad
        n.grads[here, :] = (0.5 * grad).astype(BF16)
        gather.start(chunk)
    scatter.finish()

    def nothing():
        return None

    ffn_backward(gather, scatter, n.win, n.wout, n.hidden, None, n.slope, nothing, nothing)
    weight_products(n.grad_out, n.active, n.grads)
    plan.at("grad_out")
    weight_products(n.grad_in, n.rows, n.slope)
    plan.at("grad_in")
    gathers[2].finish()
    gather = gathers[3]
    gain_three = jnp.zeros((1, width), F32)
    for chunk, here in enumerate(chunks):
        grad, gain = norm_back(n.third[here, :], n.gains[3:4, :], scatter.total(chunk))
        gain_three = gain_three + gain
        n.grad_row[here, :] += grad
        n.grads_conv[here, :] = n.grad_row[here, :].astype(BF16)
        gather.start(chunk)
    scatter.finish()
    plan.at("back_start")
    gather.wait_near()
    sums = [none, none]

    def batch_rows(slots):
        product = across_product(n.grads_conv[slot_rows(slots, height), :], n.wconv[...])
        for index, slot in enumerate(slots):
            place = span(owner(slot) * height, height)
            normal = n.normal[place, :]
            batch = normal * n.bn_gain[...] + n.bn_bias[...]
            logistic = jax.nn.sigmoid(batch)
            rows = product[index * height : (index + 1) * height]
            grad = rows * (logistic * (1.0 + batch * (1.0 - logistic)))
            n.grad_batch[place, :] = grad
            sums[0] = sums[0] + jnp.sum(grad * normal, axis=0, keepdims=True)
            sums[1] = sums[1] + jnp.sum(grad, axis=0, keepdims=True)

    batch_rows((0, 1))
    plan.at("back_near")
    for chunk in range(CHUNKS):
        gather.pass_on(chunk)
    plan.at("back_passed")
    for chunk in range(CHUNKS):
        gather.wait_last(chunk)
    batch_rows((2, 3))
    swap_back.blocks[0, 0:1, :] = sums[0]
    swap_back.blocks[0, 1:2, :] = sums[1]
    swap_back.start()
    weight_products(n.grad_conv, n.alive, n.grads_conv, 512)
    plan.at("grad_conv")
    swap_back.wait()
    grad_gain, grad_bias = none, none
    for item in in_order(swap_back):
        grad_gain = grad_gain + item[0:1]
        grad_bias = grad_bias + item[1:2]
    n.bn_sums[0:1, :] = grad_gain
    n.bn_sums[1:2, :] = grad_bias
    gain = n.bn_gain[...]

    def deconvolve(index, nothing):
        here = span(index * block, block)
        real = n.context[here, KERNEL : KERNEL + 1]
        drift = real * (gain * grad_bias + n.normal[here, :] * gain * grad_gain) / real_all
        n.back[pl.ds(pl.multiple_of(EDGE + index * block, EDGE), block), :] = inverse * (
            n.grad_batch[here, :] * gain - drift
        )
        return nothing

    lax.fori_loop(0, frames // block, deconvolve, 0)
    edges_back.start()
    plan.at("edges_back")
    me = lax.axis_index("tp")

    def part(index, carried):
        here = span(index * block, block)
        around = pl.ds(pl.multiple_of(index * block, block), block + 2 * EDGE)
        back, gated = n.back[around, :], n.gated[around, :]
        marks = n.context[here, :]
        own = back[EDGE : EDGE + block]
        grad = jnp.zeros((block, local), F32)
        result = []
        for tap in range(KERNEL):
            first = EDGE - KERNEL // 2 + tap
            mark = marks[:, tap : tap + 1]
            result.append(
                carried[tap] + jnp.sum(gated[first : first + block] * mark * own, axis=0, keepdims=True)
            )
            mirror = KERNEL - 1 - tap
            grad = grad + n.depth[mirror : mirror + 1, :] * back[first : first + block] * mark
        grad = grad * marks[:, KERNEL : KERNEL + 1]
        both = n.paired[here, :]
        logistic = jax.nn.sigmoid(both[:, local:])
        place = lax.div(index * block, height)
        slot = lax.rem(place + me, 2) + 2 * lax.rem(lax.div(place, 2) + lax.div(me, 2), 2)
        rows = span(slot * height + lax.rem(index * block, height), block)
        n.grad_paired[rows, pl.ds(0, local)] = (grad * logistic).astype(BF16)
        n.grad_paired[rows, pl.ds(local, local)] = (
            grad * both[:, :local] * logistic * (1.0 - logistic)
        ).astype(BF16)
        return tuple(result)

    taps = lax.fori_loop(1, last, part, (none,) * KERNEL)
    edges_back.wait()
    plan.at("parts")
    taps = part(last, part(0, taps))
    for tap in range(KERNEL):
        n.depth_sums[tap : tap + 1, :] = taps[tap]
    plan.at("taps")
    scatter.spread(
        lambda slots, cols: across_product(n.grad_paired[slot_rows(slots, height), :], n.wpair[cols, :]), width
    )
    plan.at("back_spread")
    weight_products(n.grad_pair, n.rows_conv, n.grad_paired)
    plan.at("grad_pair")
    gather = gathers[4]
    gain_two = jnp.zeros((1, width), F32)
    for chunk, here in enumerate(chunks):
        grad, gain = norm_back(n.second[here, :], n.gains[2:3, :], scatter.total(chunk))
        gain_two = gain_two + gain
        n.grad_second[here, :] = n.grad_row[here, :] + grad
        n.grads[here, :] = n.grad_second[here, :].astype(BF16)
        gather.start(chunk)
        plan.at(f"back_second{chunk}")
    scatter.finish()
    n.gain_sums[0:1, :] = gain_two
    n.gain_sums[1:2, :] = gain_three
    n.gain_sums[2:3, :] = gain_four
    gather.wait_near()

    def mixed_rows(slots):
        product = across_product(n.grads[slot_rows(slots, height), :], n.wattend[...]).astype(BF16)
        for index, slot in enumerate(slots):
            n.grad_mixed[span(owner(slot) * height, height), :] = product[index * height : (index + 1) * height]

    mixed_rows((0, 1))
    for chunk in range(CHUNKS):
        gather.pass_on(chunk)
    plan.at("last_passed")
    out_sum.end()
    in_sum.end()
    for chunk in range(CHUNKS):
        gather.wait_last(chunk)
    mixed_rows((2, 3))
    weight_products(n.grad_attend, n.mixed_low, n.grads, 512)
    plan.finish()
    for item in gathers[:2] + gathers[3:] + [edges, edges_back, swap, swap_back]:
        item.finish()


MIDDLE_PLAN = dict(
    start="pk1 pk3 pk2 pk0 ck1 ck3 ck2 ck0",
    spread="pt1 pt3",
    second0="pt2",
    second1="ct1 ct3 ct2 ik1 ik0 ik3",
    passed="it1",
    edges="it3 ik2",
    swapped="it2 ok1 ok0 ok3",
    alive="ot1",
    third0="ot3 ok2",
    first="ot2",
    grad_out="Ok1 Ok3 Ok2 Ok0",
    back_start="Ot1",
    back_near="Ot3",
    back_passed="Ot2",
    edges_back="Ik1 Ik3 Ik2 Ik0",
    parts="It1",
    back_spread="It3 It2",
)


def run_middle(mixed, opened, gains, context, depth, bn_gain, bn_bias, shards, out_grad):
    height, width = opened.first.shape
    frames, local = mixed.shape
    count = lax.axis_size("seq")
    inner = shards.ffn2_in.shape[1]
    settled = dict(out=(inner, width), **{"in": (width, inner)})
    weights = ("out", "in", "conv", "pair")
    return run_kernel(
        middle_kernel,
        1,
        dict(
            mixed=(mixed, True), first=(opened.first, True), gains=(gains, True), wattend=(opened.full_attend, True),
            context=(context, True), depth=(depth, True), bn_gain=(bn_gain, True), bn_bias=(bn_bias, True),
            out_grad=(out_grad, True), shard_pair=(shards.pair, True), shard_conv=(shards.conv, True),
            shard_in=(shards.ffn2_in, True), shard_out=(shards.ffn2_out, True),
        ),
        dict(
            output=((height, width), BF16, True),
            grad_second=((height, width), F32, True),
            grad_mixed=((frames, local), BF16, True),
            grad_attend=((local, width), BF16, True),
            grad_conv=((local, width), BF16, True),
            grad_pair=((width, 2 * local), BF16, True),
            depth_sums=((8, local), F32, True),
            bn_sums=((8, local), F32, True),
            gain_sums=((8, width), F32, True),
            **{f"sum_{name}": ((tall // count, wide), F32, True) for name, (tall, wide) in settled.items()},
        ),
        dict(
            wpair=pltpu.VMEM((width, 2 * local), BF16), wconv=pltpu.VMEM((local, width), BF16),
            win=pltpu.VMEM((width, inner), BF16), wout=pltpu.VMEM((inner, width), BF16),
            second=pltpu.VMEM((height, width), F32), third=pltpu.VMEM((height, width), F32),
            grad_row=pltpu.VMEM((height, width), F32),
            rows_conv=pltpu.VMEM((frames, width), BF16), rows=pltpu.VMEM((frames, width), BF16),
            grads=pltpu.VMEM((frames, width), BF16), grads_conv=pltpu.VMEM((frames, width), BF16),
            hidden=pltpu.VMEM((frames, inner), F32), active=pltpu.VMEM((frames, inner), BF16),
            slope=pltpu.VMEM((frames, inner), BF16),
            mixed_low=pltpu.VMEM((frames, local), BF16), paired=pltpu.VMEM((frames, 2 * local), F32),
            gated=pltpu.VMEM((frames + 2 * EDGE, local), F32), normal=pltpu.VMEM((frames, local), F32),
            alive=pltpu.VMEM((frames, local), BF16), grad_batch=pltpu.VMEM((frames, local), F32),
            back=pltpu.VMEM((frames + 2 * EDGE, local), F32), grad_paired=pltpu.VMEM((frames, 2 * local), BF16),
            **{f"grad_{name}": pltpu.VMEM((tall, wide), BF16) for name, (tall, wide) in settled.items()},
            **{f"t_{name}": settle_scratch(tall // count, wide) for name, (tall, wide) in settled.items()},
            **{f"c_{name}": collect_scratch() for name in weights},
            **{f"g{place}": gather_scratch() for place in range(1, 6)},
            s1=scatter_scratch(height, width),
            edge=edges_scratch(), edge_back=edges_scratch(), swap=swap_scratch(8, local), swap_back=swap_scratch(8, local),
        ),
    )


def close_kernel(n):
    height, width = n.grad_second.shape
    frames = 4 * height
    local = n.grad_query.shape[1]
    seq, count = lax.axis_index("seq"), lax.axis_size("seq")
    half = MAXLEN - frames
    loads = [
        pltpu.make_async_copy(n.full_out, n.wout, n.load.at[0]),
        pltpu.make_async_copy(n.full_hidden, n.hidden, n.load.at[1]),
        pltpu.make_async_copy(n.full_in, n.win, n.load.at[2]),
        pltpu.make_async_copy(n.grad_key.at[pl.ds(MAXLEN, frames), :], n.own_back.at[0], n.load.at[3]),
        pltpu.make_async_copy(n.grad_value.at[pl.ds(MAXLEN, frames), :], n.own_back.at[1], n.load.at[4]),
    ]
    for load in loads:
        load.start()
    attend_sum = Settle(n.grad_attend, n.sum_attend, **n.t_attend)
    conv_sum = Settle(n.grad_conv, n.sum_conv, **n.t_conv)
    pair_sum = Settle(n.grad_pair, n.sum_pair, **n.t_pair)
    project = Settle(n.grad_project, n.sum_project, **n.t_project)
    last = [Settle(n.grad_out, n.sum_out, **n.t_out), Settle(n.grad_in, n.sum_in, **n.t_in)]
    scatter, gather, scatter_two = Scatter(**n.s1), Gather(n.grads, **n.g1), Scatter(**n.s2)
    swap = Swap(**n.swap)
    plan = Plan(
        CLOSE_PLAN, dict(a=attend_sum, c=conv_sum, d=pair_sum, p=project, o=last[0], i=last[1])
    )
    ready = greet(tp_peers() + seq_peers())
    shifts = (1, -1, 2, -2)
    sources = ((MAXLEN + frames, frames), (MAXLEN - frames, frames), (MAXLEN + 2 * frames, half), (0, half))
    targets = ((0, 0), (1, 0), (2, 0), (2, frames - half))

    def back(kind, which):
        begin, size = sources[kind]
        place, row = targets[kind]
        source = (n.grad_key, n.grad_value)[which].at[pl.ds(begin, size), :]
        target = n.others_back.at[which, place, pl.ds(row, size), :]
        peer = {"seq": lax.rem(seq + shifts[kind] + count, count)}
        return remote(source, target, n.back_send.at[which, kind], n.back_receive.at[which, kind], peer)

    def there(kind, sending):
        other = seq + shifts[kind] if sending else seq - shifts[kind]
        return (other >= 0) & (other < count)

    for kind in range(4):
        place, row = targets[kind]

        @pl.when(jnp.logical_not(there(kind, False)))
        def _():
            for which in range(2):
                size = sources[kind][1]
                n.others_back[which, place, pl.ds(row, size), :] = jnp.zeros((size, local), BF16)

    ready()
    for kind in range(4):

        @pl.when(there(kind, True))
        def _():
            for which in range(2):
                back(kind, which).start()

    for slot in range(4):
        n.grad_rows[pl.ds(slot * height, height), pl.ds(0, local)] = n.grad_query[span(owner(slot) * height, height), :]
    for kind in range(4):

        @pl.when(there(kind, False))
        def _():
            for which in range(2):
                back(kind, which).wait_recv()

    plan.at("returned")
    loads[3].wait()
    loads[4].wait()
    for slot in range(4):
        place = span(owner(slot) * height, height)
        for which in range(2):
            total = n.own_back[which, place, :].astype(F32)
            for other in range(3):
                total = total + n.others_back[which, other, place, :].astype(F32)
            n.grad_rows[pl.ds(slot * height, height), pl.ds((which + 1) * local, local)] = total.astype(BF16)
    scatter.spread(
        lambda slots, cols: across_product(n.grad_rows[slot_rows(slots, height), :], n.wproject[cols, :]), width
    )
    plan.at("spread")
    weight_products(n.grad_project, n.rows_two, n.grad_rows)
    plan.at("grad_project")
    gain_one = jnp.zeros((1, width), F32)
    for chunk in range(CHUNKS):
        here = scatter.rows(chunk)
        grad, gain = norm_back(n.first[here, :], n.gains[1:2, :], scatter.total(chunk))
        gain_one = gain_one + gain
        n.grad_first[here, :] = n.grad_second[here, :] + grad
        n.grads[here, :] = (0.5 * n.grad_first[here, :]).astype(BF16)
        gather.start(chunk)
        plan.at(f"first{chunk}")

    def wait_out():
        loads[0].wait()
        loads[1].wait()

    def products():
        weight_products(n.grad_out, n.active, n.grads)
        plan.at("grad_out")
        weight_products(n.grad_in, n.rows, n.slope)
        plan.at("grad_in")

    ffn_backward(
        gather, scatter_two, n.win, n.wout, n.hidden, n.active, n.slope, wait_out, loads[2].wait, products, plan.at
    )
    gain_zero = jnp.zeros((1, width), F32)
    for chunk in range(CHUNKS):
        here = scatter.rows(chunk)
        grad, gain = norm_back(n.values[here, :].astype(F32), n.gains[0:1, :], scatter_two.total(chunk))
        gain_zero = gain_zero + gain
        n.input_grad[here, :] = n.grad_first[here, :] + grad
        plan.at(f"zero{chunk}")
    n.small[0, 0:1, :] = gain_zero
    n.small[0, 1:2, :] = gain_one
    n.small[0, 2:5, :] = n.gain_late[0:3, :]
    n.small[0, 5:8, :] = jnp.zeros((3, width), F32)
    near, far = tp_peers()
    hop = remote(n.small.at[0], n.small.at[1], n.small_sem.at[0], n.small_sem.at[1], near)
    hop.start()
    hop.wait_recv()
    n.small[2] = n.small[0] + n.small[1]
    hop_two = remote(n.small.at[2], n.small.at[3], n.small_sem.at[2], n.small_sem.at[3], far)
    hop_two.start()
    hop_two.wait_recv()
    swap.blocks[0, :, pl.ds(0, width)] = n.small[2] + n.small[3]
    swap.blocks[0, :, pl.ds(width, local)] = n.depth_sums[...]
    swap.start()
    plan.at("small")
    attend_sum.end()
    conv_sum.end()
    pair_sum.end()
    project.end()
    plan.at("ended")
    swap.wait()
    total = jnp.zeros((8, width + local), F32)
    for item in in_order(swap):
        total = total + item
    n.gain_total[...] = total[:, :width]
    n.depth_total[...] = total[:, width:]
    for task in last:
        task.end()
    for kind in range(4):

        @pl.when(there(kind, True))
        def _():
            for which in range(2):
                back(kind, which).wait_send()

    hop.wait_send()
    hop_two.wait_send()
    plan.finish()
    for item in [scatter, gather, scatter_two, swap]:
        item.finish()


CLOSE_PLAN = dict(
    returned="dk1 dk3 dk2 dk0 ck1 ck3 ck2 ck0 ak1 ak3 ak2 ak0",
    spread="dt1",
    grad_project="dt3 pk1 pk3 pk2 pk0",
    first0="dt2",
    first1="ct1 ct3 ct2",
    first="at1 at3 at2",
    grad_out="pt1 pt3 ok1 ok3 ok2 ok0",
    grad_in="pt2 ik1 ik3 ik2 ik0",
    second="ot1 ot3",
    zero0="ot2",
    small="it1",
    ended="it3 it2",
)


def run_close(values, gains, opened, middle, grad_query, grad_key, grad_value):
    height, width = values.shape
    frames, local = grad_query.shape
    count = lax.axis_size("seq")
    inner = opened.full_in.shape[1]
    settled = dict(
        pair=(width, 2 * local), conv=(local, width), attend=(local, width),
        project=(width, 3 * local), out=(inner, width), **{"in": (width, inner)},
    )
    return run_kernel(
        close_kernel,
        4,
        dict(
            values=(values, True), gains=(gains, True), first=(opened.first, True), rows=(opened.rows, True),
            rows_two=(opened.rows_two, True), full_hidden=(opened.hidden, False),
            full_in=(opened.full_in, False), full_out=(opened.full_out, False),
            wproject=(opened.full_project, True), grad_second=(middle.grad_second, True), grad_query=(grad_query, True),
            grad_key=(grad_key, False), grad_value=(grad_value, False), grad_attend=(middle.grad_attend, False),
            grad_conv=(middle.grad_conv, False), grad_pair=(middle.grad_pair, False),
            depth_sums=(middle.depth_sums, True), gain_late=(middle.gain_sums, True),
        ),
        dict(
            input_grad=((height, width), F32, True),
            gain_total=((8, width), F32, True),
            depth_total=((8, local), F32, True),
            **{f"sum_{name}": ((tall // count, wide), F32, True) for name, (tall, wide) in settled.items()},
        ),
        dict(
            win=pltpu.VMEM((width, inner), BF16), wout=pltpu.VMEM((inner, width), BF16),
            hidden=pltpu.VMEM((frames, inner), F32), active=pltpu.VMEM((frames, inner), BF16),
            slope=pltpu.VMEM((frames, inner), BF16), grads=pltpu.VMEM((frames, width), BF16),
            grad_first=pltpu.VMEM((height, width), F32),
            own_back=pltpu.VMEM((2, frames, local), BF16), others_back=pltpu.VMEM((2, 3, frames, local), BF16),
            grad_rows=pltpu.VMEM((frames, 3 * local), BF16),
            grad_project=pltpu.VMEM((width, 3 * local), BF16),
            grad_in=pltpu.VMEM((width, inner), BF16), grad_out=pltpu.VMEM((inner, width), BF16),
            **{f"t_{name}": settle_scratch(tall // count, wide, name in ("attend", "conv", "pair")) for name, (tall, wide) in settled.items()},
            g1=gather_scratch(), s1=scatter_scratch(height, width), s2=scatter_scratch(height, width),
            swap=swap_scratch(8, width + local),
            small=pltpu.VMEM((4, 8, width), F32), small_sem=pltpu.SemaphoreType.DMA((4,)),
            back_send=pltpu.SemaphoreType.DMA((2, 4)), back_receive=pltpu.SemaphoreType.DMA((2, 4)),
            load=pltpu.SemaphoreType.DMA((5,)),
        ),
    )


def attention_context(segment_ids, pad_mask, frames):
    anchor = lax.axis_index("seq") * frames
    window = frames + 2 * MAXLEN
    codes = jnp.where(pad_mask == 1, segment_ids, -1)
    codes_wide = jnp.pad(codes, (MAXLEN, MAXLEN), constant_values=-2)
    key_codes = lax.dynamic_slice_in_dim(codes_wide, anchor, window)
    query_seg = lax.dynamic_slice_in_dim(segment_ids, anchor, frames)
    blocks = query_seg.reshape(frames // QUERY_BLOCK, QUERY_BLOCK)
    low = jnp.sum((segment_ids[None, :] < blocks[:, :1]).astype(jnp.int32), axis=1)
    high = jnp.sum((segment_ids[None, :] <= blocks[:, -1:]).astype(jnp.int32), axis=1)
    first = (low - anchor + MAXLEN) // KEY_BLOCK
    last = (high - anchor + MAXLEN + KEY_BLOCK - 1) // KEY_BLOCK
    key_codes = jnp.broadcast_to(key_codes[:, None], (window, 128))
    return (first, last, query_seg[None, :], key_codes)


def allowed_block(codes, seg_row, key_begin, query_begin):
    wide = jnp.concatenate([codes] * (QUERY_BLOCK // 128), axis=1)
    place = lax.broadcasted_iota(jnp.int32, (KEY_BLOCK, QUERY_BLOCK), 0) - lax.broadcasted_iota(
        jnp.int32, (KEY_BLOCK, QUERY_BLOCK), 1
    )
    return (wide == seg_row) | (place == query_begin - key_begin)


def attend_kernel(first, last, query, keys, values, seg_row, codes, out, totals):
    step = pl.program_id(1)
    rows = query[...]
    segs = seg_row[...]

    def one(index, carried):
        highest, total, mixed = carried
        begin = pl.multiple_of(index * KEY_BLOCK, KEY_BLOCK)
        key_rows = keys[pl.ds(begin, KEY_BLOCK), :]
        value_rows = values[pl.ds(begin, KEY_BLOCK), :]
        scores = across_product(key_rows, rows) * (SCORE_SCALE * LOG2E)
        allowed = allowed_block(
            codes[pl.ds(begin, KEY_BLOCK), :], segs, begin, MAXLEN + step * QUERY_BLOCK
        )
        scores = jnp.where(allowed, scores, -1e30)
        top = jnp.maximum(highest, jnp.max(scores, axis=0, keepdims=True))
        fade = jnp.exp2(highest - top)
        weights = jnp.exp2(scores - top)
        total = total * fade + jnp.sum(weights, axis=0, keepdims=True)
        mixed = mixed * fade + inner_product(value_rows, weights.astype(jnp.bfloat16))
        return (top, total, mixed)

    start = (
        jnp.full((1, QUERY_BLOCK), -1e30, jnp.float32),
        jnp.zeros((1, QUERY_BLOCK), jnp.float32),
        jnp.zeros((HEAD_DIM, QUERY_BLOCK), jnp.float32),
    )
    highest, total, mixed = lax.fori_loop(first[step], last[step], one, start)
    out[...] = jnp.transpose(mixed / total)
    totals[...] = (highest + jnp.log2(total))[None]


def attend_back_kernel(
    first, last, query, keys, values, grad, mixed, totals, seg_row, codes, grad_query, key_out, value_out, grad_key, grad_value
):
    step = pl.program_id(1)

    @pl.when(step == 0)
    def _():
        grad_key[...] = jnp.zeros_like(grad_key)
        grad_value[...] = jnp.zeros_like(grad_value)

    rows = query[...]
    segs = seg_row[...]
    grads = grad[...]
    lse = totals[0]
    centre = jnp.sum(jnp.transpose(grads.astype(jnp.float32) * mixed[...]), axis=0, keepdims=True)

    def one(index, total):
        begin = pl.multiple_of(index * KEY_BLOCK, KEY_BLOCK)
        here = pl.ds(begin, KEY_BLOCK)
        key_rows = keys[here, :]
        scores = across_product(key_rows, rows) * (SCORE_SCALE * LOG2E)
        allowed = allowed_block(codes[here, :], segs, begin, MAXLEN + step * QUERY_BLOCK)
        probs = jnp.where(allowed, jnp.exp2(scores - lse), 0.0)
        grad_probs = across_product(values[here, :], grads)
        grad_scores = (probs * (grad_probs - centre) * SCORE_SCALE).astype(jnp.bfloat16)
        grad_value[here, :] += plain_product(probs.astype(jnp.bfloat16), grads)
        grad_key[here, :] += plain_product(grad_scores, rows)
        return total + inner_product(grad_scores, key_rows)

    grad_query[...] = lax.fori_loop(
        first[step], last[step], one, jnp.zeros((QUERY_BLOCK, HEAD_DIM), jnp.float32)
    ).astype(jnp.bfloat16)

    @pl.when(step == pl.num_programs(1) - 1)
    def _():
        key_out[...] = grad_key[...].astype(jnp.bfloat16)
        value_out[...] = grad_value[...].astype(jnp.bfloat16)


def attend(queries, both, context):
    first, last, seg_row, codes = context
    frames, local = queries.shape
    window = both.shape[0]
    grid = (local // HEAD_DIM, frames // QUERY_BLOCK)
    block = pl.BlockSpec((QUERY_BLOCK, HEAD_DIM), lambda h, i, *_: (i, h))
    whole = pl.BlockSpec((window, HEAD_DIM), lambda h, i, *_: (0, h))
    whole_values = pl.BlockSpec((window, HEAD_DIM), lambda h, i, *_: (0, grid[0] + h))
    seg_block = pl.BlockSpec((1, QUERY_BLOCK), lambda h, i, *_: (0, i))
    code_block = pl.BlockSpec((window, 128), lambda h, i, *_: (0, 0))
    row_block = pl.BlockSpec((1, 1, QUERY_BLOCK), lambda h, i, *_: (h, 0, i))
    return pl.pallas_call(
        attend_kernel,
        grid_spec=pltpu.PrefetchScalarGridSpec(
            num_scalar_prefetch=2,
            grid=grid,
            in_specs=[block, whole, whole_values, seg_block, code_block],
            out_specs=[block, row_block],
        ),
        out_shape=(
            jax.ShapeDtypeStruct((frames, local), jnp.float32),
            jax.ShapeDtypeStruct((grid[0], 1, frames), jnp.float32),
        ),
        cost_estimate=pl.CostEstimate(
            flops=4 * frames * MAXLEN * local, bytes_accessed=8 << 20, transcendentals=0
        ),
    )(first, last, queries, both, both, seg_row, codes)


def attend_back(queries, both, grads, mixed, totals, context):
    first, last, seg_row, codes = context
    frames, local = queries.shape
    window = both.shape[0]
    grid = (local // HEAD_DIM, frames // QUERY_BLOCK)
    block = pl.BlockSpec((QUERY_BLOCK, HEAD_DIM), lambda h, i, *_: (i, h))
    whole = pl.BlockSpec((window, HEAD_DIM), lambda h, i, *_: (0, h))
    whole_values = pl.BlockSpec((window, HEAD_DIM), lambda h, i, *_: (0, grid[0] + h))
    seg_block = pl.BlockSpec((1, QUERY_BLOCK), lambda h, i, *_: (0, i))
    code_block = pl.BlockSpec((window, 128), lambda h, i, *_: (0, 0))
    row_block = pl.BlockSpec((1, 1, QUERY_BLOCK), lambda h, i, *_: (h, 0, i))
    return pl.pallas_call(
        attend_back_kernel,
        grid_spec=pltpu.PrefetchScalarGridSpec(
            num_scalar_prefetch=2,
            grid=grid,
            in_specs=[block, whole, whole_values, block, block, row_block, seg_block, code_block],
            out_specs=[block, whole, whole],
            scratch_shapes=[pltpu.VMEM((window, HEAD_DIM), F32), pltpu.VMEM((window, HEAD_DIM), F32)],
        ),
        out_shape=(
            jax.ShapeDtypeStruct((frames, local), jnp.bfloat16),
            jax.ShapeDtypeStruct((window, local), jnp.bfloat16),
            jax.ShapeDtypeStruct((window, local), jnp.bfloat16),
        ),
        compiler_params=pltpu.CompilerParams(vmem_limit_bytes=48 << 20),
        cost_estimate=pl.CostEstimate(
            flops=10 * frames * MAXLEN * local, bytes_accessed=16 << 20, transcendentals=0
        ),
    )(first, last, queries, both, both, grads, mixed, totals, seg_row, codes)


def conv_context(segment_ids, pad_mask, frames):
    anchor = lax.axis_index("seq") * frames
    half = KERNEL // 2
    near = lax.dynamic_slice_in_dim(
        jnp.pad(segment_ids, (half, half), constant_values=-1), anchor, frames + 2 * half
    )
    own = lax.dynamic_slice_in_dim(segment_ids, anchor, frames)
    real = lax.dynamic_slice_in_dim(pad_mask, anchor, frames)
    columns = [near[tap : tap + frames] == own for tap in range(KERNEL)] + [real == 1]
    columns += [jnp.zeros_like(columns[0])] * (8 - len(columns))
    return jnp.stack(columns, axis=1).astype(F32)


def body(
    inputs,
    ln_gains,
    ffn1_in,
    ffn1_out,
    qkv_weight,
    attn_out,
    conv_in,
    conv_depth,
    bn_gain,
    bn_bias,
    conv_out,
    ffn2_in,
    ffn2_out,
    segment_ids,
    pad_mask,
    out_grad,
):
    frames = inputs.shape[0] * lax.axis_size("tp")
    attend_ctx = attention_context(segment_ids, pad_mask, frames)
    conv_ctx = conv_context(segment_ids, pad_mask, frames)
    gain_row, bias_row = bn_gain[None, :], bn_bias[None, :]
    shards = SimpleNamespace(
        ffn1_in=ffn1_in,
        ffn1_out=ffn1_out,
        project=qkv_weight.reshape(qkv_weight.shape[0], -1),
        attend=attn_out,
        pair=conv_in.reshape(conv_in.shape[0], -1),
        conv=conv_out,
        ffn2_in=ffn2_in,
        ffn2_out=ffn2_out,
    )
    opened = run_open(inputs, ln_gains, shards)
    mixed, totals = attend(opened.queries, opened.window, attend_ctx)
    middle = run_middle(mixed, opened, ln_gains, conv_ctx, conv_depth, gain_row, bias_row, shards, out_grad)
    grad_query, grad_key, grad_value = attend_back(
        opened.queries, opened.window, middle.grad_mixed, mixed, totals, attend_ctx
    )
    closed = run_close(inputs, ln_gains, opened, middle, grad_query, grad_key, grad_value)
    return (
        middle.output,
        closed.input_grad,
        closed.gain_total[:5],
        closed.sum_in,
        closed.sum_out,
        closed.sum_project.reshape(qkv_weight.shape),
        closed.sum_attend,
        closed.sum_pair.reshape(conv_in.shape),
        closed.depth_total[:KERNEL],
        middle.bn_sums[0],
        middle.bn_sums[1],
        closed.sum_conv,
        middle.sum_in,
        middle.sum_out,
    )


def solution(mesh):
    return jax.shard_map(
        body,
        mesh=mesh,
        in_specs=(
            P(("seq", "tp"), None),
            P(),
            P("seq", "tp"),
            P(("tp", "seq"), None),
            P("seq", None, "tp"),
            P(("tp", "seq"), None),
            P("seq", None, "tp"),
            P(None, "tp"),
            P("tp"),
            P("tp"),
            P(("tp", "seq"), None),
            P("seq", "tp"),
            P(("tp", "seq"), None),
            P(),
            P(),
            P(("seq", "tp"), None),
        ),
        out_specs=(
            P(("seq", "tp"), None),
            P(("seq", "tp"), None),
            P(),
            P("seq", "tp"),
            P(("tp", "seq"), None),
            P("seq", None, "tp"),
            P(("tp", "seq"), None),
            P("seq", None, "tp"),
            P(None, "tp"),
            P("tp"),
            P("tp"),
            P(("tp", "seq"), None),
            P("seq", "tp"),
            P(("tp", "seq"), None),
        ),
        check_vma=False,
    )
```

```python
import math
from types import SimpleNamespace

import jax
import jax.numpy as jnp
from jax import lax
from jax.experimental import pallas as pl
from jax.experimental.pallas import tpu as pltpu
from jax.sharding import PartitionSpec as P

SEQ, TP = "seq", "tp"
LOAD, KEEP = "load", "keep"
HEAD_DIM = 128
KERNEL = 5
MAXLEN = 1536
EPSILON = 1e-05
CHUNKS = 2
EDGE = 8
VMEM_LIMIT = 62 << 20
QUERY_BLOCK = 256
KEY_BLOCK = 512
SCORE_SCALE = 1.0 / math.sqrt(HEAD_DIM)
LOG2E = 1.4426950408889634
BF16 = jnp.bfloat16
F32 = jnp.float32
IN_VMEM = pl.BlockSpec(memory_space=pltpu.VMEM)
IN_PLACE = pl.BlockSpec(memory_space=pl.ANY)


def plain_product(left, right):
    return jnp.dot(left, right, preferred_element_type=F32)


def inner_product(left, right):
    return lax.dot_general(left, right, (((0,), (0,)), ((), ())), preferred_element_type=F32)


def across_product(left, right):
    return lax.dot_general(left, right, (((1,), (1,)), ((), ())), preferred_element_type=F32)


def swish(values):
    return values * jax.nn.sigmoid(values)


def standard_rows(values):
    centred = values - jnp.mean(values, axis=-1, keepdims=True)
    spread = jnp.mean(centred * centred, axis=-1, keepdims=True)
    inverse = lax.rsqrt(spread + EPSILON)
    return (centred * inverse, inverse)


def norm_rows(values, gain_row):
    return standard_rows(values)[0] * gain_row


def norm_back(values, gain_row, grads):
    normal, inverse = standard_rows(values)
    scaled = grads * gain_row
    result = inverse * (
        scaled
        - jnp.mean(scaled, axis=-1, keepdims=True)
        - normal * jnp.mean(scaled * normal, axis=-1, keepdims=True)
    )
    return (result, jnp.sum(grads * normal, axis=0, keepdims=True))


def flip(index, bit):
    return index + bit - 2 * bit * lax.rem(lax.div(index, bit), 2)


def span(begin, size):
    return pl.ds(pl.multiple_of(begin, size), size)


def static_span(begin, size):
    return pl.ds(begin, size)


def remote(source, target, send, receive, peer):
    return pltpu.make_async_remote_copy(
        src_ref=source,
        dst_ref=target,
        send_sem=send,
        recv_sem=receive,
        device_id=peer,
        device_id_type=pl.DeviceIdType.MESH,
    )


def tp_peers():
    me = lax.axis_index(TP)
    return [{TP: flip(me, 1)}, {TP: flip(me, 2)}]


def seq_peers():
    me, count = lax.axis_index(SEQ), lax.axis_size(SEQ)
    return [{SEQ: lax.rem(me + step, count)} for step in range(1, count)]


def greet(peers):
    barrier = pltpu.get_barrier_semaphore()
    for peer in peers:
        pl.semaphore_signal(barrier, inc=1, device_id=peer, device_id_type=pl.DeviceIdType.MESH)
    return lambda: pl.semaphore_wait(barrier, len(peers))


def owner(slot):
    me = lax.axis_index(TP)
    if slot & 1:
        me = flip(me, 1)
    if slot & 2:
        me = flip(me, 2)
    return me


def tiles(total, tile, body):
    def one(index, nothing):
        body(span(index * tile, tile))
        return nothing

    lax.fori_loop(0, total // tile, one, 0)


class Gather:
    def __init__(self, rows, send, receive):
        self.near, self.far = tp_peers()
        self.height = rows.shape[0] // 4
        self.piece = self.height // CHUNKS
        self.rows, self.send, self.receive = rows, send, receive

    def part(self, slot, chunk):
        return self.rows.at[pl.ds(slot * self.height + chunk * self.piece, self.piece), :]

    def hop(self, kind, chunk):
        source, target = ((0, 1), (0, 2), (2, 3))[kind]
        return remote(
            self.part(source, chunk),
            self.part(target, chunk),
            self.send.at[kind, chunk],
            self.receive.at[kind, chunk],
            self.far if kind == 1 else self.near,
        )

    def start(self, chunk):
        self.hop(1, chunk).start()
        self.hop(0, chunk).start()

    def wait_near(self):
        for chunk in range(CHUNKS):
            self.hop(0, chunk).wait_recv()

    def pass_on(self, chunk):
        self.hop(1, chunk).wait_recv()
        self.hop(2, chunk).start()

    def wait_last(self, chunk):
        self.hop(2, chunk).wait_recv()

    def finish(self):
        for chunk in range(CHUNKS):
            for kind in range(3):
                self.hop(kind, chunk).wait_send()


def gather_scratch():
    return dict(send=pltpu.SemaphoreType.DMA((3, CHUNKS)), receive=pltpu.SemaphoreType.DMA((3, CHUNKS)))


class Scatter:
    def __init__(self, own, passing, outgoing, incoming, send, receive):
        self.near, self.far = tp_peers()
        self.height = own.shape[0]
        self.piece = self.height // CHUNKS
        self.own, self.passing = own, passing
        self.outgoing, self.incoming, self.send, self.receive = outgoing, incoming, send, receive

    def rows(self, chunk):
        return pl.ds(chunk * self.piece, self.piece)

    def copy(self, kind, chunk):
        here = self.rows(chunk)
        return remote(
            self.outgoing.at[kind, here, :],
            self.incoming.at[kind, here, :],
            self.send.at[kind, chunk],
            self.receive.at[kind, chunk],
            self.far if kind == 2 else self.near,
        )

    def start(self, kind):
        for chunk in range(CHUNKS):
            self.copy(kind, chunk).start()

    def relay(self, chunk):
        here = self.rows(chunk)
        self.copy(1, chunk).wait_recv()
        self.outgoing[2, here, :] = (self.passing[here, :] + self.incoming[1, here, :].astype(F32)).astype(BF16)
        self.copy(2, chunk).start()

    def total(self, chunk):
        here = self.rows(chunk)
        self.copy(0, chunk).wait_recv()
        self.copy(2, chunk).wait_recv()
        return self.own[here, :] + self.incoming[0, here, :].astype(F32) + self.incoming[2, here, :].astype(F32)

    def spread(self, product, width, tile=512):
        height = self.height

        def far(cols):
            term = product((2, 3), cols)
            self.passing[:, cols] = term[:height]
            self.outgoing[1, :, cols] = term[height:].astype(BF16)

        tiles(width, tile, far)
        self.start(1)

        def near(cols):
            term = product((0, 1), cols)
            self.own[:, cols] = term[:height]
            self.outgoing[0, :, cols] = term[height:].astype(BF16)

        tiles(width, tile, near)
        for chunk in range(CHUNKS):
            self.relay(chunk)
        self.start(0)

    def finish(self):
        for kind in range(3):
            for chunk in range(CHUNKS):
                self.copy(kind, chunk).wait_send()


def scatter_scratch(height, width):
    return dict(
        own=pltpu.VMEM((height, width), F32),
        passing=pltpu.VMEM((height, width), F32),
        outgoing=pltpu.VMEM((3, height, width), BF16),
        incoming=pltpu.VMEM((3, height, width), BF16),
        send=pltpu.SemaphoreType.DMA((3, CHUNKS)),
        receive=pltpu.SemaphoreType.DMA((3, CHUNKS)),
    )


class Collect:
    def __init__(self, shard, full, send, receive, pair_send, pair_receive, local):
        self.me, self.count = lax.axis_index(SEQ), lax.axis_size(SEQ)
        self.groups = self.count // 2
        self.pair = {SEQ: flip(self.me, 1)}
        self.shard, self.full, self.height = shard, full, shard.shape[0]
        self.send, self.receive, self.pair_send, self.pair_receive = send, receive, pair_send, pair_receive
        self.local = pltpu.make_async_copy(shard, self.block(self.me), local.at[0])

    def block(self, index):
        return self.full.at[span(index * self.height, self.height), :]

    def out(self, step):
        peer = {SEQ: lax.rem(self.me + 2 * step, self.count)}
        return remote(self.shard, self.block(self.me), self.send.at[step - 1], self.receive.at[step - 1], peer)

    def over(self, step):
        if step == 0:
            source, place = self.shard, self.me
        else:
            place = lax.rem(self.me + self.count - 2 * step, self.count)
            source = self.block(place)
        return remote(source, self.block(place), self.pair_send.at[step], self.pair_receive.at[step], self.pair)

    def kick(self, step):
        if step == 0:
            self.over(0).start()
            self.local.start()
        else:
            self.out(step).start()

    def turn(self, step):
        if step:
            self.out(step).wait_recv()
            self.over(step).start()

    def end(self):
        self.local.wait()
        for step in range(self.groups):
            self.over(step).wait_recv()

    def finish(self):
        for step in range(self.groups):
            self.over(step).wait_send()
            if step:
                self.out(step).wait_send()


def collect_scratch():
    groups = lax.axis_size(SEQ) // 2
    return dict(
        send=pltpu.SemaphoreType.DMA((groups,)),
        receive=pltpu.SemaphoreType.DMA((groups,)),
        pair_send=pltpu.SemaphoreType.DMA((groups,)),
        pair_receive=pltpu.SemaphoreType.DMA((groups,)),
        local=pltpu.SemaphoreType.DMA((1,)),
    )


class Settle:
    def __init__(self, source, result, partner, others, send, receive, far_send, far_receive, half=None, load=None):
        self.me, self.count = lax.axis_index(SEQ), lax.axis_size(SEQ)
        self.groups = self.count // 2
        self.other = flip(self.me, 1)
        self.source, self.result, self.half, self.partner, self.others = source, result, half, partner, others
        self.height = result.shape[0]
        self.load, self.send, self.receive = load, send, receive
        self.far_send, self.far_receive = far_send, far_receive

    def block(self, base, step):
        place = lax.rem(base + 2 * step, self.count)
        return self.source.at[span(place * self.height, self.height), :]

    def mine(self, step):
        return self.block(self.me, step) if self.half is None else self.half.at[step]

    def swap(self, step):
        return remote(
            self.block(self.other, step),
            self.partner.at[step],
            self.send.at[step],
            self.receive.at[step],
            {SEQ: self.other},
        )

    def fetch(self, step):
        return pltpu.make_async_copy(self.block(self.me, step), self.half.at[step], self.load.at[step])

    def away(self, step):
        peer = {SEQ: lax.rem(self.me + 2 * step, self.count)}
        return remote(
            self.mine(step), self.others.at[step], self.far_send.at[step], self.far_receive.at[step], peer
        )

    def kick(self, step):
        self.swap(step).start()
        if self.half is not None:
            self.fetch(step).start()

    def turn(self, step):
        if step:
            if self.half is not None:
                self.fetch(step).wait()
            self.swap(step).wait_recv()
            mine = self.mine(step)
            mine[...] = (mine[...].astype(F32) + self.partner[step].astype(F32)).astype(BF16)
            self.away(step).start()

    def end(self):
        if self.half is not None:
            self.fetch(0).wait()
        self.swap(0).wait_recv()
        total = self.mine(0)[...].astype(F32) + self.partner[0].astype(F32)
        for step in range(1, self.groups):
            self.away(step).wait_recv()
            total = total + self.others[step].astype(F32)
        self.result[...] = total

    def finish(self):
        for step in range(self.groups):
            self.swap(step).wait_send()
            if step:
                self.away(step).wait_send()


def settle_scratch(height, width, apart=False):
    groups = lax.axis_size(SEQ) // 2
    more = dict(half=pltpu.VMEM((groups, height, width), BF16), load=pltpu.SemaphoreType.DMA((groups,)))
    return dict(
        **(more if apart else {}),
        partner=pltpu.VMEM((groups, height, width), BF16),
        others=pltpu.VMEM((groups, height, width), BF16),
        send=pltpu.SemaphoreType.DMA((groups,)),
        receive=pltpu.SemaphoreType.DMA((groups,)),
        far_send=pltpu.SemaphoreType.DMA((groups,)),
        far_receive=pltpu.SemaphoreType.DMA((groups,)),
    )


class Plan:
    def __init__(self, points, tasks):
        self.points, self.tasks = points, tasks
        self.left = set()
        for place in range(1, len(tasks) + 1):
            self.left |= {10 * place + step for step in range(4)} | {-10 * place - step for step in range(1, 4)}

    def at(self, point):
        for number in self.points.get(point, ()):
            self.left.remove(number)
            place, digit = divmod(abs(number), 10)
            task = self.tasks[place - 1]
            for step in range(digit, task.groups if digit == 3 else min(digit + 1, task.groups)):
                (task.kick if number > 0 else task.turn)(step)

    def finish(self):
        assert not self.left, "steps left"
        for task in self.tasks:
            task.finish()


class Swap:
    def __init__(self, blocks, send, receive):
        self.me, self.count = lax.axis_index(SEQ), lax.axis_size(SEQ)
        self.blocks, self.send, self.receive = blocks, send, receive

    def copy(self, step):
        peer = {SEQ: lax.rem(self.me + step, self.count)}
        return remote(self.blocks.at[0], self.blocks.at[step], self.send.at[step], self.receive.at[step], peer)

    def start(self):
        for step in range(1, self.count):
            self.copy(step).start()

    def wait(self):
        for step in range(1, self.count):
            self.copy(step).wait_recv()

    def finish(self):
        for step in range(1, self.count):
            self.copy(step).wait_send()


def swap_scratch(height, width):
    count = lax.axis_size(SEQ)
    return dict(
        blocks=pltpu.VMEM((count, height, width), F32),
        send=pltpu.SemaphoreType.DMA((count,)),
        receive=pltpu.SemaphoreType.DMA((count,)),
    )


class Edges:
    def __init__(self, padded, send, receive):
        self.me, self.count = lax.axis_index(SEQ), lax.axis_size(SEQ)
        self.padded, self.send, self.receive = padded, send, receive
        self.frames = padded.shape[0] - 2 * EDGE

    def up(self):
        source = self.padded.at[pl.ds(self.frames, EDGE), :]
        target = self.padded.at[pl.ds(0, EDGE), :]
        peer = {SEQ: lax.rem(self.me + 1, self.count)}
        return remote(source, target, self.send.at[0], self.receive.at[0], peer)

    def down(self):
        source = self.padded.at[pl.ds(EDGE, EDGE), :]
        target = self.padded.at[pl.ds(EDGE + self.frames, EDGE), :]
        peer = {SEQ: lax.rem(self.me + self.count - 1, self.count)}
        return remote(source, target, self.send.at[1], self.receive.at[1], peer)

    def start(self):
        self.up().start()
        self.down().start()

    def wait(self):
        self.up().wait_recv()
        self.down().wait_recv()

    def finish(self):
        self.up().wait_send()
        self.down().wait_send()


def edges_scratch():
    return dict(send=pltpu.SemaphoreType.DMA((2,)), receive=pltpu.SemaphoreType.DMA((2,)))


def run_kernel(body, number, inputs, outputs, scratch, flops=1 << 33):
    loads = [name for name, (_, place) in inputs.items() if place == LOAD]
    keeps = [name for name, (_, _, place) in outputs.items() if place == KEEP]
    moved = {name: pltpu.VMEM(inputs[name][0].shape, inputs[name][0].dtype) for name in loads}
    moved.update({name: pltpu.VMEM(outputs[name][0], outputs[name][1]) for name in keeps})
    flat, groups = list(moved.values()) + [pltpu.SemaphoreType.DMA((max(1, len(moved)),))], []
    for name, item in scratch.items():
        parts = item if isinstance(item, dict) else {None: item}
        groups.append((name, list(parts)))
        flat.extend(parts.values())

    def kernel(*refs):
        given = dict(zip(list(inputs) + list(outputs), refs))
        rest = list(refs[len(given) :])
        near = {name: rest.pop(0) for name in moved}
        sems = rest.pop(0)
        copies = {}
        for place, name in enumerate(moved):
            ends = (given[name], near[name]) if name in loads else (near[name], given[name])
            copies[name] = pltpu.make_async_copy(*ends, sems.at[place])
        given.update(near)
        for name, keys in groups:
            taken = {key: rest.pop(0) for key in keys}
            given[name] = taken[None] if None in taken else taken
        for name in loads:
            copies[name].start()
        waiting, going = list(loads), []

        def wait(*names):
            for name in names:
                waiting.remove(name)
                copies[name].wait()

        def put(*names):
            for name in names:
                going.append(name)
                copies[name].start()

        body(SimpleNamespace(**given, wait=wait, put=put))
        assert not waiting and sorted(going) == sorted(keeps), "copies left"
        for name in going:
            copies[name].wait()

    results = pl.pallas_call(
        kernel,
        out_shape=tuple(jax.ShapeDtypeStruct(shape, kind) for shape, kind, _ in outputs.values()),
        in_specs=[IN_VMEM if place is True else IN_PLACE for _, place in inputs.values()],
        out_specs=tuple(IN_VMEM if place is True else IN_PLACE for _, _, place in outputs.values()),
        scratch_shapes=flat,
        compiler_params=pltpu.CompilerParams(
            collective_id=number, has_side_effects=True, vmem_limit_bytes=VMEM_LIMIT
        ),
        cost_estimate=pl.CostEstimate(flops=flops, bytes_accessed=16 << 20, transcendentals=0),
    )(*[array for array, _ in inputs.values()])
    return SimpleNamespace(**dict(zip(outputs, results)))


def ffn_forward(gather, scatter, win, wout, hidden, active, wait_in, wait_out, late=False, at=lambda point: None):
    rows, height, piece = gather.rows, gather.height, gather.piece
    width, inner = win.shape
    pair = pl.ds(0, 2 * height)
    gather.wait_near()
    wait_in()

    def first(cols):
        product = plain_product(rows[pair, :], win[:, cols])
        hidden[pair, cols] = product
        active[pair, cols] = swish(product).astype(BF16)

    def second(cols):
        product = plain_product(active[pair, :], wout[:, cols])
        scatter.own[:, cols] = product[:height]
        scatter.outgoing[0, :, cols] = product[height:].astype(BF16)

    def far_rows(chunk):
        return (
            pl.ds(2 * height + chunk * piece, piece),
            pl.ds(3 * height + chunk * piece, piece),
            scatter.rows(chunk),
        )

    def inward(chunk):
        low, high, here = far_rows(chunk)

        def third(cols):
            both = jnp.concatenate([rows[low, :], rows[high, :]], axis=0)
            product = plain_product(both, win[:, cols])
            hidden[low, cols] = product[:piece]
            hidden[high, cols] = product[piece:]
            alive = swish(product).astype(BF16)
            active[low, cols] = alive[:piece]
            active[high, cols] = alive[piece:]

        gather.wait_last(chunk)
        tiles(inner, 512, third)

    def outward(chunk):
        low, high, here = far_rows(chunk)

        def fourth(cols):
            both = jnp.concatenate([active[low, :], active[high, :]], axis=0)
            product = plain_product(both, wout[:, cols])
            scatter.passing[here, cols] = product[:piece]
            scatter.outgoing[1, here, cols] = product[piece:].astype(BF16)

        tiles(width, 512, fourth)
        scatter.copy(1, chunk).start()
        scatter.relay(chunk)

    tiles(inner, 512, first)
    at("first")
    gather.pass_on(0)
    if late:
        for chunk in range(CHUNKS):
            if chunk > 0:
                gather.pass_on(chunk)
            inward(chunk)
            at(f"inward{chunk}")
        wait_out()
        for chunk in range(CHUNKS):
            outward(chunk)
            at(f"outward{chunk}")
    else:
        wait_out()
        tiles(width, 512, second)
        scatter.start(0)
        for chunk in range(CHUNKS):
            if chunk > 0:
                gather.pass_on(chunk)
            inward(chunk)
            outward(chunk)
    if late:
        tiles(width, 512, second)
        scatter.start(0)


def ffn_backward(gather, scatter, win, wout, hidden, active, slope, wait_out, wait_in, products=None, at=lambda point: None):
    rows, height, piece = gather.rows, gather.height, gather.piece
    width, inner = win.shape
    pair = pl.ds(0, 2 * height)
    gather.wait_near()
    wait_out()

    def bend(product, before):
        logistic = jax.nn.sigmoid(before)
        return (
            (before * logistic).astype(BF16),
            (product * (logistic * (1.0 + before * (1.0 - logistic)))).astype(BF16),
        )

    def first(cols):
        alive, steep = bend(across_product(rows[pair, :], wout[cols, :]), hidden[pair, cols])
        if active is not None:
            active[pair, cols] = alive
        slope[pair, cols] = steep

    def second(cols):
        product = across_product(slope[pair, :], win[cols, :])
        scatter.own[:, cols] = product[:height]
        scatter.outgoing[0, :, cols] = product[height:].astype(BF16)

    def far_rows(chunk):
        return (
            pl.ds(2 * height + chunk * piece, piece),
            pl.ds(3 * height + chunk * piece, piece),
            scatter.rows(chunk),
        )

    def inward(chunk):
        low, high, here = far_rows(chunk)

        def third(cols):
            both = jnp.concatenate([rows[low, :], rows[high, :]], axis=0)
            before = jnp.concatenate([hidden[low, cols], hidden[high, cols]], axis=0)
            alive, steep = bend(across_product(both, wout[cols, :]), before)
            if active is not None:
                active[low, cols] = alive[:piece]
                active[high, cols] = alive[piece:]
            slope[low, cols] = steep[:piece]
            slope[high, cols] = steep[piece:]

        gather.wait_last(chunk)
        tiles(inner, 256, third)

    def outward(chunk):
        low, high, here = far_rows(chunk)

        def fourth(cols):
            both = jnp.concatenate([slope[low, :], slope[high, :]], axis=0)
            product = across_product(both, win[cols, :])
            scatter.passing[here, cols] = product[:piece]
            scatter.outgoing[1, here, cols] = product[piece:].astype(BF16)

        tiles(width, 512, fourth)
        scatter.copy(1, chunk).start()
        scatter.relay(chunk)

    tiles(inner, 256, first)
    at("first")
    gather.pass_on(0)
    if products is not None:
        for chunk in range(CHUNKS):
            if chunk > 0:
                gather.pass_on(chunk)
            inward(chunk)
        products()
        wait_in()
        for chunk in range(CHUNKS):
            outward(chunk)
            at(f"outward{chunk}")
        tiles(width, 512, second)
        scatter.start(0)
        at("second")
    else:
        wait_in()
        tiles(width, 512, second)
        scatter.start(0)
        for chunk in range(CHUNKS):
            if chunk > 0:
                gather.pass_on(chunk)
            inward(chunk)
            outward(chunk)


def weight_products(result, left, right, tile=256):
    def one(cols):
        result[:, cols] = inner_product(left[...], right[:, cols]).astype(BF16)

    tiles(right.shape[1], tile, one)


OPEN_PLAN = dict(
    start=(11, 13, 12, 10, 21, 23, 22, 20,),
    gather=(-11, -13, -12, -21,),
    out=(-23, -22, 31, 32, 33, 30,),
    outward1=(-31, -32,),
    total0=(-33, 41, 42, 43, 40,),
    near=(-41, -42, -43,),
)


def describe_frames(n, frames):
    seq = lax.axis_index(SEQ)
    lines, reach, total = frames // 128, MAXLEN // 128, n.segs.shape[0]
    base = seq * lines

    def line_of(ids, line, outside):
        safe = lax.min(lax.max(line, 0), total - 1)
        row = ids[pl.ds(safe, 1), :]
        return jnp.where((line >= 0) & (line < total), row, outside)

    def code(index, nothing):
        line = base - reach + index
        row = jnp.where(line_of(n.pads, line, 0) == 1, line_of(n.segs, line, -2), -1)
        n.codes[span(index * 128, 128), :] = jnp.transpose(jnp.broadcast_to(row, (128, 128)))
        return nothing

    lax.fori_loop(0, lines + 2 * reach, code, 0)
    lane = lax.broadcasted_iota(jnp.int32, (8, 128), 1)
    row_at = lax.broadcasted_iota(jnp.int32, (8, 128), 0)

    def marks(index, nothing):
        before, own, after = [
            jnp.broadcast_to(line_of(n.segs, base + index + shift, -1), (8, 128)) for shift in (-1, 0, 1)
        ]
        real = jnp.broadcast_to(n.pads[pl.ds(base + index, 1), :], (8, 128))
        table = jnp.where((row_at == KERNEL) & (real == 1), 1.0, 0.0)
        for tap in range(KERNEL):
            shift = tap - KERNEL // 2
            if shift < 0:
                moved = jnp.where(lane < -shift, pltpu.roll(before, -shift, 1), pltpu.roll(own, -shift, 1))
            elif shift > 0:
                moved = jnp.where(
                    lane >= 128 - shift, pltpu.roll(after, 128 - shift, 1), pltpu.roll(own, 128 - shift, 1)
                )
            else:
                moved = own
            table = jnp.where((row_at == tap) & (moved == own), 1.0, table)
        table = jnp.concatenate([table, jnp.zeros((120, 128), F32)], axis=0)
        n.context[span(index * 128, 128), :] = jnp.transpose(table)
        return nothing

    lax.fori_loop(0, lines, marks, 0)
    everyone = n.segs[...]
    offset = (MAXLEN - seq * frames).astype(F32)
    edge = lax.broadcasted_iota(jnp.int32, (1, 128), 1)
    per = QUERY_BLOCK // 128
    for step in range(frames // QUERY_BLOCK):
        low = n.segs[pl.ds(base + step * per, 1), :][:, 0:1]
        high = n.segs[pl.ds(base + step * per + per - 1, 1), :][:, 127:128]
        below = jnp.sum(jnp.where(everyone < low, 1.0, 0.0), keepdims=True)
        upto = jnp.sum(jnp.where(everyone <= high, 1.0, 0.0), keepdims=True)
        first = jnp.floor((below + offset) * (1.0 / KEY_BLOCK))
        last = jnp.floor((upto + (offset + (KEY_BLOCK - 1))) * (1.0 / KEY_BLOCK))
        n.bounds[step : step + 1, :] = jnp.where(edge == 0, first, last).astype(jnp.int32)


def open_kernel(n):
    height, width = n.values.shape
    frames = 4 * height
    local = n.queries.shape[1]
    seq, count = lax.axis_index(SEQ), lax.axis_size(SEQ)
    first_in = Collect(n.shard_in, n.win, **n.c_in)
    first_out = Collect(n.shard_out, n.wout, **n.c_out)
    project = Collect(n.shard_project, n.wproject, **n.c_project)
    attend_out = Collect(n.shard_attend, n.full_attend, **n.c_attend)
    plan = Plan(OPEN_PLAN, (first_in, first_out, project, attend_out))
    gather = Gather(n.rows, **n.g1)
    scatter = Scatter(**n.s1)
    gather_two = Gather(n.rows_two, **n.g2)
    ready = greet(tp_peers() + seq_peers())
    n.rows[pl.ds(0, gather.piece), :] = norm_rows(
        n.values[pl.ds(0, gather.piece), :].astype(F32), n.gains[0:1, :]
    ).astype(BF16)
    for part in range(3):
        n.shard_project[:, pl.ds(part * local, local)] = n.project_parts[part]
    ready()
    plan.at("start")
    for chunk in range(CHUNKS):
        here = scatter.rows(chunk)
        if chunk > 0:
            n.rows[here, :] = norm_rows(n.values[here, :].astype(F32), n.gains[0:1, :]).astype(BF16)
        gather.start(chunk)
    describe_frames(n, frames)
    n.put("codes", "context")
    plan.at("gather")
    keeps = [
        pltpu.make_async_copy(n.win, n.full_in, n.keep.at[0]),
        pltpu.make_async_copy(n.wout, n.full_out, n.keep.at[1]),
        pltpu.make_async_copy(n.wproject, n.full_project, n.keep.at[2]),
    ]

    def wait_in():
        first_in.end()
        keeps[0].start()

    def wait_out():
        plan.at("out")
        first_out.end()
        keeps[1].start()

    ffn_forward(gather, scatter, n.win, n.wout, n.hidden, n.active, wait_in, wait_out, late=True, at=plan.at)
    for chunk in range(CHUNKS):
        here = scatter.rows(chunk)
        n.first[here, :] = n.values[here, :].astype(F32) + 0.5 * scatter.total(chunk)
        n.rows_two[here, :] = norm_rows(n.first[here, :], n.gains[1:2, :]).astype(BF16)
        gather_two.start(chunk)
        plan.at(f"total{chunk}")
    n.put("rows", "hidden", "first")
    project.end()
    keeps[2].start()
    gather_two.wait_near()

    def send_block(slot):
        place = owner(slot)
        source = n.pair_own.at[span(place * height, height), :]
        upper = lax.div(place, 2)

        def piece(kind):
            if kind == 0:
                peer, row = lax.rem(seq + 1, count), MAXLEN - frames + place * height
            elif kind == 1:
                peer, row = lax.rem(seq + count - 1, count), MAXLEN + frames + place * height
            else:
                peer = lax.rem(seq + count - 2 + 4 * upper, count)
                row = MAXLEN + place * height + 2 * frames * (1 - 2 * upper)
            target = n.window.at[span(row, height), :]
            return remote(source, target, n.halo_send.at[kind, slot], n.halo_receive.at[kind, slot], {SEQ: peer})

        return [piece(kind) for kind in range(3)]

    def there(kind, slot, sending):
        upper = lax.div(owner(slot), 2)
        if kind == 2:
            shift = 4 * upper - 2
        else:
            shift = 1 - 2 * kind
        target = seq + shift if sending else seq - shift
        return (target >= 0) & (target < count)

    def project_rows(slots, low):
        for part in range(3):
            cols = pl.ds(part * local, local)
            product = plain_product(n.rows_two[low, :], n.wproject[:, cols]).astype(BF16)
            for index, slot in enumerate(slots):
                rows = product[index * height : (index + 1) * height]
                place = span(owner(slot) * height, height)
                if part == 0:
                    n.queries[place, :] = rows
                else:
                    n.pair_own[place, pl.ds((part - 1) * local, local)] = rows
        for slot in slots:
            for kind, copy in enumerate(send_block(slot)):

                @pl.when(there(kind, slot, True))
                def _():
                    copy.start()

    project_rows((0, 1), pl.ds(0, 2 * height))
    for chunk in range(CHUNKS):
        gather_two.pass_on(chunk)
    plan.at("near")
    for chunk in range(CHUNKS):
        gather_two.wait_last(chunk)
    n.put("rows_two")
    project_rows((2, 3), pl.ds(2 * height, 2 * height))
    own = pltpu.make_async_copy(n.pair_own, n.window.at[pl.ds(MAXLEN, frames), :], n.keep.at[3])
    own.start()
    n.put("queries")
    for slot in range(4):
        for kind, copy in enumerate(send_block(slot)):

            @pl.when(there(kind, slot, False))
            def _():
                copy.wait_recv()

            @pl.when(there(kind, slot, True))
            def _():
                copy.wait_send()

    attend_out.end()
    for keep in keeps:
        keep.wait()
    own.wait()
    plan.finish()
    for item in [gather, scatter, gather_two]:
        item.finish()


def run_open(values, gains, shards, segs, pads):
    height, width = values.shape
    frames = 4 * height
    count = lax.axis_size(SEQ)
    inner, local = shards.ffn1_in.shape[1], shards.attend.shape[0] * count
    fulls = dict(
        full_in=shards.ffn1_in, full_out=shards.ffn1_out,
        full_attend=shards.attend,
    )
    return run_kernel(
        open_kernel,
        0,
        dict(
            values=(values, True), gains=(gains, True), shard_in=(shards.ffn1_in, True),
            shard_out=(shards.ffn1_out, True), project_parts=(shards.project, True),
            segs=(segs, True), pads=(pads, True),
            shard_attend=(shards.attend, True),
        ),
        dict(
            first=((height, width), F32, KEEP),
            rows=((frames, width), BF16, KEEP),
            hidden=((frames, inner), F32, KEEP),
            rows_two=((frames, width), BF16, KEEP),
            queries=((frames, local), BF16, KEEP),
            window=((frames + 2 * MAXLEN, 2 * local), BF16, False),
            codes=((frames + 2 * MAXLEN, 128), jnp.int32, KEEP),
            context=((frames, 128), F32, KEEP),
            bounds=((8, 128), jnp.int32, True),
            full_project=((width, 3 * local), BF16, False),
            **{name: ((item.shape[0] * count, item.shape[1]), BF16, False) for name, item in fulls.items()},
        ),
        dict(
            win=pltpu.VMEM((width, inner), BF16),
            wout=pltpu.VMEM((inner, width), BF16),
            wproject=pltpu.VMEM((width, 3 * local), BF16),
            shard_project=pltpu.VMEM((width // count, 3 * local), BF16),
            active=pltpu.VMEM((frames, inner), BF16),
            pair_own=pltpu.VMEM((frames, 2 * local), BF16),
            c_in=collect_scratch(), c_out=collect_scratch(), c_project=collect_scratch(),
            c_attend=collect_scratch(),
            g1=gather_scratch(), s1=scatter_scratch(height, width), g2=gather_scratch(),
            halo_send=pltpu.SemaphoreType.DMA((3, 4)), halo_receive=pltpu.SemaphoreType.DMA((3, 4)),
            keep=pltpu.SemaphoreType.DMA((4,)),
        ),
    )


def slot_rows(slots, height):
    return pl.ds(slots[0] * height, 2 * height)


def in_order(swap):
    for place in range(swap.count):
        yield swap.blocks[lax.rem(swap.me + swap.count - place, swap.count)]


def middle_kernel(n):
    height, width = n.first.shape
    frames = 4 * height
    local = n.mixed.shape[1]
    block = 128
    none = jnp.zeros((1, local), F32)
    pair_weight, conv_weight = Collect(n.shard_pair, n.wpair, **n.c_pair), Collect(n.shard_conv, n.wconv, **n.c_conv)
    in_weight, out_weight = Collect(n.shard_in, n.win, **n.c_in), Collect(n.shard_out, n.wout, **n.c_out)
    out_sum, in_sum = Settle(n.grad_out, n.sum_out, **n.t_out), Settle(n.grad_in, n.sum_in, **n.t_in)
    plan = Plan(
        MIDDLE_PLAN,
        (pair_weight, conv_weight, in_weight, out_weight, out_sum, in_sum),
    )
    scatter = Scatter(**n.s1)
    gathers = [
        Gather(n.rows_conv, **n.g1), Gather(n.rows, **n.g2), Gather(n.grads, **n.g3),
        Gather(n.grads_conv, **n.g4), Gather(n.grads, **n.g5),
    ]
    edges, edges_back = Edges(n.gated, **n.edge), Edges(n.back, **n.edge_back)
    swap, swap_back = Swap(**n.swap), Swap(**n.swap_back)
    chunks = [scatter.rows(chunk) for chunk in range(CHUNKS)]
    ready = greet(tp_peers() + seq_peers())
    for slot in range(4):
        n.mixed_low[pl.ds(slot * height, height), :] = n.mixed[span(owner(slot) * height, height), :].astype(BF16)
    for part in range(2):
        n.shard_pair[:, pl.ds(part * local, local)] = n.pair_parts[:, part, :]
    ready()
    plan.at("start")
    scatter.spread(
        lambda slots, cols: plain_product(n.mixed_low[slot_rows(slots, height), :], n.wattend[:, cols]), width
    )
    gather = gathers[0]
    plan.at("spread")
    n.wait("first")
    for chunk, here in enumerate(chunks):
        n.second[here, :] = n.first[here, :] + scatter.total(chunk)
        n.rows_conv[here, :] = norm_rows(n.second[here, :], n.gains[2:3, :]).astype(BF16)
        gather.start(chunk)
        plan.at(f"second{chunk}")
    scatter.finish()
    gather.wait_near()
    pair_weight.end()
    n.wait("context")

    def pair_rows(slots):
        product = plain_product(n.rows_conv[slot_rows(slots, height), :], n.wpair[...])
        for index, slot in enumerate(slots):
            rows = product[index * height : (index + 1) * height]
            place = owner(slot) * height
            n.paired[span(place, height), :] = rows
            real = n.context[span(place, height), KERNEL : KERNEL + 1]
            gated = rows[:, :local] * jax.nn.sigmoid(rows[:, local:]) * real
            n.gated[pl.ds(pl.multiple_of(EDGE + place, EDGE), height), :] = gated.astype(BF16).astype(F32)

    pair_rows((0, 1))
    for chunk in range(CHUNKS):
        gather.pass_on(chunk)
    plan.at("passed")
    for chunk in range(CHUNKS):
        gather.wait_last(chunk)
    pair_rows((2, 3))
    edges.start()
    plan.at("edged")

    def convolve(index, carried):
        total, real_count = carried
        around = n.gated[pl.ds(pl.multiple_of(index * block, block), block + 2 * EDGE), :]
        marks = n.context[span(index * block, block), :]
        conv = jnp.zeros((block, local), F32)
        for tap in range(KERNEL):
            begin = EDGE - KERNEL // 2 + tap
            conv = conv + n.depth[tap : tap + 1, :] * around[begin : begin + block] * marks[:, tap : tap + 1]
        n.normal[span(index * block, block), :] = conv
        real = marks[:, KERNEL : KERNEL + 1]
        return (
            total + jnp.sum(real * conv, axis=0, keepdims=True),
            real_count + jnp.sum(jnp.broadcast_to(real, conv.shape), axis=0, keepdims=True),
        )

    last = frames // block - 1
    carried = lax.fori_loop(1, last, convolve, (none, none))
    edges.wait()
    plan.at("edges")
    total, real_count = convolve(last, convolve(0, carried))
    middle = total / jnp.maximum(real_count, 1.0)

    def deviate(index, carried):
        conv = n.normal[span(index * block, block), :]
        real = n.context[span(index * block, block), KERNEL : KERNEL + 1]
        away = conv - middle
        return carried + jnp.sum(real * away * away, axis=0, keepdims=True)

    squares = lax.fori_loop(0, frames // block, deviate, none)
    swap.blocks[0, 0:1, :] = total
    swap.blocks[0, 1:2, :] = squares
    swap.blocks[0, 2:3, :] = real_count
    swap.start()
    swap.wait()
    plan.at("swapped")
    total_all, real_all = none, none
    for item in in_order(swap):
        total_all = total_all + item[0:1]
        real_all = real_all + item[2:3]
    centre = total_all / real_all
    squares_all = none
    for item in in_order(swap):
        away = item[0:1] / jnp.maximum(item[2:3], 1.0) - centre
        squares_all = squares_all + item[1:2] + item[2:3] * away * away
    inverse = lax.rsqrt(squares_all / real_all + EPSILON)
    for slot in range(4):
        place = span(owner(slot) * height, height)
        normal = (n.normal[place, :] - centre) * inverse
        n.normal[place, :] = normal
        n.alive[pl.ds(slot * height, height), :] = swish(normal * n.bn_gain[...] + n.bn_bias[...]).astype(BF16)
    conv_weight.end()
    scatter.spread(
        lambda slots, cols: plain_product(n.alive[slot_rows(slots, height), :], n.wconv[:, cols]), width
    )
    plan.at("alive")
    gather = gathers[1]
    for chunk, here in enumerate(chunks):
        n.third[here, :] = n.second[here, :] + scatter.total(chunk)
        n.rows[here, :] = norm_rows(n.third[here, :], n.gains[3:4, :]).astype(BF16)
        gather.start(chunk)
        plan.at(f"third{chunk}")
    scatter.finish()
    ffn_forward(gather, scatter, n.win, n.wout, n.hidden, n.active, in_weight.end, out_weight.end, True, plan.at)
    gather = gathers[2]
    n.wait("out_grad")
    gain_four = jnp.zeros((1, width), F32)
    for chunk, here in enumerate(chunks):
        fourth = n.third[here, :] + 0.5 * scatter.total(chunk)
        n.output[here, :] = norm_rows(fourth, n.gains[4:5, :]).astype(BF16)
        grad, gain = norm_back(fourth, n.gains[4:5, :], n.out_grad[here, :].astype(F32))
        gain_four = gain_four + gain
        n.grad_row[here, :] = grad
        n.grads[here, :] = (0.5 * grad).astype(BF16)
        gather.start(chunk)
    scatter.finish()
    n.put("output")

    def nothing():
        return None

    ffn_backward(gather, scatter, n.win, n.wout, n.hidden, None, n.slope, nothing, nothing)
    weight_products(n.grad_out, n.active, n.grads)
    plan.at("grad_out")
    weight_products(n.grad_in, n.rows, n.slope)
    plan.at("grad_in")
    gathers[2].finish()
    gather = gathers[3]
    gain_three = jnp.zeros((1, width), F32)
    for chunk, here in enumerate(chunks):
        grad, gain = norm_back(n.third[here, :], n.gains[3:4, :], scatter.total(chunk))
        gain_three = gain_three + gain
        n.grad_row[here, :] += grad
        n.grads_conv[here, :] = n.grad_row[here, :].astype(BF16)
        gather.start(chunk)
    scatter.finish()
    plan.at("back_start")
    gather.wait_near()
    sums = [none, none]

    def batch_rows(slots):
        product = across_product(n.grads_conv[slot_rows(slots, height), :], n.wconv[...])
        for index, slot in enumerate(slots):
            place = span(owner(slot) * height, height)
            normal = n.normal[place, :]
            batch = normal * n.bn_gain[...] + n.bn_bias[...]
            logistic = jax.nn.sigmoid(batch)
            rows = product[index * height : (index + 1) * height]
            grad = rows * (logistic * (1.0 + batch * (1.0 - logistic)))
            n.grad_batch[place, :] = grad
            sums[0] = sums[0] + jnp.sum(grad * normal, axis=0, keepdims=True)
            sums[1] = sums[1] + jnp.sum(grad, axis=0, keepdims=True)

    batch_rows((0, 1))
    plan.at("back_near")
    for chunk in range(CHUNKS):
        gather.pass_on(chunk)
    plan.at("back_passed")
    for chunk in range(CHUNKS):
        gather.wait_last(chunk)
    batch_rows((2, 3))
    swap_back.blocks[0, 0:1, :] = sums[0]
    swap_back.blocks[0, 1:2, :] = sums[1]
    swap_back.start()
    weight_products(n.grad_conv, n.alive, n.grads_conv, 512)
    n.put("grad_conv")
    plan.at("grad_conv")
    swap_back.wait()
    grad_gain, grad_bias = none, none
    for item in in_order(swap_back):
        grad_gain = grad_gain + item[0:1]
        grad_bias = grad_bias + item[1:2]
    n.sum_gain[...] = grad_gain
    n.sum_bias[...] = grad_bias
    gain = n.bn_gain[...]

    def deconvolve(index, nothing):
        here = span(index * block, block)
        real = n.context[here, KERNEL : KERNEL + 1]
        drift = real * (gain * grad_bias + n.normal[here, :] * gain * grad_gain) / real_all
        n.back[pl.ds(pl.multiple_of(EDGE + index * block, EDGE), block), :] = inverse * (
            n.grad_batch[here, :] * gain - drift
        )
        return nothing

    lax.fori_loop(0, frames // block, deconvolve, 0)
    edges_back.start()
    plan.at("edges_back")
    me = lax.axis_index(TP)

    def part(index, carried):
        here = span(index * block, block)
        around = pl.ds(pl.multiple_of(index * block, block), block + 2 * EDGE)
        back, gated = n.back[around, :], n.gated[around, :]
        marks = n.context[here, :]
        own = back[EDGE : EDGE + block]
        grad = jnp.zeros((block, local), F32)
        result = []
        for tap in range(KERNEL):
            first = EDGE - KERNEL // 2 + tap
            mark = marks[:, tap : tap + 1]
            result.append(
                carried[tap] + jnp.sum(gated[first : first + block] * mark * own, axis=0, keepdims=True)
            )
            mirror = KERNEL - 1 - tap
            grad = grad + n.depth[mirror : mirror + 1, :] * back[first : first + block] * mark
        grad = grad * marks[:, KERNEL : KERNEL + 1]
        both = n.paired[here, :]
        logistic = jax.nn.sigmoid(both[:, local:])
        place = lax.div(index * block, height)
        slot = lax.rem(place + me, 2) + 2 * lax.rem(lax.div(place, 2) + lax.div(me, 2), 2)
        rows = span(slot * height + lax.rem(index * block, height), block)
        n.grad_paired[rows, pl.ds(0, local)] = (grad * logistic).astype(BF16)
        n.grad_paired[rows, pl.ds(local, local)] = (
            grad * both[:, :local] * logistic * (1.0 - logistic)
        ).astype(BF16)
        return tuple(result)

    taps = lax.fori_loop(1, last, part, (none,) * KERNEL)
    edges_back.wait()
    plan.at("parts")
    taps = part(last, part(0, taps))
    for tap in range(KERNEL):
        n.depth_sums[tap : tap + 1, :] = taps[tap]
    plan.at("taps")
    scatter.spread(
        lambda slots, cols: across_product(n.grad_paired[slot_rows(slots, height), :], n.wpair[cols, :]), width
    )
    plan.at("back_spread")
    weight_products(n.grad_pair, n.rows_conv, n.grad_paired)
    n.put("grad_pair")
    plan.at("grad_pair")
    gather = gathers[4]
    gain_two = jnp.zeros((1, width), F32)
    for chunk, here in enumerate(chunks):
        grad, gain = norm_back(n.second[here, :], n.gains[2:3, :], scatter.total(chunk))
        gain_two = gain_two + gain
        n.grad_second[here, :] = n.grad_row[here, :] + grad
        n.grads[here, :] = n.grad_second[here, :].astype(BF16)
        gather.start(chunk)
        plan.at(f"back_second{chunk}")
    scatter.finish()
    n.put("grad_second")
    n.gain_sums[0:1, :] = gain_two
    n.gain_sums[1:2, :] = gain_three
    n.gain_sums[2:3, :] = gain_four
    gather.wait_near()

    def mixed_rows(slots):
        product = across_product(n.grads[slot_rows(slots, height), :], n.wattend[...]).astype(BF16)
        for index, slot in enumerate(slots):
            n.grad_mixed[span(owner(slot) * height, height), :] = product[index * height : (index + 1) * height]

    mixed_rows((0, 1))
    for chunk in range(CHUNKS):
        gather.pass_on(chunk)
    plan.at("last_passed")
    out_sum.end()
    in_sum.end()
    n.put("sum_out", "sum_in")
    for chunk in range(CHUNKS):
        gather.wait_last(chunk)
    mixed_rows((2, 3))
    n.put("grad_mixed")
    weight_products(n.grad_attend, n.mixed_low, n.grads, 512)
    plan.finish()
    for item in gathers[:2] + gathers[3:] + [edges, edges_back, swap, swap_back]:
        item.finish()


MIDDLE_PLAN = dict(
    start=(11, 13, 12, 10, 21, 23, 22, 20,),
    spread=(-11, -13,),
    second0=(-12,),
    second1=(-21, -23, -22, 31, 30, 33, ),
    passed=(-31, ),
    edges=(-33, ),
    swapped=(-32, 41, 40, 43, 42, ),
    alive=(-41, ),
    third0=(-43, ),
    first=(-42, ),
    grad_out=(51, 53, 52, 50, ),
    back_start=(-51, ),
    back_near=(-53, ),
    back_passed=(-52, ),
    edges_back=(-61, 62, 60, ),
    parts=(-63, ),
    back_spread=(-62, ),
    edged=(32, ),
    grad_in=(61, 63, ),
)


def run_middle(mixed, opened, gains, depth, bn_gain, bn_bias, shards, out_grad):
    height, width = opened.first.shape
    frames, local = mixed.shape
    count = lax.axis_size(SEQ)
    inner = shards.ffn2_in.shape[1]
    settled = dict(out=(inner, width), **{"in": (width, inner)})
    weights = ("out", "in", "conv", "pair")
    return run_kernel(
        middle_kernel,
        1,
        dict(
            mixed=(mixed, True), first=(opened.first, LOAD), gains=(gains, True), wattend=(opened.full_attend, True),
            context=(opened.context, LOAD), depth=(depth, True), bn_gain=(bn_gain, True), bn_bias=(bn_bias, True),
            out_grad=(out_grad, LOAD), pair_parts=(shards.pair, True), shard_conv=(shards.conv, True),
            shard_in=(shards.ffn2_in, True), shard_out=(shards.ffn2_out, True),
        ),
        dict(
            output=((height, width), BF16, KEEP),
            grad_second=((height, width), F32, KEEP),
            grad_mixed=((frames, local), BF16, KEEP),
            grad_attend=((local, width), BF16, True),
            grad_conv=((local, width), BF16, KEEP),
            grad_pair=((width, 2 * local), BF16, KEEP),
            depth_sums=((8, local), F32, True),
            sum_gain=((1, local), F32, True),
            sum_bias=((1, local), F32, True),
            gain_sums=((8, width), F32, True),
            **{f"sum_{name}": ((tall // count, wide), F32, KEEP) for name, (tall, wide) in settled.items()},
        ),
        dict(
            shard_pair=pltpu.VMEM((width // count, 2 * local), BF16),
            wpair=pltpu.VMEM((width, 2 * local), BF16), wconv=pltpu.VMEM((local, width), BF16),
            win=pltpu.VMEM((width, inner), BF16), wout=pltpu.VMEM((inner, width), BF16),
            second=pltpu.VMEM((height, width), F32), third=pltpu.VMEM((height, width), F32),
            grad_row=pltpu.VMEM((height, width), F32),
            rows_conv=pltpu.VMEM((frames, width), BF16), rows=pltpu.VMEM((frames, width), BF16),
            grads=pltpu.VMEM((frames, width), BF16), grads_conv=pltpu.VMEM((frames, width), BF16),
            hidden=pltpu.VMEM((frames, inner), F32), active=pltpu.VMEM((frames, inner), BF16),
            slope=pltpu.VMEM((frames, inner), BF16),
            mixed_low=pltpu.VMEM((frames, local), BF16), paired=pltpu.VMEM((frames, 2 * local), F32),
            gated=pltpu.VMEM((frames + 2 * EDGE, local), F32), normal=pltpu.VMEM((frames, local), F32),
            alive=pltpu.VMEM((frames, local), BF16), grad_batch=pltpu.VMEM((frames, local), F32),
            back=pltpu.VMEM((frames + 2 * EDGE, local), F32), grad_paired=pltpu.VMEM((frames, 2 * local), BF16),
            **{f"grad_{name}": pltpu.VMEM((tall, wide), BF16) for name, (tall, wide) in settled.items()},
            **{f"t_{name}": settle_scratch(tall // count, wide) for name, (tall, wide) in settled.items()},
            **{f"c_{name}": collect_scratch() for name in weights},
            **{f"g{place}": gather_scratch() for place in range(1, 6)},
            s1=scatter_scratch(height, width),
            edge=edges_scratch(), edge_back=edges_scratch(), swap=swap_scratch(8, local), swap_back=swap_scratch(8, local),
        ),
    )


def close_kernel(n):
    height, width = n.grad_second.shape
    frames = 4 * height
    local = n.grad_query.shape[1]
    seq, count = lax.axis_index(SEQ), lax.axis_size(SEQ)
    half = MAXLEN - frames
    loads = [
        pltpu.make_async_copy(n.full_out, n.wout, n.load.at[0]),
        pltpu.make_async_copy(n.full_hidden, n.hidden, n.load.at[1]),
        pltpu.make_async_copy(n.full_in, n.win, n.load.at[2]),
        pltpu.make_async_copy(n.grad_key.at[pl.ds(MAXLEN, frames), :], n.own_back.at[0], n.load.at[3]),
        pltpu.make_async_copy(n.grad_value.at[pl.ds(MAXLEN, frames), :], n.own_back.at[1], n.load.at[4]),
    ]
    for load in loads:
        load.start()
    attend_sum = Settle(n.grad_attend, n.sum_attend, **n.t_attend)
    conv_sum = Settle(n.grad_conv, n.sum_conv, **n.t_conv)
    pair_sum = Settle(n.grad_pair, n.sum_pair, **n.t_pair)
    project = Settle(n.grad_project, n.sum_project, **n.t_project)
    last = [Settle(n.grad_out, n.sum_out, **n.t_out), Settle(n.grad_in, n.sum_in, **n.t_in)]
    scatter, gather, scatter_two = Scatter(**n.s1), Gather(n.grads, **n.g1), Scatter(**n.s2)
    swap = Swap(**n.swap)
    plan = Plan(
        CLOSE_PLAN, (attend_sum, conv_sum, pair_sum, project, last[0], last[1])
    )
    ready = greet(tp_peers() + seq_peers())
    shifts = (1, -1, 2, -2)
    sources = ((MAXLEN + frames, frames), (MAXLEN - frames, frames), (MAXLEN + 2 * frames, half), (0, half))
    targets = ((0, 0), (1, 0), (2, 0), (2, frames - half))

    def back(kind, which):
        begin, size = sources[kind]
        place, row = targets[kind]
        source = (n.grad_key, n.grad_value)[which].at[pl.ds(begin, size), :]
        target = n.others_back.at[which, place, pl.ds(row, size), :]
        peer = {SEQ: lax.rem(seq + shifts[kind] + count, count)}
        return remote(source, target, n.back_send.at[which, kind], n.back_receive.at[which, kind], peer)

    def there(kind, sending):
        other = seq + shifts[kind] if sending else seq - shifts[kind]
        return (other >= 0) & (other < count)

    for kind in range(4):
        place, row = targets[kind]

        @pl.when(jnp.logical_not(there(kind, False)))
        def _():
            for which in range(2):
                size = sources[kind][1]
                n.others_back[which, place, pl.ds(row, size), :] = jnp.zeros((size, local), BF16)

    ready()
    for kind in range(4):

        @pl.when(there(kind, True))
        def _():
            for which in range(2):
                back(kind, which).start()

    n.wait("grad_query")
    for slot in range(4):
        n.grad_rows[pl.ds(slot * height, height), pl.ds(0, local)] = n.grad_query[span(owner(slot) * height, height), :]
    for kind in range(4):

        @pl.when(there(kind, False))
        def _():
            for which in range(2):
                back(kind, which).wait_recv()

    plan.at("returned")
    loads[3].wait()
    loads[4].wait()
    for slot in range(4):
        place = span(owner(slot) * height, height)
        for which in range(2):
            total = n.own_back[which, place, :].astype(F32)
            for other in range(3):
                total = total + n.others_back[which, other, place, :].astype(F32)
            n.grad_rows[pl.ds(slot * height, height), pl.ds((which + 1) * local, local)] = total.astype(BF16)
    n.wait("wproject")
    scatter.spread(
        lambda slots, cols: across_product(n.grad_rows[slot_rows(slots, height), :], n.wproject[cols, :]), width
    )
    plan.at("spread")
    n.wait("rows_two")
    weight_products(n.grad_project, n.rows_two, n.grad_rows)
    plan.at("grad_project")
    n.wait("first", "grad_second")
    gain_one = jnp.zeros((1, width), F32)
    for chunk in range(CHUNKS):
        here = scatter.rows(chunk)
        grad, gain = norm_back(n.first[here, :], n.gains[1:2, :], scatter.total(chunk))
        gain_one = gain_one + gain
        n.grad_first[here, :] = n.grad_second[here, :] + grad
        n.grads[here, :] = (0.5 * n.grad_first[here, :]).astype(BF16)
        gather.start(chunk)
        plan.at(f"first{chunk}")

    def wait_out():
        loads[0].wait()
        loads[1].wait()

    def products():
        weight_products(n.grad_out, n.active, n.grads)
        plan.at("grad_out")
        n.wait("rows")
        weight_products(n.grad_in, n.rows, n.slope)
        plan.at("grad_in")

    ffn_backward(
        gather, scatter_two, n.win, n.wout, n.hidden, n.active, n.slope, wait_out, loads[2].wait, products, plan.at
    )
    n.wait("values")
    gain_zero = jnp.zeros((1, width), F32)
    for chunk in range(CHUNKS):
        here = scatter.rows(chunk)
        grad, gain = norm_back(n.values[here, :].astype(F32), n.gains[0:1, :], scatter_two.total(chunk))
        gain_zero = gain_zero + gain
        n.input_grad[here, :] = n.grad_first[here, :] + grad
        plan.at(f"zero{chunk}")
    n.small[0, 0:1, :] = gain_zero
    n.small[0, 1:2, :] = gain_one
    n.small[0, 2:5, :] = n.gain_late[0:3, :]
    n.small[0, 5:8, :] = jnp.zeros((3, width), F32)
    near, far = tp_peers()
    hop = remote(n.small.at[0], n.small.at[1], n.small_sem.at[0], n.small_sem.at[1], near)
    hop.start()
    hop.wait_recv()
    n.small[2] = n.small[0] + n.small[1]
    hop_two = remote(n.small.at[2], n.small.at[3], n.small_sem.at[2], n.small_sem.at[3], far)
    hop_two.start()
    hop_two.wait_recv()
    swap.blocks[0, :, pl.ds(0, width)] = n.small[2] + n.small[3]
    swap.blocks[0, :, pl.ds(width, local)] = n.depth_sums[...]
    swap.start()
    plan.at("small")
    n.put("input_grad")
    attend_sum.end()
    conv_sum.end()
    pair_sum.end()
    project.end()
    n.put("sum_attend", "sum_conv", "sum_pair", "sum_project")
    plan.at("ended")
    swap.wait()
    total = jnp.zeros((8, width + local), F32)
    for item in in_order(swap):
        total = total + item
    n.gain_total[...] = total[:5, :width]
    n.depth_total[...] = total[:KERNEL, width:]
    for name, task in zip(("sum_out", "sum_in"), last):
        task.end()
        n.put(name)
    for kind in range(4):

        @pl.when(there(kind, True))
        def _():
            for which in range(2):
                back(kind, which).wait_send()

    hop.wait_send()
    hop_two.wait_send()
    plan.finish()
    for item in [scatter, gather, scatter_two, swap]:
        item.finish()


CLOSE_PLAN = dict(
    returned=(31, 33, 32, 30, 21, 23, 22, 20, 11, 13, 12, 10,),
    spread=(-31,),
    grad_project=(-33, 41, 43, 42, 40,),
    first0=(-32,),
    first1=(-21, -23, -22,),
    first=(-11, -13, -12,),
    grad_out=(-41, -43, 51, 53, 52, 50,),
    grad_in=(-42, 61, 63, 62, 60,),
    second=(-51, -53,),
    zero0=(-52,),
    small=(-61,),
    ended=(-63, -62,),
)


def run_close(values, gains, opened, middle, grad_query, grad_key, grad_value):
    height, width = values.shape
    frames, local = grad_query.shape
    count = lax.axis_size(SEQ)
    inner = opened.full_in.shape[1]
    settled = dict(
        pair=(width, 2 * local), conv=(local, width), attend=(local, width),
        project=(width, 3 * local), out=(inner, width), **{"in": (width, inner)},
    )
    return run_kernel(
        close_kernel,
        4,
        dict(
            values=(values, LOAD), gains=(gains, True), first=(opened.first, LOAD), rows=(opened.rows, LOAD),
            rows_two=(opened.rows_two, LOAD), full_hidden=(opened.hidden, False),
            full_in=(opened.full_in, False), full_out=(opened.full_out, False),
            wproject=(opened.full_project, LOAD), grad_second=(middle.grad_second, LOAD), grad_query=(grad_query, LOAD),
            grad_key=(grad_key, False), grad_value=(grad_value, False), grad_attend=(middle.grad_attend, False),
            grad_conv=(middle.grad_conv, False), grad_pair=(middle.grad_pair, False),
            depth_sums=(middle.depth_sums, True), gain_late=(middle.gain_sums, True),
        ),
        dict(
            input_grad=((height, width), F32, KEEP),
            gain_total=((5, width), F32, True),
            depth_total=((KERNEL, local), F32, True),
            **{f"sum_{name}": ((tall // count, wide), F32, KEEP) for name, (tall, wide) in settled.items()},
        ),
        dict(
            win=pltpu.VMEM((width, inner), BF16), wout=pltpu.VMEM((inner, width), BF16),
            hidden=pltpu.VMEM((frames, inner), F32), active=pltpu.VMEM((frames, inner), BF16),
            slope=pltpu.VMEM((frames, inner), BF16), grads=pltpu.VMEM((frames, width), BF16),
            grad_first=pltpu.VMEM((height, width), F32),
            own_back=pltpu.VMEM((2, frames, local), BF16), others_back=pltpu.VMEM((2, 3, frames, local), BF16),
            grad_rows=pltpu.VMEM((frames, 3 * local), BF16),
            grad_project=pltpu.VMEM((width, 3 * local), BF16),
            grad_in=pltpu.VMEM((width, inner), BF16), grad_out=pltpu.VMEM((inner, width), BF16),
            **{f"t_{name}": settle_scratch(tall // count, wide, name in ("attend", "conv", "pair")) for name, (tall, wide) in settled.items()},
            g1=gather_scratch(), s1=scatter_scratch(height, width), s2=scatter_scratch(height, width),
            swap=swap_scratch(8, width + local),
            small=pltpu.VMEM((4, 8, width), F32), small_sem=pltpu.SemaphoreType.DMA((4,)),
            back_send=pltpu.SemaphoreType.DMA((2, 4)), back_receive=pltpu.SemaphoreType.DMA((2, 4)),
            load=pltpu.SemaphoreType.DMA((5,)),
        ),
    )


def hand_kernel(names, n):
    taken = [pltpu.make_async_copy(n.source[name], n.buffer[name], n.sems.at[0, place]) for place, name in enumerate(names)]
    given = []
    for copy in taken:
        copy.start()
    for place, name in enumerate(names):
        taken[place].wait()
        buffer, target = n.buffer[name], n.target[name]
        if name == "project":
            wide = target.shape[2]
            copies = [
                pltpu.make_async_copy(buffer.at[:, pl.ds(part * wide, wide)], target.at[part], n.sems.at[1 + part, place])
                for part in range(3)
            ]
        elif name == "pair":
            wide = target.shape[2]
            for part in range(2):
                n.apart[:, part, :] = buffer[:, pl.ds(part * wide, wide)]
            copies = [pltpu.make_async_copy(n.apart, target, n.sems.at[1, place])]
        else:
            copies = [pltpu.make_async_copy(buffer, target, n.sems.at[1, place])]
        for copy in copies:
            copy.start()
        given += copies
    for copy in given:
        copy.wait()


def hand_over(arrays):
    names = list(arrays)

    def shape_of(name):
        tall, wide = arrays[name].shape
        return {"project": (3, tall, wide // 3), "pair": (tall, 2, wide // 2)}.get(name, (tall, wide))

    def kernel(*refs):
        count = len(names)
        hand_kernel(
            names,
            SimpleNamespace(
                source=dict(zip(names, refs)),
                target=dict(zip(names, refs[count:])),
                buffer=dict(zip(names, refs[2 * count :])),
                apart=refs[3 * count],
                sems=refs[3 * count + 1],
            ),
        )

    results = pl.pallas_call(
        kernel,
        out_shape=tuple(jax.ShapeDtypeStruct(shape_of(name), arrays[name].dtype) for name in names),
        in_specs=[IN_PLACE] * len(names),
        out_specs=tuple([IN_PLACE] * len(names)),
        scratch_shapes=[pltpu.VMEM(arrays[name].shape, arrays[name].dtype) for name in names]
        + [pltpu.VMEM(shape_of("pair"), F32), pltpu.SemaphoreType.DMA((4, len(names)))],
        compiler_params=pltpu.CompilerParams(vmem_limit_bytes=VMEM_LIMIT),
    )(*arrays.values())
    return SimpleNamespace(**dict(zip(names, results)))


def allowed_block(codes, seg_row, key_begin, query_begin):
    wide = jnp.concatenate([codes] * (QUERY_BLOCK // 128), axis=1)
    place = lax.broadcasted_iota(jnp.int32, (KEY_BLOCK, QUERY_BLOCK), 0) - lax.broadcasted_iota(
        jnp.int32, (KEY_BLOCK, QUERY_BLOCK), 1
    )
    return (wide == seg_row) | (place == query_begin - key_begin)


def head_cols(local):
    return [pl.ds(head * HEAD_DIM, HEAD_DIM) for head in range(local // HEAD_DIM)]


def attend_kernel(bounds, query, keys, values, seg_row, codes, out, totals):
    step = pl.program_id(0)
    heads = head_cols(query.shape[1])
    segs = seg_row[...]

    def one(index, carried):
        here = span(index * KEY_BLOCK, KEY_BLOCK)
        allowed = allowed_block(codes[here, :], segs, index * KEY_BLOCK, MAXLEN + step * QUERY_BLOCK)
        scores = [across_product(keys[here, cols], query[:, cols]) * (SCORE_SCALE * LOG2E) for cols in heads]
        result = []
        for (highest, total, mixed), score, cols in zip(carried, scores, heads):
            score = jnp.where(allowed, score, -1e30)
            top = jnp.maximum(highest, jnp.max(score, axis=0, keepdims=True))
            fade = jnp.exp2(highest - top)
            weights = jnp.exp2(score - top)
            total = total * fade + jnp.sum(weights, axis=0, keepdims=True)
            mixed = mixed * fade + inner_product(values[here, cols], weights.astype(BF16))
            result.append((top, total, mixed))
        return tuple(result)

    start = (
        jnp.full((1, QUERY_BLOCK), -1e30, F32),
        jnp.zeros((1, QUERY_BLOCK), F32),
        jnp.zeros((HEAD_DIM, QUERY_BLOCK), F32),
    )
    ends = lax.fori_loop(bounds[step, 0], bounds[step, 1], one, (start,) * len(heads))
    for head, ((highest, total, mixed), cols) in enumerate(zip(ends, heads)):
        out[:, cols] = jnp.transpose(mixed / total)
        totals[head] = highest + jnp.log2(total)


def attend_back_kernel(
    bounds, query, keys, values, grad, mixed, totals, seg_row, codes, grad_query, key_out, value_out, grad_key, grad_value
):
    step = pl.program_id(0)
    heads = head_cols(query.shape[1])

    @pl.when(step == 0)
    def _():
        grad_key[...] = jnp.zeros_like(grad_key)
        grad_value[...] = jnp.zeros_like(grad_value)

    segs = seg_row[...]
    centres = [
        jnp.sum(jnp.transpose(grad[:, cols].astype(F32) * mixed[:, cols]), axis=0, keepdims=True) for cols in heads
    ]

    def one(index, carried):
        here = span(index * KEY_BLOCK, KEY_BLOCK)
        allowed = allowed_block(codes[here, :], segs, index * KEY_BLOCK, MAXLEN + step * QUERY_BLOCK)
        scores = [across_product(keys[here, cols], query[:, cols]) * (SCORE_SCALE * LOG2E) for cols in heads]
        slopes = [across_product(values[here, cols], grad[:, cols]) for cols in heads]
        result = []
        for head, (total, score, slope, centre, cols) in enumerate(zip(carried, scores, slopes, centres, heads)):
            probs = jnp.where(allowed, jnp.exp2(score - totals[head]), 0.0)
            grad_scores = (probs * (slope - centre) * SCORE_SCALE).astype(BF16)
            grad_value[here, cols] += plain_product(probs.astype(BF16), grad[:, cols])
            grad_key[here, cols] += plain_product(grad_scores, query[:, cols])
            result.append(total + inner_product(grad_scores, keys[here, cols]))
        return tuple(result)

    ends = lax.fori_loop(
        bounds[step, 0], bounds[step, 1], one, (jnp.zeros((QUERY_BLOCK, HEAD_DIM), F32),) * len(heads)
    )
    for total, cols in zip(ends, heads):
        grad_query[:, cols] = total.astype(BF16)

    @pl.when(step == pl.num_programs(0) - 1)
    def _():
        key_out[...] = grad_key[...].astype(BF16)
        value_out[...] = grad_value[...].astype(BF16)


def attend_specs(frames, local, window):
    heads = local // HEAD_DIM
    return dict(
        bounds=pl.BlockSpec(memory_space=pltpu.SMEM),
        rows=pl.BlockSpec((QUERY_BLOCK, local), lambda i: (i, 0)),
        keys=pl.BlockSpec((window, local), lambda i: (0, 0)),
        values=pl.BlockSpec((window, local), lambda i: (0, 1)),
        segs=pl.BlockSpec((1, QUERY_BLOCK), lambda i: (0, i)),
        codes=pl.BlockSpec((window, 128), lambda i: (0, 0)),
        totals=pl.BlockSpec((heads, 1, QUERY_BLOCK), lambda i: (0, 0, i)),
    )


def attend(queries, both, context):
    bounds, seg_row, codes = context
    frames, local = queries.shape
    specs = attend_specs(frames, local, both.shape[0])
    return pl.pallas_call(
        attend_kernel,
        grid=(frames // QUERY_BLOCK,),
        in_specs=[specs[name] for name in ("bounds", "rows", "keys", "values", "segs", "codes")],
        out_specs=[specs["rows"], specs["totals"]],
        out_shape=(
            jax.ShapeDtypeStruct((frames, local), F32),
            jax.ShapeDtypeStruct((local // HEAD_DIM, 1, frames), F32),
        ),
        compiler_params=pltpu.CompilerParams(vmem_limit_bytes=VMEM_LIMIT),
        cost_estimate=pl.CostEstimate(
            flops=4 * frames * MAXLEN * local, bytes_accessed=8 << 20, transcendentals=0
        ),
    )(bounds, queries, both, both, seg_row, codes)


def attend_back(queries, both, grads, mixed, totals, context):
    bounds, seg_row, codes = context
    frames, local = queries.shape
    window = both.shape[0]
    specs = attend_specs(frames, local, window)
    return pl.pallas_call(
        attend_back_kernel,
        grid=(frames // QUERY_BLOCK,),
        in_specs=[
            specs[name]
            for name in ("bounds", "rows", "keys", "values", "rows", "rows", "totals", "segs", "codes")
        ],
        out_specs=[specs["rows"], specs["keys"], specs["keys"]],
        out_shape=(
            jax.ShapeDtypeStruct((frames, local), BF16),
            jax.ShapeDtypeStruct((window, local), BF16),
            jax.ShapeDtypeStruct((window, local), BF16),
        ),
        scratch_shapes=[pltpu.VMEM((window, local), F32), pltpu.VMEM((window, local), F32)],
        compiler_params=pltpu.CompilerParams(vmem_limit_bytes=VMEM_LIMIT),
        cost_estimate=pl.CostEstimate(
            flops=10 * frames * MAXLEN * local, bytes_accessed=16 << 20, transcendentals=0
        ),
    )(bounds, queries, both, both, grads, mixed, totals, seg_row, codes)


def body(
    inputs,
    ln_gains,
    ffn1_in,
    ffn1_out,
    qkv_weight,
    attn_out,
    conv_in,
    conv_depth,
    bn_gain,
    bn_bias,
    conv_out,
    ffn2_in,
    ffn2_out,
    segment_ids,
    pad_mask,
    out_grad,
):
    frames = inputs.shape[0] * lax.axis_size(TP)
    gain_row, bias_row = bn_gain[None, :], bn_bias[None, :]
    shards = SimpleNamespace(
        ffn1_in=ffn1_in,
        ffn1_out=ffn1_out,
        project=jnp.transpose(qkv_weight, (1, 0, 2)),
        attend=attn_out,
        pair=conv_in,
        conv=conv_out,
        ffn2_in=ffn2_in,
        ffn2_out=ffn2_out,
    )
    opened = run_open(
        inputs, ln_gains, shards, segment_ids.reshape(-1, 128), pad_mask.reshape(-1, 128)
    )
    seg_row = lax.dynamic_slice_in_dim(segment_ids, lax.axis_index(SEQ) * frames, frames)[None, :]
    context = (opened.bounds, seg_row, opened.codes)
    mixed, totals = attend(opened.queries, opened.window, context)
    middle = run_middle(mixed, opened, ln_gains, conv_depth, gain_row, bias_row, shards, out_grad)
    grad_query, grad_key, grad_value = attend_back(
        opened.queries, opened.window, middle.grad_mixed, mixed, totals, context
    )
    closed = run_close(inputs, ln_gains, opened, middle, grad_query, grad_key, grad_value)
    given = hand_over(
        dict(
            output=middle.output,
            input_grad=closed.input_grad,
            gains=closed.gain_total,
            first_in=closed.sum_in,
            first_out=closed.sum_out,
            project=closed.sum_project,
            attend=closed.sum_attend,
            pair=closed.sum_pair,
            depth=closed.depth_total,
            gain=middle.sum_gain,
            bias=middle.sum_bias,
            conv=closed.sum_conv,
            second_in=middle.sum_in,
            second_out=middle.sum_out,
        )
    )
    return (
        given.output,
        given.input_grad,
        given.gains,
        given.first_in,
        given.first_out,
        jnp.transpose(given.project, (1, 0, 2)),
        given.attend,
        given.pair,
        given.depth,
        given.gain[0],
        given.bias[0],
        given.conv,
        given.second_in,
        given.second_out,
    )


def solution(mesh):
    return jax.shard_map(
        body,
        mesh=mesh,
        in_specs=(
            P((SEQ, TP), None),
            P(),
            P(SEQ, TP),
            P((TP, SEQ), None),
            P(SEQ, None, TP),
            P((TP, SEQ), None),
            P(SEQ, None, TP),
            P(None, TP),
            P(TP),
            P(TP),
            P((TP, SEQ), None),
            P(SEQ, TP),
            P((TP, SEQ), None),
            P(),
            P(),
            P((SEQ, TP), None),
        ),
        out_specs=(
            P((SEQ, TP), None),
            P((SEQ, TP), None),
            P(),
            P(SEQ, TP),
            P((TP, SEQ), None),
            P(SEQ, None, TP),
            P((TP, SEQ), None),
            P(SEQ, None, TP),
            P(None, TP),
            P(TP),
            P(TP),
            P((TP, SEQ), None),
            P(SEQ, TP),
            P((TP, SEQ), None),
        ),
        check_vma=False,
    )
```

```python
import math
from types import SimpleNamespace

import jax
import jax.numpy as jnp
from jax import lax
from jax.experimental import pallas as pl
from jax.experimental.pallas import tpu as pltpu
from jax.sharding import PartitionSpec as P

SEQ, TP = "seq", "tp"
LOAD, KEEP = "load", "keep"
HEAD_DIM = 128
KERNEL = 5
MAXLEN = 1536
EPSILON = 1e-05
CHUNKS = 2
EDGE = 8
VMEM_LIMIT = 62 << 20
QUERY_BLOCK = 256
KEY_BLOCK = 512
SCORE_SCALE = 1.0 / math.sqrt(HEAD_DIM)
LOG2E = 1.4426950408889634
BF16 = jnp.bfloat16
F32 = jnp.float32
IN_VMEM = pl.BlockSpec(memory_space=pltpu.VMEM)
IN_PLACE = pl.BlockSpec(memory_space=pl.ANY)


def plain_product(left, right):
    return jnp.dot(left, right, preferred_element_type=F32)


def inner_product(left, right):
    return lax.dot_general(left, right, (((0,), (0,)), ((), ())), preferred_element_type=F32)


def across_product(left, right):
    return lax.dot_general(left, right, (((1,), (1,)), ((), ())), preferred_element_type=F32)


def swish(values):
    return values * jax.nn.sigmoid(values)


def standard_rows(values):
    centred = values - jnp.mean(values, axis=-1, keepdims=True)
    spread = jnp.mean(centred * centred, axis=-1, keepdims=True)
    inverse = lax.rsqrt(spread + EPSILON)
    return (centred * inverse, inverse)


def norm_rows(values, gain_row):
    return standard_rows(values)[0] * gain_row


def norm_back(values, gain_row, grads):
    normal, inverse = standard_rows(values)
    scaled = grads * gain_row
    result = inverse * (
        scaled
        - jnp.mean(scaled, axis=-1, keepdims=True)
        - normal * jnp.mean(scaled * normal, axis=-1, keepdims=True)
    )
    return (result, jnp.sum(grads * normal, axis=0, keepdims=True))


def flip(index, bit):
    return index + bit - 2 * bit * lax.rem(lax.div(index, bit), 2)


def span(begin, size):
    return pl.ds(pl.multiple_of(begin, size), size)


def rows_at(begin, size):
    return pl.ds(begin, size) if isinstance(begin, int) else span(begin, size)


def remote(source, target, send, receive, peer):
    return pltpu.make_async_remote_copy(
        src_ref=source,
        dst_ref=target,
        send_sem=send,
        recv_sem=receive,
        device_id=peer,
        device_id_type=pl.DeviceIdType.MESH,
    )


def tp_peers():
    me = lax.axis_index(TP)
    return [{TP: flip(me, 1)}, {TP: flip(me, 2)}]


def seq_peers():
    me, count = lax.axis_index(SEQ), lax.axis_size(SEQ)
    return [{SEQ: lax.rem(me + step, count)} for step in range(1, count)]


def greet(peers):
    barrier = pltpu.get_barrier_semaphore()
    for peer in peers:
        pl.semaphore_signal(barrier, inc=1, device_id=peer, device_id_type=pl.DeviceIdType.MESH)
    return lambda: pl.semaphore_wait(barrier, len(peers))


def owner(slot):
    me = lax.axis_index(TP)
    if slot & 1:
        me = flip(me, 1)
    if slot & 2:
        me = flip(me, 2)
    return me


def tiles(total, tile, body):
    def one(index, nothing):
        body(span(index * tile, tile))
        return nothing

    lax.fori_loop(0, total // tile, one, 0)


class Gather:
    def __init__(self, rows, send, receive):
        self.near, self.far = tp_peers()
        self.height = rows.shape[0] // 4
        self.piece = self.height // CHUNKS
        self.rows, self.send, self.receive = rows, send, receive

    def part(self, slot, chunk):
        return self.rows.at[rows_at(slot * self.height + chunk * self.piece, self.piece), :]

    def hop(self, kind, chunk):
        source, target = ((0, 1), (0, 2), (2, 3))[kind]
        return remote(
            self.part(source, chunk),
            self.part(target, chunk),
            self.send.at[kind, chunk],
            self.receive.at[kind, chunk],
            self.far if kind == 1 else self.near,
        )

    def start(self, chunk):
        self.hop(1, chunk).start()
        self.hop(0, chunk).start()

    def wait_near(self):
        for chunk in range(CHUNKS):
            self.hop(0, chunk).wait_recv()

    def pass_on(self, chunk):
        self.hop(1, chunk).wait_recv()
        self.hop(2, chunk).start()

    def wait_last(self, chunk):
        self.hop(2, chunk).wait_recv()

    def finish(self):
        for chunk in range(CHUNKS):
            for kind in range(3):
                self.hop(kind, chunk).wait_send()


def each_chunk(body):
    def one(chunk, nothing):
        body(chunk)
        return nothing

    lax.fori_loop(0, CHUNKS, one, 0)


def gather_scratch():
    return dict(send=pltpu.SemaphoreType.DMA((3, CHUNKS)), receive=pltpu.SemaphoreType.DMA((3, CHUNKS)))


class Scatter:
    def __init__(self, own, passing, outgoing, incoming, send, receive):
        self.near, self.far = tp_peers()
        self.height = own.shape[0]
        self.piece = self.height // CHUNKS
        self.own, self.passing = own, passing
        self.outgoing, self.incoming, self.send, self.receive = outgoing, incoming, send, receive

    def rows(self, chunk):
        return rows_at(chunk * self.piece, self.piece)

    def copy(self, kind, chunk):
        here = self.rows(chunk)
        return remote(
            self.outgoing.at[kind, here, :],
            self.incoming.at[kind, here, :],
            self.send.at[kind, chunk],
            self.receive.at[kind, chunk],
            self.far if kind == 2 else self.near,
        )

    def start(self, kind):
        for chunk in range(CHUNKS):
            self.copy(kind, chunk).start()

    def relay(self, chunk):
        here = self.rows(chunk)
        self.copy(1, chunk).wait_recv()
        self.outgoing[2, here, :] = (self.passing[here, :] + self.incoming[1, here, :].astype(F32)).astype(BF16)
        self.copy(2, chunk).start()

    def total(self, chunk):
        here = self.rows(chunk)
        self.copy(0, chunk).wait_recv()
        self.copy(2, chunk).wait_recv()
        return self.own[here, :] + self.incoming[0, here, :].astype(F32) + self.incoming[2, here, :].astype(F32)

    def spread(self, product, width, tile=256):
        height = self.height

        def far(cols):
            term = product((2, 3), cols)
            self.passing[:, cols] = term[:height]
            self.outgoing[1, :, cols] = term[height:].astype(BF16)

        tiles(width, tile, far)
        self.start(1)

        def near(cols):
            term = product((0, 1), cols)
            self.own[:, cols] = term[:height]
            self.outgoing[0, :, cols] = term[height:].astype(BF16)

        tiles(width, tile, near)
        for chunk in range(CHUNKS):
            self.relay(chunk)
        self.start(0)

    def finish(self):
        for kind in range(3):
            for chunk in range(CHUNKS):
                self.copy(kind, chunk).wait_send()


def scatter_scratch(height, width):
    return dict(
        own=pltpu.VMEM((height, width), F32),
        passing=pltpu.VMEM((height, width), F32),
        outgoing=pltpu.VMEM((3, height, width), BF16),
        incoming=pltpu.VMEM((3, height, width), BF16),
        send=pltpu.SemaphoreType.DMA((3, CHUNKS)),
        receive=pltpu.SemaphoreType.DMA((3, CHUNKS)),
    )


class Collect:
    def __init__(self, shard, full, send, receive, pair_send, pair_receive, local):
        self.me, self.count = lax.axis_index(SEQ), lax.axis_size(SEQ)
        self.groups = self.count // 2
        self.pair = {SEQ: flip(self.me, 1)}
        self.shard, self.full, self.height = shard, full, shard.shape[0]
        self.send, self.receive, self.pair_send, self.pair_receive = send, receive, pair_send, pair_receive
        self.local = pltpu.make_async_copy(shard, self.block(self.me), local.at[0])

    def block(self, index):
        return self.full.at[span(index * self.height, self.height), :]

    def out(self, step):
        peer = {SEQ: lax.rem(self.me + 2 * step, self.count)}
        return remote(self.shard, self.block(self.me), self.send.at[step - 1], self.receive.at[step - 1], peer)

    def over(self, step):
        if step == 0:
            source, place = self.shard, self.me
        else:
            place = lax.rem(self.me + self.count - 2 * step, self.count)
            source = self.block(place)
        return remote(source, self.block(place), self.pair_send.at[step], self.pair_receive.at[step], self.pair)

    def kick(self, step):
        if step == 0:
            self.over(0).start()
            self.local.start()
        else:
            self.out(step).start()

    def turn(self, step):
        if step:
            self.out(step).wait_recv()
            self.over(step).start()

    def end(self):
        self.local.wait()
        for step in range(self.groups):
            self.over(step).wait_recv()

    def finish(self):
        for step in range(self.groups):
            self.over(step).wait_send()
            if step:
                self.out(step).wait_send()


def collect_scratch():
    groups = lax.axis_size(SEQ) // 2
    return dict(
        send=pltpu.SemaphoreType.DMA((groups,)),
        receive=pltpu.SemaphoreType.DMA((groups,)),
        pair_send=pltpu.SemaphoreType.DMA((groups,)),
        pair_receive=pltpu.SemaphoreType.DMA((groups,)),
        local=pltpu.SemaphoreType.DMA((1,)),
    )


class Settle:
    def __init__(self, source, result, partner, others, send, receive, far_send, far_receive, half=None, load=None):
        self.me, self.count = lax.axis_index(SEQ), lax.axis_size(SEQ)
        self.groups = self.count // 2
        self.other = flip(self.me, 1)
        self.source, self.result, self.half, self.partner, self.others = source, result, half, partner, others
        self.height = result.shape[0]
        self.load, self.send, self.receive = load, send, receive
        self.far_send, self.far_receive = far_send, far_receive

    def block(self, base, step):
        place = lax.rem(base + 2 * step, self.count)
        return self.source.at[span(place * self.height, self.height), :]

    def mine(self, step):
        return self.block(self.me, step) if self.half is None else self.half.at[step]

    def swap(self, step):
        return remote(
            self.block(self.other, step),
            self.partner.at[step],
            self.send.at[step],
            self.receive.at[step],
            {SEQ: self.other},
        )

    def fetch(self, step):
        return pltpu.make_async_copy(self.block(self.me, step), self.half.at[step], self.load.at[step])

    def away(self, step):
        peer = {SEQ: lax.rem(self.me + 2 * step, self.count)}
        return remote(
            self.mine(step), self.others.at[step], self.far_send.at[step], self.far_receive.at[step], peer
        )

    def kick(self, step):
        self.swap(step).start()
        if self.half is not None:
            self.fetch(step).start()

    def turn(self, step):
        if step:
            if self.half is not None:
                self.fetch(step).wait()
            self.swap(step).wait_recv()
            mine = self.mine(step)
            mine[...] = (mine[...].astype(F32) + self.partner[step].astype(F32)).astype(BF16)
            self.away(step).start()

    def end(self):
        if self.half is not None:
            self.fetch(0).wait()
        self.swap(0).wait_recv()
        total = self.mine(0)[...].astype(F32) + self.partner[0].astype(F32)
        for step in range(1, self.groups):
            self.away(step).wait_recv()
            total = total + self.others[step].astype(F32)
        self.result[...] = total

    def finish(self):
        for step in range(self.groups):
            self.swap(step).wait_send()
            if step:
                self.away(step).wait_send()


def settle_scratch(height, width, apart=False):
    groups = lax.axis_size(SEQ) // 2
    more = dict(half=pltpu.VMEM((groups, height, width), BF16), load=pltpu.SemaphoreType.DMA((groups,)))
    return dict(
        **(more if apart else {}),
        partner=pltpu.VMEM((groups, height, width), BF16),
        others=pltpu.VMEM((groups, height, width), BF16),
        send=pltpu.SemaphoreType.DMA((groups,)),
        receive=pltpu.SemaphoreType.DMA((groups,)),
        far_send=pltpu.SemaphoreType.DMA((groups,)),
        far_receive=pltpu.SemaphoreType.DMA((groups,)),
    )


class Plan:
    def __init__(self, points, tasks):
        self.points, self.tasks = points, tasks
        self.left = set()
        for place in range(1, len(tasks) + 1):
            self.left |= {10 * place + step for step in range(4)} | {-10 * place - step for step in range(1, 4)}

    def at(self, point):
        for number in self.points.get(point, ()):
            self.left.remove(number)
            place, digit = divmod(abs(number), 10)
            task = self.tasks[place - 1]
            for step in range(digit, task.groups if digit == 3 else min(digit + 1, task.groups)):
                (task.kick if number > 0 else task.turn)(step)

    def finish(self):
        assert not self.left, "steps left"
        for task in self.tasks:
            task.finish()


class Swap:
    def __init__(self, blocks, send, receive):
        self.me, self.count = lax.axis_index(SEQ), lax.axis_size(SEQ)
        self.blocks, self.send, self.receive = blocks, send, receive

    def copy(self, step):
        peer = {SEQ: lax.rem(self.me + step, self.count)}
        return remote(self.blocks.at[0], self.blocks.at[step], self.send.at[step], self.receive.at[step], peer)

    def start(self):
        for step in range(1, self.count):
            self.copy(step).start()

    def wait(self):
        for step in range(1, self.count):
            self.copy(step).wait_recv()

    def finish(self):
        for step in range(1, self.count):
            self.copy(step).wait_send()


def swap_scratch(height, width):
    count = lax.axis_size(SEQ)
    return dict(
        blocks=pltpu.VMEM((count, height, width), F32),
        send=pltpu.SemaphoreType.DMA((count,)),
        receive=pltpu.SemaphoreType.DMA((count,)),
    )


class Edges:
    def __init__(self, padded, send, receive):
        self.me, self.count = lax.axis_index(SEQ), lax.axis_size(SEQ)
        self.padded, self.send, self.receive = padded, send, receive
        self.frames = padded.shape[0] - 2 * EDGE

    def up(self):
        source = self.padded.at[pl.ds(self.frames, EDGE), :]
        target = self.padded.at[pl.ds(0, EDGE), :]
        peer = {SEQ: lax.rem(self.me + 1, self.count)}
        return remote(source, target, self.send.at[0], self.receive.at[0], peer)

    def down(self):
        source = self.padded.at[pl.ds(EDGE, EDGE), :]
        target = self.padded.at[pl.ds(EDGE + self.frames, EDGE), :]
        peer = {SEQ: lax.rem(self.me + self.count - 1, self.count)}
        return remote(source, target, self.send.at[1], self.receive.at[1], peer)

    def start(self):
        self.up().start()
        self.down().start()

    def wait(self):
        self.up().wait_recv()
        self.down().wait_recv()

    def finish(self):
        self.up().wait_send()
        self.down().wait_send()


def edges_scratch():
    return dict(send=pltpu.SemaphoreType.DMA((2,)), receive=pltpu.SemaphoreType.DMA((2,)))


def run_kernel(body, number, inputs, outputs, scratch, flops=1 << 33):
    loads = [name for name, (_, place) in inputs.items() if place == LOAD]
    keeps = [name for name, (_, _, place) in outputs.items() if place == KEEP]
    moved = {name: pltpu.VMEM(inputs[name][0].shape, inputs[name][0].dtype) for name in loads}
    moved.update({name: pltpu.VMEM(outputs[name][0], outputs[name][1]) for name in keeps})
    flat, groups = list(moved.values()) + [pltpu.SemaphoreType.DMA((max(1, len(moved)),))], []
    for name, item in scratch.items():
        parts = item if isinstance(item, dict) else {None: item}
        groups.append((name, list(parts)))
        flat.extend(parts.values())

    def kernel(*refs):
        given = dict(zip(list(inputs) + list(outputs), refs))
        rest = list(refs[len(given) :])
        near = {name: rest.pop(0) for name in moved}
        sems = rest.pop(0)
        copies = {}
        for place, name in enumerate(moved):
            ends = (given[name], near[name]) if name in loads else (near[name], given[name])
            copies[name] = pltpu.make_async_copy(*ends, sems.at[place])
        given.update(near)
        for name, keys in groups:
            taken = {key: rest.pop(0) for key in keys}
            given[name] = taken[None] if None in taken else taken
        for name in loads:
            copies[name].start()
        waiting, going = list(loads), []

        def wait(*names):
            for name in names:
                waiting.remove(name)
                copies[name].wait()

        def put(*names):
            for name in names:
                going.append(name)
                copies[name].start()

        body(SimpleNamespace(**given, wait=wait, put=put))
        assert not waiting and sorted(going) == sorted(keeps), "copies left"
        for name in going:
            copies[name].wait()

    results = pl.pallas_call(
        kernel,
        out_shape=tuple(jax.ShapeDtypeStruct(shape, kind) for shape, kind, _ in outputs.values()),
        in_specs=[IN_VMEM if place is True else IN_PLACE for _, place in inputs.values()],
        out_specs=tuple(IN_VMEM if place is True else IN_PLACE for _, _, place in outputs.values()),
        scratch_shapes=flat,
        compiler_params=pltpu.CompilerParams(
            collective_id=number, has_side_effects=True, vmem_limit_bytes=VMEM_LIMIT
        ),
        cost_estimate=pl.CostEstimate(flops=flops, bytes_accessed=16 << 20, transcendentals=0),
    )(*[array for array, _ in inputs.values()])
    return SimpleNamespace(**dict(zip(outputs, results)))


def ffn_forward(gather, scatter, win, wout, hidden, active, wait_in, wait_out, late=False, at=lambda point: None):
    rows, height, piece = gather.rows, gather.height, gather.piece
    width, inner = win.shape
    pair = pl.ds(0, 2 * height)
    gather.wait_near()
    wait_in()

    def first(cols):
        product = plain_product(rows[pair, :], win[:, cols])
        hidden[pair, cols] = product
        active[pair, cols] = swish(product).astype(BF16)

    def second(cols):
        product = plain_product(active[pair, :], wout[:, cols])
        scatter.own[:, cols] = product[:height]
        scatter.outgoing[0, :, cols] = product[height:].astype(BF16)

    def far_rows(chunk):
        return (
            rows_at(2 * height + chunk * piece, piece),
            rows_at(3 * height + chunk * piece, piece),
            scatter.rows(chunk),
        )

    def inward(chunk):
        low, high, here = far_rows(chunk)

        def third(cols):
            both = jnp.concatenate([rows[low, :], rows[high, :]], axis=0)
            product = plain_product(both, win[:, cols])
            hidden[low, cols] = product[:piece]
            hidden[high, cols] = product[piece:]
            alive = swish(product).astype(BF16)
            active[low, cols] = alive[:piece]
            active[high, cols] = alive[piece:]

        gather.wait_last(chunk)
        tiles(inner, 512, third)

    def outward(chunk):
        low, high, here = far_rows(chunk)

        def fourth(cols):
            both = jnp.concatenate([active[low, :], active[high, :]], axis=0)
            product = plain_product(both, wout[:, cols])
            scatter.passing[here, cols] = product[:piece]
            scatter.outgoing[1, here, cols] = product[piece:].astype(BF16)

        tiles(width, 512, fourth)
        scatter.copy(1, chunk).start()
        scatter.relay(chunk)

    tiles(inner, 512, first)
    at("first")
    gather.pass_on(0)

    def take(chunk):
        @pl.when(chunk > 0)
        def _():
            gather.pass_on(chunk)

        inward(chunk)

    def both_ways(chunk):
        take(chunk)
        outward(chunk)

    if late:
        each_chunk(take)
        wait_out()
        each_chunk(outward)
        at("outward")
        tiles(width, 512, second)
        scatter.start(0)
    else:
        wait_out()
        tiles(width, 512, second)
        scatter.start(0)
        each_chunk(both_ways)


def ffn_backward(gather, scatter, win, wout, hidden, active, slope, wait_out, wait_in, products=None, at=lambda point: None):
    rows, height, piece = gather.rows, gather.height, gather.piece
    width, inner = win.shape
    pair = pl.ds(0, 2 * height)
    gather.wait_near()
    wait_out()

    def bend(product, before):
        logistic = jax.nn.sigmoid(before)
        return (
            (before * logistic).astype(BF16),
            (product * (logistic * (1.0 + before * (1.0 - logistic)))).astype(BF16),
        )

    def first(cols):
        alive, steep = bend(across_product(rows[pair, :], wout[cols, :]), hidden[pair, cols])
        if active is not None:
            active[pair, cols] = alive
        slope[pair, cols] = steep

    def second(cols):
        product = across_product(slope[pair, :], win[cols, :])
        scatter.own[:, cols] = product[:height]
        scatter.outgoing[0, :, cols] = product[height:].astype(BF16)

    def far_rows(chunk):
        return (
            rows_at(2 * height + chunk * piece, piece),
            rows_at(3 * height + chunk * piece, piece),
            scatter.rows(chunk),
        )

    def inward(chunk):
        low, high, here = far_rows(chunk)

        def third(cols):
            both = jnp.concatenate([rows[low, :], rows[high, :]], axis=0)
            before = jnp.concatenate([hidden[low, cols], hidden[high, cols]], axis=0)
            alive, steep = bend(across_product(both, wout[cols, :]), before)
            if active is not None:
                active[low, cols] = alive[:piece]
                active[high, cols] = alive[piece:]
            slope[low, cols] = steep[:piece]
            slope[high, cols] = steep[piece:]

        gather.wait_last(chunk)
        tiles(inner, 256, third)

    def outward(chunk):
        low, high, here = far_rows(chunk)

        def fourth(cols):
            both = jnp.concatenate([slope[low, :], slope[high, :]], axis=0)
            product = across_product(both, win[cols, :])
            scatter.passing[here, cols] = product[:piece]
            scatter.outgoing[1, here, cols] = product[piece:].astype(BF16)

        tiles(width, 512, fourth)
        scatter.copy(1, chunk).start()
        scatter.relay(chunk)

    tiles(inner, 256, first)
    at("first")
    gather.pass_on(0)

    def take(chunk):
        @pl.when(chunk > 0)
        def _():
            gather.pass_on(chunk)

        inward(chunk)

    def both_ways(chunk):
        take(chunk)
        outward(chunk)

    if products is not None:
        each_chunk(take)
        products()
        wait_in()
        each_chunk(outward)
        tiles(width, 512, second)
        scatter.start(0)
        at("second")
    else:
        wait_in()
        tiles(width, 512, second)
        scatter.start(0)
        each_chunk(both_ways)


def weight_products(result, left, right, tile=256):
    def one(cols):
        result[:, cols] = inner_product(left[...], right[:, cols]).astype(BF16)

    tiles(right.shape[1], tile, one)


OPEN_PLAN = dict(
    start=(11, 13, 12, 10, 21, 23, 22, 20,),
    gather=(-11, -13, -12, -21,),
    out=(-23, -22, 31, 32, 33, 30,),
    outward=(-31, -32,),
    total0=(-33, 41, 42, 43, 40,),
    near=(-41, -42, -43,),
)


def describe_frames(n, frames):
    seq = lax.axis_index(SEQ)
    lines, reach, total = frames // 128, MAXLEN // 128, n.segs.shape[0]
    base = seq * lines

    def line_of(ids, line, outside):
        safe = lax.min(lax.max(line, 0), total - 1)
        row = ids[pl.ds(safe, 1), :]
        return jnp.where((line >= 0) & (line < total), row, outside)

    def code(index, nothing):
        line = base - reach + index
        row = jnp.where(line_of(n.pads, line, 0) == 1, line_of(n.segs, line, -2), -1)
        n.codes[span(index * 128, 128), :] = jnp.transpose(jnp.broadcast_to(row, (128, 128)))
        return nothing

    lax.fori_loop(0, lines + 2 * reach, code, 0)
    lane = lax.broadcasted_iota(jnp.int32, (8, 128), 1)
    row_at = lax.broadcasted_iota(jnp.int32, (8, 128), 0)

    def marks(index, nothing):
        before, own, after = [
            jnp.broadcast_to(line_of(n.segs, base + index + shift, -1), (8, 128)) for shift in (-1, 0, 1)
        ]
        real = jnp.broadcast_to(n.pads[pl.ds(base + index, 1), :], (8, 128))
        table = jnp.where((row_at == KERNEL) & (real == 1), 1.0, 0.0)
        for tap in range(KERNEL):
            shift = tap - KERNEL // 2
            if shift < 0:
                moved = jnp.where(lane < -shift, pltpu.roll(before, -shift, 1), pltpu.roll(own, -shift, 1))
            elif shift > 0:
                moved = jnp.where(
                    lane >= 128 - shift, pltpu.roll(after, 128 - shift, 1), pltpu.roll(own, 128 - shift, 1)
                )
            else:
                moved = own
            table = jnp.where((row_at == tap) & (moved == own), 1.0, table)
        table = jnp.concatenate([table, jnp.zeros((120, 128), F32)], axis=0)
        n.context[span(index * 128, 128), :] = jnp.transpose(table)
        return nothing

    lax.fori_loop(0, lines, marks, 0)
    everyone = n.segs[...]
    offset = (MAXLEN - seq * frames).astype(F32)
    edge = lax.broadcasted_iota(jnp.int32, (1, 128), 1)
    per = QUERY_BLOCK // 128
    for step in range(frames // QUERY_BLOCK):
        low = n.segs[pl.ds(base + step * per, 1), :][:, 0:1]
        high = n.segs[pl.ds(base + step * per + per - 1, 1), :][:, 127:128]
        below = jnp.sum(jnp.where(everyone < low, 1.0, 0.0), keepdims=True)
        upto = jnp.sum(jnp.where(everyone <= high, 1.0, 0.0), keepdims=True)
        first = jnp.floor((below + offset) * (1.0 / KEY_BLOCK))
        last = jnp.floor((upto + (offset + (KEY_BLOCK - 1))) * (1.0 / KEY_BLOCK))
        n.bounds[step : step + 1, :] = jnp.where(edge == 0, first, last).astype(jnp.int32)


def open_kernel(n):
    height, width = n.values.shape
    frames = 4 * height
    local = n.queries.shape[1]
    seq, count = lax.axis_index(SEQ), lax.axis_size(SEQ)
    first_in = Collect(n.shard_in, n.win, **n.c_in)
    first_out = Collect(n.shard_out, n.wout, **n.c_out)
    project = Collect(n.shard_project, n.wproject, **n.c_project)
    attend_out = Collect(n.shard_attend, n.full_attend, **n.c_attend)
    plan = Plan(OPEN_PLAN, (first_in, first_out, project, attend_out))
    gather = Gather(n.rows, **n.g1)
    scatter = Scatter(**n.s1)
    gather_two = Gather(n.rows_two, **n.g2)
    ready = greet(tp_peers() + seq_peers())
    n.rows[pl.ds(0, gather.piece), :] = norm_rows(
        n.values[pl.ds(0, gather.piece), :].astype(F32), n.gains[0:1, :]
    ).astype(BF16)
    for part in range(3):
        n.shard_project[:, pl.ds(part * local, local)] = n.project_parts[part]
    ready()
    plan.at("start")
    for chunk in range(CHUNKS):
        here = scatter.rows(chunk)
        if chunk > 0:
            n.rows[here, :] = norm_rows(n.values[here, :].astype(F32), n.gains[0:1, :]).astype(BF16)
        gather.start(chunk)
    describe_frames(n, frames)
    n.put("codes", "context")
    plan.at("gather")
    keeps = [
        pltpu.make_async_copy(n.win, n.full_in, n.keep.at[0]),
        pltpu.make_async_copy(n.wout, n.full_out, n.keep.at[1]),
        pltpu.make_async_copy(n.wproject, n.full_project, n.keep.at[2]),
    ]

    def wait_in():
        first_in.end()
        keeps[0].start()

    def wait_out():
        plan.at("out")
        first_out.end()
        keeps[1].start()

    ffn_forward(gather, scatter, n.win, n.wout, n.hidden, n.active, wait_in, wait_out, late=True, at=plan.at)
    for chunk in range(CHUNKS):
        here = scatter.rows(chunk)
        n.first[here, :] = n.values[here, :].astype(F32) + 0.5 * scatter.total(chunk)
        n.rows_two[here, :] = norm_rows(n.first[here, :], n.gains[1:2, :]).astype(BF16)
        gather_two.start(chunk)
        plan.at(f"total{chunk}")
    n.put("rows", "hidden", "first")
    project.end()
    keeps[2].start()
    gather_two.wait_near()

    def send_block(slot):
        place = owner(slot)
        source = n.all_own.at[span(place * height, height), pl.ds(local, 2 * local)]
        upper = lax.div(place, 2)

        def piece(kind):
            if kind == 0:
                peer, row = lax.rem(seq + 1, count), MAXLEN - frames + place * height
            elif kind == 1:
                peer, row = lax.rem(seq + count - 1, count), MAXLEN + frames + place * height
            else:
                peer = lax.rem(seq + count - 2 + 4 * upper, count)
                row = MAXLEN + place * height + 2 * frames * (1 - 2 * upper)
            target = n.window.at[span(row, height), :]
            return remote(source, target, n.halo_send.at[kind, slot], n.halo_receive.at[kind, slot], {SEQ: peer})

        return [piece(kind) for kind in range(3)]

    def there(kind, slot, sending):
        upper = lax.div(owner(slot), 2)
        if kind == 2:
            shift = 4 * upper - 2
        else:
            shift = 1 - 2 * kind
        target = seq + shift if sending else seq - shift
        return (target >= 0) & (target < count)

    def project_rows(slots, low):
        def part(cols):
            product = plain_product(n.rows_two[low, :], n.wproject[:, cols]).astype(BF16)
            for index, slot in enumerate(slots):
                n.all_own[span(owner(slot) * height, height), cols] = product[index * height : (index + 1) * height]

        tiles(3 * local, local, part)
        for slot in slots:
            for kind, copy in enumerate(send_block(slot)):

                @pl.when(there(kind, slot, True))
                def _():
                    copy.start()

    project_rows((0, 1), pl.ds(0, 2 * height))
    for chunk in range(CHUNKS):
        gather_two.pass_on(chunk)
    plan.at("near")
    for chunk in range(CHUNKS):
        gather_two.wait_last(chunk)
    n.put("rows_two")
    project_rows((2, 3), pl.ds(2 * height, 2 * height))
    own = pltpu.make_async_copy(
        n.all_own.at[:, pl.ds(local, 2 * local)], n.window.at[pl.ds(MAXLEN, frames), :], n.keep.at[3]
    )
    own.start()
    asked = pltpu.make_async_copy(n.all_own.at[:, pl.ds(0, local)], n.queries, n.keep.at[4])
    asked.start()
    for slot in range(4):
        for kind, copy in enumerate(send_block(slot)):

            @pl.when(there(kind, slot, False))
            def _():
                copy.wait_recv()

            @pl.when(there(kind, slot, True))
            def _():
                copy.wait_send()

    attend_out.end()
    for keep in keeps:
        keep.wait()
    own.wait()
    asked.wait()
    plan.finish()
    for item in [gather, scatter, gather_two]:
        item.finish()


def run_open(values, gains, shards, segs, pads):
    height, width = values.shape
    frames = 4 * height
    count = lax.axis_size(SEQ)
    inner, local = shards.ffn1_in.shape[1], shards.attend.shape[0] * count
    fulls = dict(
        full_in=shards.ffn1_in, full_out=shards.ffn1_out,
        full_attend=shards.attend,
    )
    return run_kernel(
        open_kernel,
        0,
        dict(
            values=(values, True), gains=(gains, True), shard_in=(shards.ffn1_in, True),
            shard_out=(shards.ffn1_out, True), project_parts=(shards.project, True),
            segs=(segs, True), pads=(pads, True),
            shard_attend=(shards.attend, True),
        ),
        dict(
            first=((height, width), F32, KEEP),
            rows=((frames, width), BF16, KEEP),
            hidden=((frames, inner), F32, KEEP),
            rows_two=((frames, width), BF16, KEEP),
            queries=((frames, local), BF16, False),
            window=((frames + 2 * MAXLEN, 2 * local), BF16, False),
            codes=((frames + 2 * MAXLEN, 128), jnp.int32, KEEP),
            context=((frames, 128), F32, KEEP),
            bounds=((8, 128), jnp.int32, True),
            full_project=((width, 3 * local), BF16, False),
            **{name: ((item.shape[0] * count, item.shape[1]), BF16, False) for name, item in fulls.items()},
        ),
        dict(
            win=pltpu.VMEM((width, inner), BF16),
            wout=pltpu.VMEM((inner, width), BF16),
            wproject=pltpu.VMEM((width, 3 * local), BF16),
            shard_project=pltpu.VMEM((width // count, 3 * local), BF16),
            active=pltpu.VMEM((frames, inner), BF16),
            all_own=pltpu.VMEM((frames, 3 * local), BF16),
            c_in=collect_scratch(), c_out=collect_scratch(), c_project=collect_scratch(),
            c_attend=collect_scratch(),
            g1=gather_scratch(), s1=scatter_scratch(height, width), g2=gather_scratch(),
            halo_send=pltpu.SemaphoreType.DMA((3, 4)), halo_receive=pltpu.SemaphoreType.DMA((3, 4)),
            keep=pltpu.SemaphoreType.DMA((5,)),
        ),
    )


def slot_rows(slots, height):
    return pl.ds(slots[0] * height, 2 * height)


def in_order(swap):
    for place in range(swap.count):
        yield swap.blocks[lax.rem(swap.me + swap.count - place, swap.count)]


def middle_kernel(n):
    height, width = n.first.shape
    frames = 4 * height
    local = n.mixed.shape[1]
    block = 128
    none = jnp.zeros((1, local), F32)
    pair_weight, conv_weight = Collect(n.shard_pair, n.wpair, **n.c_pair), Collect(n.shard_conv, n.wconv, **n.c_conv)
    in_weight, out_weight = Collect(n.shard_in, n.win, **n.c_in), Collect(n.shard_out, n.wout, **n.c_out)
    out_sum, in_sum = Settle(n.grad_out, n.sum_out, **n.t_out), Settle(n.grad_in, n.sum_in, **n.t_in)
    plan = Plan(
        MIDDLE_PLAN,
        (pair_weight, conv_weight, in_weight, out_weight, out_sum, in_sum),
    )
    scatter = Scatter(**n.s1)
    gathers = [
        Gather(n.rows_conv, **n.g1), Gather(n.rows, **n.g2), Gather(n.grads, **n.g3),
        Gather(n.grads_conv, **n.g4), Gather(n.grads, **n.g5),
    ]
    edges, edges_back = Edges(n.gated, **n.edge), Edges(n.back, **n.edge_back)
    swap, swap_back = Swap(**n.swap), Swap(**n.swap_back)
    chunks = [scatter.rows(chunk) for chunk in range(CHUNKS)]
    ready = greet(tp_peers() + seq_peers())
    for slot in range(4):
        n.mixed_low[pl.ds(slot * height, height), :] = n.mixed[span(owner(slot) * height, height), :].astype(BF16)
    for part in range(2):
        n.shard_pair[:, pl.ds(part * local, local)] = n.pair_parts[:, part, :]
    ready()
    plan.at("start")
    scatter.spread(
        lambda slots, cols: plain_product(n.mixed_low[slot_rows(slots, height), :], n.wattend[:, cols]), width
    )
    gather = gathers[0]
    plan.at("spread")
    n.wait("first")
    for chunk, here in enumerate(chunks):
        n.second[here, :] = n.first[here, :] + scatter.total(chunk)
        n.rows_conv[here, :] = norm_rows(n.second[here, :], n.gains[2:3, :]).astype(BF16)
        gather.start(chunk)
        plan.at(f"second{chunk}")
    scatter.finish()
    gather.wait_near()
    pair_weight.end()
    n.wait("context")

    def pair_rows(slots):
        product = plain_product(n.rows_conv[slot_rows(slots, height), :], n.wpair[...])
        for index, slot in enumerate(slots):
            rows = product[index * height : (index + 1) * height]
            place = owner(slot) * height
            n.paired[span(place, height), :] = rows
            real = n.context[span(place, height), KERNEL : KERNEL + 1]
            gated = rows[:, :local] * jax.nn.sigmoid(rows[:, local:]) * real
            n.gated[pl.ds(pl.multiple_of(EDGE + place, EDGE), height), :] = gated.astype(BF16).astype(F32)

    pair_rows((0, 1))
    for chunk in range(CHUNKS):
        gather.pass_on(chunk)
    plan.at("passed")
    for chunk in range(CHUNKS):
        gather.wait_last(chunk)
    pair_rows((2, 3))
    edges.start()
    plan.at("edged")

    def convolve(index, carried):
        total, real_count = carried
        around = n.gated[pl.ds(pl.multiple_of(index * block, block), block + 2 * EDGE), :]
        marks = n.context[span(index * block, block), :]
        conv = jnp.zeros((block, local), F32)
        for tap in range(KERNEL):
            begin = EDGE - KERNEL // 2 + tap
            conv = conv + n.depth[tap : tap + 1, :] * around[begin : begin + block] * marks[:, tap : tap + 1]
        n.normal[span(index * block, block), :] = conv
        real = marks[:, KERNEL : KERNEL + 1]
        return (
            total + jnp.sum(real * conv, axis=0, keepdims=True),
            real_count + jnp.sum(jnp.broadcast_to(real, conv.shape), axis=0, keepdims=True),
        )

    last = frames // block - 1
    carried = lax.fori_loop(1, last, convolve, (none, none))
    edges.wait()
    plan.at("edges")
    total, real_count = convolve(last, convolve(0, carried))
    middle = total / jnp.maximum(real_count, 1.0)

    def deviate(index, carried):
        conv = n.normal[span(index * block, block), :]
        real = n.context[span(index * block, block), KERNEL : KERNEL + 1]
        away = conv - middle
        return carried + jnp.sum(real * away * away, axis=0, keepdims=True)

    squares = lax.fori_loop(0, frames // block, deviate, none)
    swap.blocks[0, 0:1, :] = total
    swap.blocks[0, 1:2, :] = squares
    swap.blocks[0, 2:3, :] = real_count
    swap.start()
    swap.wait()
    plan.at("swapped")
    total_all, real_all = none, none
    for item in in_order(swap):
        total_all = total_all + item[0:1]
        real_all = real_all + item[2:3]
    centre = total_all / real_all
    squares_all = none
    for item in in_order(swap):
        away = item[0:1] / jnp.maximum(item[2:3], 1.0) - centre
        squares_all = squares_all + item[1:2] + item[2:3] * away * away
    inverse = lax.rsqrt(squares_all / real_all + EPSILON)
    for slot in range(4):
        place = span(owner(slot) * height, height)
        normal = (n.normal[place, :] - centre) * inverse
        n.normal[place, :] = normal
        n.alive[pl.ds(slot * height, height), :] = swish(normal * n.bn_gain[...] + n.bn_bias[...]).astype(BF16)
    conv_weight.end()
    scatter.spread(
        lambda slots, cols: plain_product(n.alive[slot_rows(slots, height), :], n.wconv[:, cols]), width
    )
    plan.at("alive")
    gather = gathers[1]
    for chunk, here in enumerate(chunks):
        n.third[here, :] = n.second[here, :] + scatter.total(chunk)
        n.rows[here, :] = norm_rows(n.third[here, :], n.gains[3:4, :]).astype(BF16)
        gather.start(chunk)
        plan.at(f"third{chunk}")
    scatter.finish()
    ffn_forward(gather, scatter, n.win, n.wout, n.hidden, n.active, in_weight.end, out_weight.end, True, plan.at)
    gather = gathers[2]
    n.wait("out_grad")
    gain_four = jnp.zeros((1, width), F32)
    for chunk, here in enumerate(chunks):
        fourth = n.third[here, :] + 0.5 * scatter.total(chunk)
        n.output[here, :] = norm_rows(fourth, n.gains[4:5, :]).astype(BF16)
        grad, gain = norm_back(fourth, n.gains[4:5, :], n.out_grad[here, :].astype(F32))
        gain_four = gain_four + gain
        n.grad_row[here, :] = grad
        n.grads[here, :] = (0.5 * grad).astype(BF16)
        gather.start(chunk)
    scatter.finish()
    n.put("output")

    def nothing():
        return None

    ffn_backward(gather, scatter, n.win, n.wout, n.hidden, None, n.slope, nothing, nothing)
    weight_products(n.grad_out, n.active, n.grads)
    plan.at("grad_out")
    weight_products(n.grad_in, n.rows, n.slope)
    plan.at("grad_in")
    gathers[2].finish()
    gather = gathers[3]
    gain_three = jnp.zeros((1, width), F32)
    for chunk, here in enumerate(chunks):
        grad, gain = norm_back(n.third[here, :], n.gains[3:4, :], scatter.total(chunk))
        gain_three = gain_three + gain
        n.grad_row[here, :] += grad
        n.grads_conv[here, :] = n.grad_row[here, :].astype(BF16)
        gather.start(chunk)
    scatter.finish()
    plan.at("back_start")
    gather.wait_near()
    sums = [none, none]

    def batch_rows(slots):
        product = across_product(n.grads_conv[slot_rows(slots, height), :], n.wconv[...])
        for index, slot in enumerate(slots):
            place = span(owner(slot) * height, height)
            normal = n.normal[place, :]
            batch = normal * n.bn_gain[...] + n.bn_bias[...]
            logistic = jax.nn.sigmoid(batch)
            rows = product[index * height : (index + 1) * height]
            grad = rows * (logistic * (1.0 + batch * (1.0 - logistic)))
            n.grad_batch[place, :] = grad
            sums[0] = sums[0] + jnp.sum(grad * normal, axis=0, keepdims=True)
            sums[1] = sums[1] + jnp.sum(grad, axis=0, keepdims=True)

    batch_rows((0, 1))
    plan.at("back_near")
    for chunk in range(CHUNKS):
        gather.pass_on(chunk)
    plan.at("back_passed")
    for chunk in range(CHUNKS):
        gather.wait_last(chunk)
    batch_rows((2, 3))
    swap_back.blocks[0, 0:1, :] = sums[0]
    swap_back.blocks[0, 1:2, :] = sums[1]
    swap_back.start()
    weight_products(n.grad_conv, n.alive, n.grads_conv)
    n.put("grad_conv")
    plan.at("grad_conv")
    swap_back.wait()
    grad_gain, grad_bias = none, none
    for item in in_order(swap_back):
        grad_gain = grad_gain + item[0:1]
        grad_bias = grad_bias + item[1:2]
    n.sum_gain[...] = grad_gain
    n.sum_bias[...] = grad_bias
    gain = n.bn_gain[...]

    def deconvolve(index, nothing):
        here = span(index * block, block)
        real = n.context[here, KERNEL : KERNEL + 1]
        drift = real * (gain * grad_bias + n.normal[here, :] * gain * grad_gain) / real_all
        n.back[pl.ds(pl.multiple_of(EDGE + index * block, EDGE), block), :] = inverse * (
            n.grad_batch[here, :] * gain - drift
        )
        return nothing

    lax.fori_loop(0, frames // block, deconvolve, 0)
    edges_back.start()
    plan.at("edges_back")
    me = lax.axis_index(TP)

    def part(index, carried):
        here = span(index * block, block)
        around = pl.ds(pl.multiple_of(index * block, block), block + 2 * EDGE)
        back, gated = n.back[around, :], n.gated[around, :]
        marks = n.context[here, :]
        own = back[EDGE : EDGE + block]
        grad = jnp.zeros((block, local), F32)
        result = []
        for tap in range(KERNEL):
            first = EDGE - KERNEL // 2 + tap
            mark = marks[:, tap : tap + 1]
            result.append(
                carried[tap] + jnp.sum(gated[first : first + block] * mark * own, axis=0, keepdims=True)
            )
            mirror = KERNEL - 1 - tap
            grad = grad + n.depth[mirror : mirror + 1, :] * back[first : first + block] * mark
        grad = grad * marks[:, KERNEL : KERNEL + 1]
        both = n.paired[here, :]
        logistic = jax.nn.sigmoid(both[:, local:])
        place = lax.div(index * block, height)
        slot = lax.rem(place + me, 2) + 2 * lax.rem(lax.div(place, 2) + lax.div(me, 2), 2)
        rows = span(slot * height + lax.rem(index * block, height), block)
        n.grad_paired[rows, pl.ds(0, local)] = (grad * logistic).astype(BF16)
        n.grad_paired[rows, pl.ds(local, local)] = (
            grad * both[:, :local] * logistic * (1.0 - logistic)
        ).astype(BF16)
        return tuple(result)

    taps = lax.fori_loop(1, last, part, (none,) * KERNEL)
    edges_back.wait()
    plan.at("parts")
    taps = part(last, part(0, taps))
    for tap in range(KERNEL):
        n.depth_sums[tap : tap + 1, :] = taps[tap]
    plan.at("taps")
    scatter.spread(
        lambda slots, cols: across_product(n.grad_paired[slot_rows(slots, height), :], n.wpair[cols, :]), width
    )
    plan.at("back_spread")
    weight_products(n.grad_pair, n.rows_conv, n.grad_paired)
    n.put("grad_pair")
    plan.at("grad_pair")
    gather = gathers[4]
    gain_two = jnp.zeros((1, width), F32)
    for chunk, here in enumerate(chunks):
        grad, gain = norm_back(n.second[here, :], n.gains[2:3, :], scatter.total(chunk))
        gain_two = gain_two + gain
        n.grad_second[here, :] = n.grad_row[here, :] + grad
        n.grads[here, :] = n.grad_second[here, :].astype(BF16)
        gather.start(chunk)
        plan.at(f"back_second{chunk}")
    scatter.finish()
    n.put("grad_second")
    n.gain_sums[0:1, :] = gain_two
    n.gain_sums[1:2, :] = gain_three
    n.gain_sums[2:3, :] = gain_four
    gather.wait_near()

    def mixed_rows(slots):
        product = across_product(n.grads[slot_rows(slots, height), :], n.wattend[...]).astype(BF16)
        for index, slot in enumerate(slots):
            n.grad_mixed[span(owner(slot) * height, height), :] = product[index * height : (index + 1) * height]

    mixed_rows((0, 1))
    for chunk in range(CHUNKS):
        gather.pass_on(chunk)
    plan.at("last_passed")
    out_sum.end()
    in_sum.end()
    n.put("sum_out", "sum_in")
    for chunk in range(CHUNKS):
        gather.wait_last(chunk)
    mixed_rows((2, 3))
    n.put("grad_mixed")
    weight_products(n.grad_attend, n.mixed_low, n.grads)
    plan.finish()
    for item in gathers[:2] + gathers[3:] + [edges, edges_back, swap, swap_back]:
        item.finish()


MIDDLE_PLAN = dict(
    start=(11, 13, 12, 10, 21, 23, 22, 20,),
    spread=(-11, -13,),
    second0=(-12,),
    second1=(-21, -23, -22, 31, 30, 33, ),
    passed=(-31, ),
    edges=(-33, ),
    swapped=(-32, 41, 40, 43, 42, ),
    alive=(-41, ),
    third0=(-43, ),
    first=(-42, ),
    grad_out=(51, 53, 52, 50, ),
    back_start=(-51, ),
    back_near=(-53, ),
    back_passed=(-52, ),
    edges_back=(-61, 62, 60, ),
    parts=(-63, ),
    back_spread=(-62, ),
    edged=(32, ),
    grad_in=(61, 63, ),
)


def run_middle(mixed, opened, gains, depth, bn_gain, bn_bias, shards, out_grad):
    height, width = opened.first.shape
    frames, local = mixed.shape
    count = lax.axis_size(SEQ)
    inner = shards.ffn2_in.shape[1]
    settled = dict(out=(inner, width), **{"in": (width, inner)})
    weights = ("out", "in", "conv", "pair")
    return run_kernel(
        middle_kernel,
        1,
        dict(
            mixed=(mixed, True), first=(opened.first, LOAD), gains=(gains, True), wattend=(opened.full_attend, True),
            context=(opened.context, LOAD), depth=(depth, True), bn_gain=(bn_gain, True), bn_bias=(bn_bias, True),
            out_grad=(out_grad, LOAD), pair_parts=(shards.pair, True), shard_conv=(shards.conv, True),
            shard_in=(shards.ffn2_in, True), shard_out=(shards.ffn2_out, True),
        ),
        dict(
            output=((height, width), BF16, KEEP),
            grad_second=((height, width), F32, KEEP),
            grad_mixed=((frames, local), BF16, KEEP),
            grad_attend=((local, width), BF16, True),
            grad_conv=((local, width), BF16, KEEP),
            grad_pair=((width, 2 * local), BF16, KEEP),
            depth_sums=((8, local), F32, True),
            sum_gain=((1, local), F32, True),
            sum_bias=((1, local), F32, True),
            gain_sums=((8, width), F32, True),
            **{f"sum_{name}": ((tall // count, wide), F32, KEEP) for name, (tall, wide) in settled.items()},
        ),
        dict(
            shard_pair=pltpu.VMEM((width // count, 2 * local), BF16),
            wpair=pltpu.VMEM((width, 2 * local), BF16), wconv=pltpu.VMEM((local, width), BF16),
            win=pltpu.VMEM((width, inner), BF16), wout=pltpu.VMEM((inner, width), BF16),
            second=pltpu.VMEM((height, width), F32), third=pltpu.VMEM((height, width), F32),
            grad_row=pltpu.VMEM((height, width), F32),
            rows_conv=pltpu.VMEM((frames, width), BF16), rows=pltpu.VMEM((frames, width), BF16),
            grads=pltpu.VMEM((frames, width), BF16), grads_conv=pltpu.VMEM((frames, width), BF16),
            hidden=pltpu.VMEM((frames, inner), F32), active=pltpu.VMEM((frames, inner), BF16),
            slope=pltpu.VMEM((frames, inner), BF16),
            mixed_low=pltpu.VMEM((frames, local), BF16), paired=pltpu.VMEM((frames, 2 * local), F32),
            gated=pltpu.VMEM((frames + 2 * EDGE, local), F32), normal=pltpu.VMEM((frames, local), F32),
            alive=pltpu.VMEM((frames, local), BF16), grad_batch=pltpu.VMEM((frames, local), F32),
            back=pltpu.VMEM((frames + 2 * EDGE, local), F32), grad_paired=pltpu.VMEM((frames, 2 * local), BF16),
            **{f"grad_{name}": pltpu.VMEM((tall, wide), BF16) for name, (tall, wide) in settled.items()},
            **{f"t_{name}": settle_scratch(tall // count, wide) for name, (tall, wide) in settled.items()},
            **{f"c_{name}": collect_scratch() for name in weights},
            **{f"g{place}": gather_scratch() for place in range(1, 6)},
            s1=scatter_scratch(height, width),
            edge=edges_scratch(), edge_back=edges_scratch(), swap=swap_scratch(8, local), swap_back=swap_scratch(8, local),
        ),
    )


def close_kernel(n):
    height, width = n.grad_second.shape
    frames = 4 * height
    local = n.grad_query.shape[1]
    seq, count = lax.axis_index(SEQ), lax.axis_size(SEQ)
    half = MAXLEN - frames
    loads = [
        pltpu.make_async_copy(n.full_out, n.wout, n.load.at[0]),
        pltpu.make_async_copy(n.full_hidden, n.hidden, n.load.at[1]),
        pltpu.make_async_copy(n.full_in, n.win, n.load.at[2]),
        pltpu.make_async_copy(n.grad_key.at[pl.ds(MAXLEN, frames), :], n.own_back.at[0], n.load.at[3]),
        pltpu.make_async_copy(n.grad_value.at[pl.ds(MAXLEN, frames), :], n.own_back.at[1], n.load.at[4]),
    ]
    for load in loads:
        load.start()
    attend_sum = Settle(n.grad_attend, n.sum_attend, **n.t_attend)
    conv_sum = Settle(n.grad_conv, n.sum_conv, **n.t_conv)
    pair_sum = Settle(n.grad_pair, n.sum_pair, **n.t_pair)
    project = Settle(n.grad_project, n.sum_project, **n.t_project)
    last = [Settle(n.grad_out, n.sum_out, **n.t_out), Settle(n.grad_in, n.sum_in, **n.t_in)]
    scatter, gather, scatter_two = Scatter(**n.s1), Gather(n.grads, **n.g1), Scatter(**n.s2)
    swap = Swap(**n.swap)
    plan = Plan(
        CLOSE_PLAN, (attend_sum, conv_sum, pair_sum, project, last[0], last[1])
    )
    ready = greet(tp_peers() + seq_peers())
    shifts = (1, -1, 2, -2)
    sources = ((MAXLEN + frames, frames), (MAXLEN - frames, frames), (MAXLEN + 2 * frames, half), (0, half))
    targets = ((0, 0), (1, 0), (2, 0), (2, frames - half))

    def back(kind, which):
        begin, size = sources[kind]
        place, row = targets[kind]
        source = (n.grad_key, n.grad_value)[which].at[pl.ds(begin, size), :]
        target = n.others_back.at[which, place, pl.ds(row, size), :]
        peer = {SEQ: lax.rem(seq + shifts[kind] + count, count)}
        return remote(source, target, n.back_send.at[which, kind], n.back_receive.at[which, kind], peer)

    def there(kind, sending):
        other = seq + shifts[kind] if sending else seq - shifts[kind]
        return (other >= 0) & (other < count)

    for kind in range(4):
        place, row = targets[kind]

        @pl.when(jnp.logical_not(there(kind, False)))
        def _():
            for which in range(2):
                size = sources[kind][1]
                n.others_back[which, place, pl.ds(row, size), :] = jnp.zeros((size, local), BF16)

    ready()
    for kind in range(4):

        @pl.when(there(kind, True))
        def _():
            for which in range(2):
                back(kind, which).start()

    n.wait("grad_query")
    for slot in range(4):
        n.grad_rows[pl.ds(slot * height, height), pl.ds(0, local)] = n.grad_query[span(owner(slot) * height, height), :]
    for kind in range(4):

        @pl.when(there(kind, False))
        def _():
            for which in range(2):
                back(kind, which).wait_recv()

    plan.at("returned")
    loads[3].wait()
    loads[4].wait()
    for slot in range(4):
        place = span(owner(slot) * height, height)
        for which in range(2):
            total = n.own_back[which, place, :].astype(F32)
            for other in range(3):
                total = total + n.others_back[which, other, place, :].astype(F32)
            n.grad_rows[pl.ds(slot * height, height), pl.ds((which + 1) * local, local)] = total.astype(BF16)
    n.wait("wproject")
    scatter.spread(
        lambda slots, cols: across_product(n.grad_rows[slot_rows(slots, height), :], n.wproject[cols, :]), width
    )
    plan.at("spread")
    n.wait("rows_two")
    weight_products(n.grad_project, n.rows_two, n.grad_rows)
    plan.at("grad_project")
    n.wait("first", "grad_second")
    gain_one = jnp.zeros((1, width), F32)
    for chunk in range(CHUNKS):
        here = scatter.rows(chunk)
        grad, gain = norm_back(n.first[here, :], n.gains[1:2, :], scatter.total(chunk))
        gain_one = gain_one + gain
        n.grad_first[here, :] = n.grad_second[here, :] + grad
        n.grads[here, :] = (0.5 * n.grad_first[here, :]).astype(BF16)
        gather.start(chunk)
        plan.at(f"first{chunk}")

    def wait_out():
        loads[0].wait()
        loads[1].wait()

    def products():
        weight_products(n.grad_out, n.active, n.grads)
        plan.at("grad_out")
        n.wait("rows")
        weight_products(n.grad_in, n.rows, n.slope)
        plan.at("grad_in")

    ffn_backward(
        gather, scatter_two, n.win, n.wout, n.hidden, n.active, n.slope, wait_out, loads[2].wait, products, plan.at
    )
    n.wait("values")
    gain_zero = jnp.zeros((1, width), F32)
    for chunk in range(CHUNKS):
        here = scatter.rows(chunk)
        grad, gain = norm_back(n.values[here, :].astype(F32), n.gains[0:1, :], scatter_two.total(chunk))
        gain_zero = gain_zero + gain
        n.input_grad[here, :] = n.grad_first[here, :] + grad
        plan.at(f"zero{chunk}")
    n.small[0, 0:1, :] = gain_zero
    n.small[0, 1:2, :] = gain_one
    n.small[0, 2:5, :] = n.gain_late[0:3, :]
    n.small[0, 5:8, :] = jnp.zeros((3, width), F32)
    near, far = tp_peers()
    hop = remote(n.small.at[0], n.small.at[1], n.small_sem.at[0], n.small_sem.at[1], near)
    hop.start()
    hop.wait_recv()
    n.small[2] = n.small[0] + n.small[1]
    hop_two = remote(n.small.at[2], n.small.at[3], n.small_sem.at[2], n.small_sem.at[3], far)
    hop_two.start()
    hop_two.wait_recv()
    swap.blocks[0, :, pl.ds(0, width)] = n.small[2] + n.small[3]
    swap.blocks[0, :, pl.ds(width, local)] = n.depth_sums[...]
    swap.start()
    plan.at("small")
    n.put("input_grad")
    attend_sum.end()
    conv_sum.end()
    pair_sum.end()
    project.end()
    n.put("sum_attend", "sum_conv", "sum_pair", "sum_project")
    plan.at("ended")
    swap.wait()
    total = jnp.zeros((8, width + local), F32)
    for item in in_order(swap):
        total = total + item
    n.gain_total[...] = total[:5, :width]
    n.depth_total[...] = total[:KERNEL, width:]
    for name, task in zip(("sum_out", "sum_in"), last):
        task.end()
        n.put(name)
    for kind in range(4):

        @pl.when(there(kind, True))
        def _():
            for which in range(2):
                back(kind, which).wait_send()

    hop.wait_send()
    hop_two.wait_send()
    plan.finish()
    for item in [scatter, gather, scatter_two, swap]:
        item.finish()


CLOSE_PLAN = dict(
    returned=(31, 33, 32, 30, 21, 23, 22, 20, 11, 13, 12, 10,),
    spread=(-31,),
    grad_project=(-33, 41, 43, 42, 40,),
    first0=(-32,),
    first1=(-21, -23, -22,),
    first=(-11, -13, -12,),
    grad_out=(-41, -43, 51, 53, 52, 50,),
    grad_in=(-42, 61, 63, 62, 60,),
    second=(-51, -53,),
    zero0=(-52,),
    small=(-61,),
    ended=(-63, -62,),
)


def run_close(values, gains, opened, middle, grad_query, grad_key, grad_value):
    height, width = values.shape
    frames, local = grad_query.shape
    count = lax.axis_size(SEQ)
    inner = opened.full_in.shape[1]
    settled = dict(
        pair=(width, 2 * local), conv=(local, width), attend=(local, width),
        project=(width, 3 * local), out=(inner, width), **{"in": (width, inner)},
    )
    return run_kernel(
        close_kernel,
        4,
        dict(
            values=(values, LOAD), gains=(gains, True), first=(opened.first, LOAD), rows=(opened.rows, LOAD),
            rows_two=(opened.rows_two, LOAD), full_hidden=(opened.hidden, False),
            full_in=(opened.full_in, False), full_out=(opened.full_out, False),
            wproject=(opened.full_project, LOAD), grad_second=(middle.grad_second, LOAD), grad_query=(grad_query, LOAD),
            grad_key=(grad_key, False), grad_value=(grad_value, False), grad_attend=(middle.grad_attend, False),
            grad_conv=(middle.grad_conv, False), grad_pair=(middle.grad_pair, False),
            depth_sums=(middle.depth_sums, True), gain_late=(middle.gain_sums, True),
        ),
        dict(
            input_grad=((height, width), F32, KEEP),
            gain_total=((5, width), F32, True),
            depth_total=((KERNEL, local), F32, True),
            **{f"sum_{name}": ((tall // count, wide), F32, KEEP) for name, (tall, wide) in settled.items()},
        ),
        dict(
            win=pltpu.VMEM((width, inner), BF16), wout=pltpu.VMEM((inner, width), BF16),
            hidden=pltpu.VMEM((frames, inner), F32), active=pltpu.VMEM((frames, inner), BF16),
            slope=pltpu.VMEM((frames, inner), BF16), grads=pltpu.VMEM((frames, width), BF16),
            grad_first=pltpu.VMEM((height, width), F32),
            own_back=pltpu.VMEM((2, frames, local), BF16), others_back=pltpu.VMEM((2, 3, frames, local), BF16),
            grad_rows=pltpu.VMEM((frames, 3 * local), BF16),
            grad_project=pltpu.VMEM((width, 3 * local), BF16),
            grad_in=pltpu.VMEM((width, inner), BF16), grad_out=pltpu.VMEM((inner, width), BF16),
            **{f"t_{name}": settle_scratch(tall // count, wide, name in ("attend", "conv", "pair")) for name, (tall, wide) in settled.items()},
            g1=gather_scratch(), s1=scatter_scratch(height, width), s2=scatter_scratch(height, width),
            swap=swap_scratch(8, width + local),
            small=pltpu.VMEM((4, 8, width), F32), small_sem=pltpu.SemaphoreType.DMA((4,)),
            back_send=pltpu.SemaphoreType.DMA((2, 4)), back_receive=pltpu.SemaphoreType.DMA((2, 4)),
            load=pltpu.SemaphoreType.DMA((5,)),
        ),
    )


def hand_kernel(names, n):
    taken = [pltpu.make_async_copy(n.source[name], n.buffer[name], n.sems.at[0, place]) for place, name in enumerate(names)]
    given = []
    for copy in taken:
        copy.start()
    for place, name in enumerate(names):
        taken[place].wait()
        buffer, target = n.buffer[name], n.target[name]
        if name == "project":
            wide = target.shape[2]
            copies = [
                pltpu.make_async_copy(buffer.at[:, pl.ds(part * wide, wide)], target.at[part], n.sems.at[1 + part, place])
                for part in range(3)
            ]
        elif name == "pair":
            wide = target.shape[2]
            for part in range(2):
                n.apart[:, part, :] = buffer[:, pl.ds(part * wide, wide)]
            copies = [pltpu.make_async_copy(n.apart, target, n.sems.at[1, place])]
        else:
            copies = [pltpu.make_async_copy(buffer, target, n.sems.at[1, place])]
        for copy in copies:
            copy.start()
        given += copies
    for copy in given:
        copy.wait()


def hand_over(arrays):
    names = list(arrays)

    def shape_of(name):
        tall, wide = arrays[name].shape
        return {"project": (3, tall, wide // 3), "pair": (tall, 2, wide // 2)}.get(name, (tall, wide))

    def kernel(*refs):
        count = len(names)
        hand_kernel(
            names,
            SimpleNamespace(
                source=dict(zip(names, refs)),
                target=dict(zip(names, refs[count:])),
                buffer=dict(zip(names, refs[2 * count :])),
                apart=refs[3 * count],
                sems=refs[3 * count + 1],
            ),
        )

    results = pl.pallas_call(
        kernel,
        out_shape=tuple(jax.ShapeDtypeStruct(shape_of(name), arrays[name].dtype) for name in names),
        in_specs=[IN_PLACE] * len(names),
        out_specs=tuple([IN_PLACE] * len(names)),
        scratch_shapes=[pltpu.VMEM(arrays[name].shape, arrays[name].dtype) for name in names]
        + [pltpu.VMEM(shape_of("pair"), F32), pltpu.SemaphoreType.DMA((4, len(names)))],
        compiler_params=pltpu.CompilerParams(vmem_limit_bytes=VMEM_LIMIT),
    )(*arrays.values())
    return SimpleNamespace(**dict(zip(names, results)))


def allowed_block(codes, seg_row, key_begin, query_begin):
    wide = jnp.concatenate([codes] * (QUERY_BLOCK // 128), axis=1)
    place = lax.broadcasted_iota(jnp.int32, (KEY_BLOCK, QUERY_BLOCK), 0) - lax.broadcasted_iota(
        jnp.int32, (KEY_BLOCK, QUERY_BLOCK), 1
    )
    return (wide == seg_row) | (place == query_begin - key_begin)


def head_cols(local):
    return [pl.ds(head * HEAD_DIM, HEAD_DIM) for head in range(local // HEAD_DIM)]


def attend_kernel(bounds, query, keys, values, seg_row, codes, out, totals):
    step = pl.program_id(0)
    heads = head_cols(query.shape[1])
    segs = seg_row[...]

    def one(index, carried):
        here = span(index * KEY_BLOCK, KEY_BLOCK)
        allowed = allowed_block(codes[here, :], segs, index * KEY_BLOCK, MAXLEN + step * QUERY_BLOCK)
        scores = [across_product(keys[here, cols], query[:, cols]) * (SCORE_SCALE * LOG2E) for cols in heads]
        result = []
        for (highest, total, mixed), score, cols in zip(carried, scores, heads):
            score = jnp.where(allowed, score, -1e30)
            top = jnp.maximum(highest, jnp.max(score, axis=0, keepdims=True))
            fade = jnp.exp2(highest - top)
            weights = jnp.exp2(score - top)
            total = total * fade + jnp.sum(weights, axis=0, keepdims=True)
            mixed = mixed * fade + inner_product(values[here, cols], weights.astype(BF16))
            result.append((top, total, mixed))
        return tuple(result)

    start = (
        jnp.full((1, QUERY_BLOCK), -1e30, F32),
        jnp.zeros((1, QUERY_BLOCK), F32),
        jnp.zeros((HEAD_DIM, QUERY_BLOCK), F32),
    )
    ends = lax.fori_loop(bounds[step, 0], bounds[step, 1], one, (start,) * len(heads))
    for head, ((highest, total, mixed), cols) in enumerate(zip(ends, heads)):
        out[:, cols] = jnp.transpose(mixed / total)
        totals[head] = highest + jnp.log2(total)


def attend_back_kernel(
    bounds, query, keys, values, grad, mixed, totals, seg_row, codes, grad_query, key_out, value_out, grad_key, grad_value
):
    step = pl.program_id(0)
    heads = head_cols(query.shape[1])

    @pl.when(step == 0)
    def _():
        grad_key[...] = jnp.zeros_like(grad_key)
        grad_value[...] = jnp.zeros_like(grad_value)

    segs = seg_row[...]
    centres = [
        jnp.sum(jnp.transpose(grad[:, cols].astype(F32) * mixed[:, cols]), axis=0, keepdims=True) for cols in heads
    ]

    def one(index, carried):
        here = span(index * KEY_BLOCK, KEY_BLOCK)
        allowed = allowed_block(codes[here, :], segs, index * KEY_BLOCK, MAXLEN + step * QUERY_BLOCK)
        scores = [across_product(keys[here, cols], query[:, cols]) * (SCORE_SCALE * LOG2E) for cols in heads]
        slopes = [across_product(values[here, cols], grad[:, cols]) for cols in heads]
        result = []
        for head, (total, score, slope, centre, cols) in enumerate(zip(carried, scores, slopes, centres, heads)):
            probs = jnp.where(allowed, jnp.exp2(score - totals[head]), 0.0)
            grad_scores = (probs * (slope - centre) * SCORE_SCALE).astype(BF16)
            grad_value[here, cols] += plain_product(probs.astype(BF16), grad[:, cols])
            grad_key[here, cols] += plain_product(grad_scores, query[:, cols])
            result.append(total + inner_product(grad_scores, keys[here, cols]))
        return tuple(result)

    ends = lax.fori_loop(
        bounds[step, 0], bounds[step, 1], one, (jnp.zeros((QUERY_BLOCK, HEAD_DIM), F32),) * len(heads)
    )
    for total, cols in zip(ends, heads):
        grad_query[:, cols] = total.astype(BF16)

    @pl.when(step == pl.num_programs(0) - 1)
    def _():
        key_out[...] = grad_key[...].astype(BF16)
        value_out[...] = grad_value[...].astype(BF16)


def attend_specs(frames, local, window):
    heads = local // HEAD_DIM
    return dict(
        bounds=pl.BlockSpec(memory_space=pltpu.SMEM),
        rows=pl.BlockSpec((QUERY_BLOCK, local), lambda i: (i, 0)),
        keys=pl.BlockSpec((window, local), lambda i: (0, 0)),
        values=pl.BlockSpec((window, local), lambda i: (0, 1)),
        segs=pl.BlockSpec((1, QUERY_BLOCK), lambda i: (0, i)),
        codes=pl.BlockSpec((window, 128), lambda i: (0, 0)),
        totals=pl.BlockSpec((heads, 1, QUERY_BLOCK), lambda i: (0, 0, i)),
    )


def attend(queries, both, context):
    bounds, seg_row, codes = context
    frames, local = queries.shape
    specs = attend_specs(frames, local, both.shape[0])
    return pl.pallas_call(
        attend_kernel,
        grid=(frames // QUERY_BLOCK,),
        in_specs=[specs[name] for name in ("bounds", "rows", "keys", "values", "segs", "codes")],
        out_specs=[specs["rows"], specs["totals"]],
        out_shape=(
            jax.ShapeDtypeStruct((frames, local), F32),
            jax.ShapeDtypeStruct((local // HEAD_DIM, 1, frames), F32),
        ),
        compiler_params=pltpu.CompilerParams(vmem_limit_bytes=VMEM_LIMIT),
        cost_estimate=pl.CostEstimate(
            flops=4 * frames * MAXLEN * local, bytes_accessed=8 << 20, transcendentals=0
        ),
    )(bounds, queries, both, both, seg_row, codes)


def attend_back(queries, both, grads, mixed, totals, context):
    bounds, seg_row, codes = context
    frames, local = queries.shape
    window = both.shape[0]
    specs = attend_specs(frames, local, window)
    return pl.pallas_call(
        attend_back_kernel,
        grid=(frames // QUERY_BLOCK,),
        in_specs=[
            specs[name]
            for name in ("bounds", "rows", "keys", "values", "rows", "rows", "totals", "segs", "codes")
        ],
        out_specs=[specs["rows"], specs["keys"], specs["keys"]],
        out_shape=(
            jax.ShapeDtypeStruct((frames, local), BF16),
            jax.ShapeDtypeStruct((window, local), BF16),
            jax.ShapeDtypeStruct((window, local), BF16),
        ),
        scratch_shapes=[pltpu.VMEM((window, local), F32), pltpu.VMEM((window, local), F32)],
        compiler_params=pltpu.CompilerParams(vmem_limit_bytes=VMEM_LIMIT),
        cost_estimate=pl.CostEstimate(
            flops=10 * frames * MAXLEN * local, bytes_accessed=16 << 20, transcendentals=0
        ),
    )(bounds, queries, both, both, grads, mixed, totals, seg_row, codes)


def body(
    inputs,
    ln_gains,
    ffn1_in,
    ffn1_out,
    qkv_weight,
    attn_out,
    conv_in,
    conv_depth,
    bn_gain,
    bn_bias,
    conv_out,
    ffn2_in,
    ffn2_out,
    segment_ids,
    pad_mask,
    out_grad,
):
    frames = inputs.shape[0] * lax.axis_size(TP)
    gain_row, bias_row = bn_gain[None, :], bn_bias[None, :]
    shards = SimpleNamespace(
        ffn1_in=ffn1_in,
        ffn1_out=ffn1_out,
        project=jnp.transpose(qkv_weight, (1, 0, 2)),
        attend=attn_out,
        pair=conv_in,
        conv=conv_out,
        ffn2_in=ffn2_in,
        ffn2_out=ffn2_out,
    )
    opened = run_open(
        inputs, ln_gains, shards, segment_ids.reshape(-1, 128), pad_mask.reshape(-1, 128)
    )
    seg_row = lax.dynamic_slice_in_dim(segment_ids, lax.axis_index(SEQ) * frames, frames)[None, :]
    context = (opened.bounds, seg_row, opened.codes)
    mixed, totals = attend(opened.queries, opened.window, context)
    middle = run_middle(mixed, opened, ln_gains, conv_depth, gain_row, bias_row, shards, out_grad)
    grad_query, grad_key, grad_value = attend_back(
        opened.queries, opened.window, middle.grad_mixed, mixed, totals, context
    )
    closed = run_close(inputs, ln_gains, opened, middle, grad_query, grad_key, grad_value)
    given = hand_over(
        dict(
            output=middle.output,
            input_grad=closed.input_grad,
            gains=closed.gain_total,
            first_in=closed.sum_in,
            first_out=closed.sum_out,
            project=closed.sum_project,
            attend=closed.sum_attend,
            pair=closed.sum_pair,
            depth=closed.depth_total,
            gain=middle.sum_gain,
            bias=middle.sum_bias,
            conv=closed.sum_conv,
            second_in=middle.sum_in,
            second_out=middle.sum_out,
        )
    )
    return (
        given.output,
        given.input_grad,
        given.gains,
        given.first_in,
        given.first_out,
        jnp.transpose(given.project, (1, 0, 2)),
        given.attend,
        given.pair,
        given.depth,
        given.gain[0],
        given.bias[0],
        given.conv,
        given.second_in,
        given.second_out,
    )


def solution(mesh):
    return jax.shard_map(
        body,
        mesh=mesh,
        in_specs=(
            P((SEQ, TP), None),
            P(),
            P(SEQ, TP),
            P((TP, SEQ), None),
            P(SEQ, None, TP),
            P((TP, SEQ), None),
            P(SEQ, None, TP),
            P(None, TP),
            P(TP),
            P(TP),
            P((TP, SEQ), None),
            P(SEQ, TP),
            P((TP, SEQ), None),
            P(),
            P(),
            P((SEQ, TP), None),
        ),
        out_specs=(
            P((SEQ, TP), None),
            P((SEQ, TP), None),
            P(),
            P(SEQ, TP),
            P((TP, SEQ), None),
            P(SEQ, None, TP),
            P((TP, SEQ), None),
            P(SEQ, None, TP),
            P(None, TP),
            P(TP),
            P(TP),
            P((TP, SEQ), None),
            P(SEQ, TP),
            P((TP, SEQ), None),
        ),
        check_vma=False,
    )
```

```python
import math
from types import SimpleNamespace

import jax
import jax.numpy as jnp
from jax import lax
from jax.experimental import pallas as pl
from jax.experimental.pallas import tpu as pltpu
from jax.sharding import PartitionSpec as P

SEQ, TP = "seq", "tp"
LOAD, KEEP = "load", "keep"
HEAD_DIM = 128
KERNEL = 5
MAXLEN = 1536
EPSILON = 1e-05
CHUNKS = 2
EDGE = 8
VMEM_LIMIT = 62 << 20
QUERY_BLOCK = 256
KEY_BLOCK = 512
SCORE_SCALE = 1.0 / math.sqrt(HEAD_DIM)
LOG2E = 1.4426950408889634
BF16 = jnp.bfloat16
F32 = jnp.float32
IN_VMEM = pl.BlockSpec(memory_space=pltpu.VMEM)
IN_PLACE = pl.BlockSpec(memory_space=pl.ANY)


def plain_product(left, right):
    return jnp.dot(left, right, preferred_element_type=F32)


def inner_product(left, right):
    return lax.dot_general(left, right, (((0,), (0,)), ((), ())), preferred_element_type=F32)


def across_product(left, right):
    return lax.dot_general(left, right, (((1,), (1,)), ((), ())), preferred_element_type=F32)


def swish(values):
    return values * jax.nn.sigmoid(values)


def standard_rows(values):
    centred = values - jnp.mean(values, axis=-1, keepdims=True)
    spread = jnp.mean(centred * centred, axis=-1, keepdims=True)
    inverse = lax.rsqrt(spread + EPSILON)
    return (centred * inverse, inverse)


def norm_rows(values, gain_row):
    return standard_rows(values)[0] * gain_row


def norm_back(values, gain_row, grads):
    normal, inverse = standard_rows(values)
    scaled = grads * gain_row
    result = inverse * (
        scaled
        - jnp.mean(scaled, axis=-1, keepdims=True)
        - normal * jnp.mean(scaled * normal, axis=-1, keepdims=True)
    )
    return (result, jnp.sum(grads * normal, axis=0, keepdims=True))


def flip(index, bit):
    return index + bit - 2 * bit * lax.rem(lax.div(index, bit), 2)


def span(begin, size):
    return pl.ds(pl.multiple_of(begin, size), size)


def rows_at(begin, size):
    return pl.ds(begin, size) if isinstance(begin, int) else span(begin, size)


def remote(source, target, send, receive, peer):
    return pltpu.make_async_remote_copy(
        src_ref=source,
        dst_ref=target,
        send_sem=send,
        recv_sem=receive,
        device_id=peer,
        device_id_type=pl.DeviceIdType.MESH,
    )


def tp_peers():
    me = lax.axis_index(TP)
    return [{TP: flip(me, 1)}, {TP: flip(me, 2)}]


def seq_peers():
    me, count = lax.axis_index(SEQ), lax.axis_size(SEQ)
    return [{SEQ: lax.rem(me + step, count)} for step in range(1, count)]


def greet(peers):
    barrier = pltpu.get_barrier_semaphore()
    for peer in peers:
        pl.semaphore_signal(barrier, inc=1, device_id=peer, device_id_type=pl.DeviceIdType.MESH)
    return lambda: pl.semaphore_wait(barrier, len(peers))


def owner(slot):
    me = lax.axis_index(TP)
    if slot & 1:
        me = flip(me, 1)
    if slot & 2:
        me = flip(me, 2)
    return me


def tiles(total, tile, body):
    def one(index, nothing):
        body(span(index * tile, tile))
        return nothing

    lax.fori_loop(0, total // tile, one, 0)


class Gather:
    def __init__(self, rows, send, receive):
        self.near, self.far = tp_peers()
        self.height = rows.shape[0] // 4
        self.piece = self.height // CHUNKS
        self.rows, self.send, self.receive = rows, send, receive

    def part(self, slot, chunk):
        return self.rows.at[rows_at(slot * self.height + chunk * self.piece, self.piece), :]

    def hop(self, kind, chunk):
        source, target = ((0, 1), (0, 2), (2, 3))[kind]
        return remote(
            self.part(source, chunk),
            self.part(target, chunk),
            self.send.at[kind, chunk],
            self.receive.at[kind, chunk],
            self.far if kind == 1 else self.near,
        )

    def start(self, chunk):
        self.hop(1, chunk).start()
        self.hop(0, chunk).start()

    def wait_near(self):
        for chunk in range(CHUNKS):
            self.hop(0, chunk).wait_recv()

    def pass_on(self, chunk):
        self.hop(1, chunk).wait_recv()
        self.hop(2, chunk).start()

    def wait_last(self, chunk):
        self.hop(2, chunk).wait_recv()

    def finish(self):
        for chunk in range(CHUNKS):
            for kind in range(3):
                self.hop(kind, chunk).wait_send()


def each_chunk(body):
    def one(chunk, nothing):
        body(chunk)
        return nothing

    lax.fori_loop(0, CHUNKS, one, 0)


def gather_scratch():
    return dict(send=pltpu.SemaphoreType.DMA((3, CHUNKS)), receive=pltpu.SemaphoreType.DMA((3, CHUNKS)))


class Scatter:
    def __init__(self, own, passing, outgoing, incoming, send, receive):
        self.near, self.far = tp_peers()
        self.height = own.shape[0]
        self.piece = self.height // CHUNKS
        self.own, self.passing = own, passing
        self.outgoing, self.incoming, self.send, self.receive = outgoing, incoming, send, receive

    def rows(self, chunk):
        return rows_at(chunk * self.piece, self.piece)

    def copy(self, kind, chunk):
        here = self.rows(chunk)
        return remote(
            self.outgoing.at[kind, here, :],
            self.incoming.at[kind, here, :],
            self.send.at[kind, chunk],
            self.receive.at[kind, chunk],
            self.far if kind == 2 else self.near,
        )

    def start(self, kind):
        for chunk in range(CHUNKS):
            self.copy(kind, chunk).start()

    def relay(self, chunk):
        here = self.rows(chunk)
        self.copy(1, chunk).wait_recv()
        self.outgoing[2, here, :] = (self.passing[here, :] + self.incoming[1, here, :].astype(F32)).astype(BF16)
        self.copy(2, chunk).start()

    def total(self, chunk):
        here = self.rows(chunk)
        self.copy(0, chunk).wait_recv()
        self.copy(2, chunk).wait_recv()
        return self.own[here, :] + self.incoming[0, here, :].astype(F32) + self.incoming[2, here, :].astype(F32)

    def spread(self, product, width, tile=256):
        height = self.height

        def far(cols):
            term = product((2, 3), cols)
            self.passing[:, cols] = term[:height]
            self.outgoing[1, :, cols] = term[height:].astype(BF16)

        tiles(width, tile, far)
        self.start(1)

        def near(cols):
            term = product((0, 1), cols)
            self.own[:, cols] = term[:height]
            self.outgoing[0, :, cols] = term[height:].astype(BF16)

        tiles(width, tile, near)
        for chunk in range(CHUNKS):
            self.relay(chunk)
        self.start(0)

    def finish(self):
        for kind in range(3):
            for chunk in range(CHUNKS):
                self.copy(kind, chunk).wait_send()


def scatter_scratch(height, width):
    return dict(
        own=pltpu.VMEM((height, width), F32),
        passing=pltpu.VMEM((height, width), F32),
        outgoing=pltpu.VMEM((3, height, width), BF16),
        incoming=pltpu.VMEM((3, height, width), BF16),
        send=pltpu.SemaphoreType.DMA((3, CHUNKS)),
        receive=pltpu.SemaphoreType.DMA((3, CHUNKS)),
    )


class Collect:
    def __init__(self, shard, full, send, receive, pair_send, pair_receive, local):
        self.me, self.count = lax.axis_index(SEQ), lax.axis_size(SEQ)
        self.groups = self.count // 2
        self.pair = {SEQ: flip(self.me, 1)}
        self.shard, self.full, self.height = shard, full, shard.shape[0]
        self.send, self.receive, self.pair_send, self.pair_receive = send, receive, pair_send, pair_receive
        self.local = pltpu.make_async_copy(shard, self.block(self.me), local.at[0])

    def block(self, index):
        return self.full.at[span(index * self.height, self.height), :]

    def out(self, step):
        peer = {SEQ: lax.rem(self.me + 2 * step, self.count)}
        return remote(self.shard, self.block(self.me), self.send.at[step - 1], self.receive.at[step - 1], peer)

    def over(self, step):
        if step == 0:
            source, place = self.shard, self.me
        else:
            place = lax.rem(self.me + self.count - 2 * step, self.count)
            source = self.block(place)
        return remote(source, self.block(place), self.pair_send.at[step], self.pair_receive.at[step], self.pair)

    def kick(self, step):
        if step == 0:
            self.over(0).start()
            self.local.start()
        else:
            self.out(step).start()

    def turn(self, step):
        if step:
            self.out(step).wait_recv()
            self.over(step).start()

    def end(self):
        self.local.wait()
        for step in range(self.groups):
            self.over(step).wait_recv()

    def finish(self):
        for step in range(self.groups):
            self.over(step).wait_send()
            if step:
                self.out(step).wait_send()


def collect_scratch():
    groups = lax.axis_size(SEQ) // 2
    return dict(
        send=pltpu.SemaphoreType.DMA((groups,)),
        receive=pltpu.SemaphoreType.DMA((groups,)),
        pair_send=pltpu.SemaphoreType.DMA((groups,)),
        pair_receive=pltpu.SemaphoreType.DMA((groups,)),
        local=pltpu.SemaphoreType.DMA((1,)),
    )


class Settle:
    def __init__(self, source, result, partner, others, send, receive, far_send, far_receive, half=None, load=None):
        self.me, self.count = lax.axis_index(SEQ), lax.axis_size(SEQ)
        self.groups = self.count // 2
        self.other = flip(self.me, 1)
        self.source, self.result, self.half, self.partner, self.others = source, result, half, partner, others
        self.height = result.shape[0]
        self.load, self.send, self.receive = load, send, receive
        self.far_send, self.far_receive = far_send, far_receive

    def block(self, base, step):
        place = lax.rem(base + 2 * step, self.count)
        return self.source.at[span(place * self.height, self.height), :]

    def mine(self, step):
        return self.block(self.me, step) if self.half is None else self.half.at[step]

    def swap(self, step):
        return remote(
            self.block(self.other, step),
            self.partner.at[step],
            self.send.at[step],
            self.receive.at[step],
            {SEQ: self.other},
        )

    def fetch(self, step):
        return pltpu.make_async_copy(self.block(self.me, step), self.half.at[step], self.load.at[step])

    def away(self, step):
        peer = {SEQ: lax.rem(self.me + 2 * step, self.count)}
        return remote(
            self.mine(step), self.others.at[step], self.far_send.at[step], self.far_receive.at[step], peer
        )

    def kick(self, step):
        self.swap(step).start()
        if self.half is not None:
            self.fetch(step).start()

    def turn(self, step):
        if step:
            if self.half is not None:
                self.fetch(step).wait()
            self.swap(step).wait_recv()
            mine = self.mine(step)
            mine[...] = (mine[...].astype(F32) + self.partner[step].astype(F32)).astype(BF16)
            self.away(step).start()

    def end(self):
        if self.half is not None:
            self.fetch(0).wait()
        self.swap(0).wait_recv()
        total = self.mine(0)[...].astype(F32) + self.partner[0].astype(F32)
        for step in range(1, self.groups):
            self.away(step).wait_recv()
            total = total + self.others[step].astype(F32)
        self.result[...] = total

    def finish(self):
        for step in range(self.groups):
            self.swap(step).wait_send()
            if step:
                self.away(step).wait_send()


def settle_scratch(height, width, apart=False):
    groups = lax.axis_size(SEQ) // 2
    more = dict(half=pltpu.VMEM((groups, height, width), BF16), load=pltpu.SemaphoreType.DMA((groups,)))
    return dict(
        **(more if apart else {}),
        partner=pltpu.VMEM((groups, height, width), BF16),
        others=pltpu.VMEM((groups, height, width), BF16),
        send=pltpu.SemaphoreType.DMA((groups,)),
        receive=pltpu.SemaphoreType.DMA((groups,)),
        far_send=pltpu.SemaphoreType.DMA((groups,)),
        far_receive=pltpu.SemaphoreType.DMA((groups,)),
    )


class Plan:
    def __init__(self, points, tasks):
        self.points, self.tasks = points, tasks
        self.left = set()
        for place in range(1, len(tasks) + 1):
            self.left |= {10 * place + step for step in range(4)} | {-10 * place - step for step in range(1, 4)}

    def at(self, point):
        for number in self.points.get(point, ()):
            self.left.remove(number)
            place, digit = divmod(abs(number), 10)
            task = self.tasks[place - 1]
            for step in range(digit, task.groups if digit == 3 else min(digit + 1, task.groups)):
                (task.kick if number > 0 else task.turn)(step)

    def finish(self):
        assert not self.left, "steps left"
        for task in self.tasks:
            task.finish()


class Swap:
    def __init__(self, blocks, send, receive):
        self.me, self.count = lax.axis_index(SEQ), lax.axis_size(SEQ)
        self.blocks, self.send, self.receive = blocks, send, receive

    def copy(self, step):
        peer = {SEQ: lax.rem(self.me + step, self.count)}
        return remote(self.blocks.at[0], self.blocks.at[step], self.send.at[step], self.receive.at[step], peer)

    def start(self):
        for step in range(1, self.count):
            self.copy(step).start()

    def wait(self):
        for step in range(1, self.count):
            self.copy(step).wait_recv()

    def finish(self):
        for step in range(1, self.count):
            self.copy(step).wait_send()


def swap_scratch(height, width):
    count = lax.axis_size(SEQ)
    return dict(
        blocks=pltpu.VMEM((count, height, width), F32),
        send=pltpu.SemaphoreType.DMA((count,)),
        receive=pltpu.SemaphoreType.DMA((count,)),
    )


class Edges:
    def __init__(self, padded, send, receive):
        self.me, self.count = lax.axis_index(SEQ), lax.axis_size(SEQ)
        self.padded, self.send, self.receive = padded, send, receive
        self.frames = padded.shape[0] - 2 * EDGE

    def up(self):
        source = self.padded.at[pl.ds(self.frames, EDGE), :]
        target = self.padded.at[pl.ds(0, EDGE), :]
        peer = {SEQ: lax.rem(self.me + 1, self.count)}
        return remote(source, target, self.send.at[0], self.receive.at[0], peer)

    def down(self):
        source = self.padded.at[pl.ds(EDGE, EDGE), :]
        target = self.padded.at[pl.ds(EDGE + self.frames, EDGE), :]
        peer = {SEQ: lax.rem(self.me + self.count - 1, self.count)}
        return remote(source, target, self.send.at[1], self.receive.at[1], peer)

    def start(self):
        self.up().start()
        self.down().start()

    def wait(self):
        self.up().wait_recv()
        self.down().wait_recv()

    def finish(self):
        self.up().wait_send()
        self.down().wait_send()


def edges_scratch():
    return dict(send=pltpu.SemaphoreType.DMA((2,)), receive=pltpu.SemaphoreType.DMA((2,)))


def run_kernel(body, number, inputs, outputs, scratch, flops=1 << 33):
    loads = [name for name, (_, place) in inputs.items() if place == LOAD]
    keeps = [name for name, (_, _, place) in outputs.items() if place == KEEP]
    moved = {name: pltpu.VMEM(inputs[name][0].shape, inputs[name][0].dtype) for name in loads}
    moved.update({name: pltpu.VMEM(outputs[name][0], outputs[name][1]) for name in keeps})
    flat, groups = list(moved.values()) + [pltpu.SemaphoreType.DMA((max(1, len(moved)),))], []
    for name, item in scratch.items():
        parts = item if isinstance(item, dict) else {None: item}
        groups.append((name, list(parts)))
        flat.extend(parts.values())

    def kernel(*refs):
        given = dict(zip(list(inputs) + list(outputs), refs))
        rest = list(refs[len(given) :])
        near = {name: rest.pop(0) for name in moved}
        sems = rest.pop(0)
        copies = {}
        for place, name in enumerate(moved):
            ends = (given[name], near[name]) if name in loads else (near[name], given[name])
            copies[name] = pltpu.make_async_copy(*ends, sems.at[place])
        given.update(near)
        for name, keys in groups:
            taken = {key: rest.pop(0) for key in keys}
            given[name] = taken[None] if None in taken else taken
        for name in loads:
            copies[name].start()
        waiting, going = list(loads), []

        def wait(*names):
            for name in names:
                waiting.remove(name)
                copies[name].wait()

        def put(*names):
            for name in names:
                going.append(name)
                copies[name].start()

        body(SimpleNamespace(**given, wait=wait, put=put))
        assert not waiting and sorted(going) == sorted(keeps), "copies left"
        for name in going:
            copies[name].wait()

    results = pl.pallas_call(
        kernel,
        out_shape=tuple(jax.ShapeDtypeStruct(shape, kind) for shape, kind, _ in outputs.values()),
        in_specs=[IN_VMEM if place is True else IN_PLACE for _, place in inputs.values()],
        out_specs=tuple(IN_VMEM if place is True else IN_PLACE for _, _, place in outputs.values()),
        scratch_shapes=flat,
        compiler_params=pltpu.CompilerParams(
            collective_id=number, has_side_effects=True, vmem_limit_bytes=VMEM_LIMIT
        ),
        cost_estimate=pl.CostEstimate(flops=flops, bytes_accessed=16 << 20, transcendentals=0),
    )(*[array for array, _ in inputs.values()])
    return SimpleNamespace(**dict(zip(outputs, results)))


def ffn_forward(gather, scatter, win, wout, hidden, active, wait_in, wait_out, late=False, at=lambda point: None):
    rows, height, piece = gather.rows, gather.height, gather.piece
    width, inner = win.shape
    pair = pl.ds(0, 2 * height)
    gather.wait_near()
    wait_in()

    def first(cols):
        product = plain_product(rows[pair, :], win[:, cols])
        hidden[pair, cols] = product
        active[pair, cols] = swish(product).astype(BF16)

    def second(cols):
        product = plain_product(active[pair, :], wout[:, cols])
        scatter.own[:, cols] = product[:height]
        scatter.outgoing[0, :, cols] = product[height:].astype(BF16)

    def far_rows(chunk):
        return (
            rows_at(2 * height + chunk * piece, piece),
            rows_at(3 * height + chunk * piece, piece),
            scatter.rows(chunk),
        )

    def inward(chunk):
        low, high, here = far_rows(chunk)

        def third(cols):
            both = jnp.concatenate([rows[low, :], rows[high, :]], axis=0)
            product = plain_product(both, win[:, cols])
            hidden[low, cols] = product[:piece]
            hidden[high, cols] = product[piece:]
            alive = swish(product).astype(BF16)
            active[low, cols] = alive[:piece]
            active[high, cols] = alive[piece:]

        gather.wait_last(chunk)
        tiles(inner, 512, third)

    def outward(chunk):
        low, high, here = far_rows(chunk)

        def fourth(cols):
            both = jnp.concatenate([active[low, :], active[high, :]], axis=0)
            product = plain_product(both, wout[:, cols])
            scatter.passing[here, cols] = product[:piece]
            scatter.outgoing[1, here, cols] = product[piece:].astype(BF16)

        tiles(width, 512, fourth)
        scatter.copy(1, chunk).start()
        scatter.relay(chunk)

    tiles(inner, 512, first)
    at("first")
    gather.pass_on(0)

    def take(chunk):
        @pl.when(chunk > 0)
        def _():
            gather.pass_on(chunk)

        inward(chunk)

    def both_ways(chunk):
        take(chunk)
        outward(chunk)

    if late:
        each_chunk(take)
        wait_out()
        each_chunk(outward)
        at("outward")
        tiles(width, 512, second)
        scatter.start(0)
    else:
        wait_out()
        tiles(width, 512, second)
        scatter.start(0)
        each_chunk(both_ways)


def ffn_backward(gather, scatter, win, wout, hidden, active, slope, wait_out, wait_in, products=None, at=lambda point: None):
    rows, height, piece = gather.rows, gather.height, gather.piece
    width, inner = win.shape
    pair = pl.ds(0, 2 * height)
    gather.wait_near()
    wait_out()

    def bend(product, before):
        logistic = jax.nn.sigmoid(before)
        return (
            (before * logistic).astype(BF16),
            (product * (logistic * (1.0 + before * (1.0 - logistic)))).astype(BF16),
        )

    def first(cols):
        alive, steep = bend(across_product(rows[pair, :], wout[cols, :]), hidden[pair, cols])
        if active is not None:
            active[pair, cols] = alive
        slope[pair, cols] = steep

    def second(cols):
        product = across_product(slope[pair, :], win[cols, :])
        scatter.own[:, cols] = product[:height]
        scatter.outgoing[0, :, cols] = product[height:].astype(BF16)

    def far_rows(chunk):
        return (
            rows_at(2 * height + chunk * piece, piece),
            rows_at(3 * height + chunk * piece, piece),
            scatter.rows(chunk),
        )

    def inward(chunk):
        low, high, here = far_rows(chunk)

        def third(cols):
            both = jnp.concatenate([rows[low, :], rows[high, :]], axis=0)
            before = jnp.concatenate([hidden[low, cols], hidden[high, cols]], axis=0)
            alive, steep = bend(across_product(both, wout[cols, :]), before)
            if active is not None:
                active[low, cols] = alive[:piece]
                active[high, cols] = alive[piece:]
            slope[low, cols] = steep[:piece]
            slope[high, cols] = steep[piece:]

        gather.wait_last(chunk)
        tiles(inner, 256, third)

    def outward(chunk):
        low, high, here = far_rows(chunk)

        def fourth(cols):
            both = jnp.concatenate([slope[low, :], slope[high, :]], axis=0)
            product = across_product(both, win[cols, :])
            scatter.passing[here, cols] = product[:piece]
            scatter.outgoing[1, here, cols] = product[piece:].astype(BF16)

        tiles(width, 512, fourth)
        scatter.copy(1, chunk).start()
        scatter.relay(chunk)

    tiles(inner, 256, first)
    at("first")
    gather.pass_on(0)

    def take(chunk):
        @pl.when(chunk > 0)
        def _():
            gather.pass_on(chunk)

        inward(chunk)

    def both_ways(chunk):
        take(chunk)
        outward(chunk)

    if products is not None:
        each_chunk(take)
        products()
        wait_in()
        each_chunk(outward)
        tiles(width, 512, second)
        scatter.start(0)
        at("second")
    else:
        wait_in()
        tiles(width, 512, second)
        scatter.start(0)
        each_chunk(both_ways)


def weight_products(result, left, right, tile=256):
    def one(cols):
        result[:, cols] = inner_product(left[...], right[:, cols]).astype(BF16)

    tiles(right.shape[1], tile, one)


OPEN_PLAN = dict(
    start=(11, 13, 12, 10, 21, 23, 22, 20,),
    gather=(-11, -13, -12, -21,),
    out=(-23, -22, 31, 32, 33, 30,),
    outward=(-31, -32,),
    total0=(-33, 41, 42, 43, 40,),
    near=(-41, -42, -43,),
)


def describe_frames(n, frames):
    seq = lax.axis_index(SEQ)
    lines, reach, total = frames // 128, MAXLEN // 128, n.segs.shape[0]
    base = seq * lines

    def line_of(ids, line, outside):
        safe = lax.min(lax.max(line, 0), total - 1)
        row = ids[pl.ds(safe, 1), :]
        return jnp.where((line >= 0) & (line < total), row, outside)

    def code(index, nothing):
        line = base - reach + index
        row = jnp.where(line_of(n.pads, line, 0) == 1, line_of(n.segs, line, -2), -1)
        n.codes[span(index * 128, 128), :] = jnp.transpose(jnp.broadcast_to(row, (128, 128)))
        return nothing

    lax.fori_loop(0, lines + 2 * reach, code, 0)
    lane = lax.broadcasted_iota(jnp.int32, (8, 128), 1)
    row_at = lax.broadcasted_iota(jnp.int32, (8, 128), 0)

    def marks(index, nothing):
        before, own, after = [
            jnp.broadcast_to(line_of(n.segs, base + index + shift, -1), (8, 128)) for shift in (-1, 0, 1)
        ]
        real = jnp.broadcast_to(n.pads[pl.ds(base + index, 1), :], (8, 128))
        table = jnp.where((row_at == KERNEL) & (real == 1), 1.0, 0.0)
        for tap in range(KERNEL):
            shift = tap - KERNEL // 2
            if shift < 0:
                moved = jnp.where(lane < -shift, pltpu.roll(before, -shift, 1), pltpu.roll(own, -shift, 1))
            elif shift > 0:
                moved = jnp.where(
                    lane >= 128 - shift, pltpu.roll(after, 128 - shift, 1), pltpu.roll(own, 128 - shift, 1)
                )
            else:
                moved = own
            table = jnp.where((row_at == tap) & (moved == own), 1.0, table)
        table = jnp.concatenate([table, jnp.zeros((120, 128), F32)], axis=0)
        n.context[span(index * 128, 128), :] = jnp.transpose(table)
        return nothing

    lax.fori_loop(0, lines, marks, 0)
    everyone = n.segs[...]
    offset = (MAXLEN - seq * frames).astype(F32)
    edge = lax.broadcasted_iota(jnp.int32, (1, 128), 1)
    per = QUERY_BLOCK // 128
    for step in range(frames // QUERY_BLOCK):
        low = n.segs[pl.ds(base + step * per, 1), :][:, 0:1]
        high = n.segs[pl.ds(base + step * per + per - 1, 1), :][:, 127:128]
        below = jnp.sum(jnp.where(everyone < low, 1.0, 0.0), keepdims=True)
        upto = jnp.sum(jnp.where(everyone <= high, 1.0, 0.0), keepdims=True)
        first = jnp.floor((below + offset) * (1.0 / KEY_BLOCK))
        last = jnp.floor((upto + (offset + (KEY_BLOCK - 1))) * (1.0 / KEY_BLOCK))
        n.bounds[step : step + 1, :] = jnp.where(edge == 0, first, last).astype(jnp.int32)


def open_kernel(n):
    height, width = n.values.shape
    frames = 4 * height
    local = n.queries.shape[1]
    seq, count = lax.axis_index(SEQ), lax.axis_size(SEQ)
    first_in = Collect(n.shard_in, n.win, **n.c_in)
    first_out = Collect(n.shard_out, n.wout, **n.c_out)
    project = Collect(n.shard_project, n.wproject, **n.c_project)
    attend_out = Collect(n.shard_attend, n.full_attend, **n.c_attend)
    plan = Plan(OPEN_PLAN, (first_in, first_out, project, attend_out))
    gather = Gather(n.rows, **n.g1)
    scatter = Scatter(**n.s1)
    gather_two = Gather(n.rows_two, **n.g2)
    ready = greet(tp_peers() + seq_peers())
    n.rows[pl.ds(0, gather.piece), :] = norm_rows(
        n.values[pl.ds(0, gather.piece), :].astype(F32), n.gains[0:1, :]
    ).astype(BF16)
    for part in range(3):
        n.shard_project[:, pl.ds(part * local, local)] = n.project_parts[part]
    ready()
    plan.at("start")
    for chunk in range(CHUNKS):
        here = scatter.rows(chunk)
        if chunk > 0:
            n.rows[here, :] = norm_rows(n.values[here, :].astype(F32), n.gains[0:1, :]).astype(BF16)
        gather.start(chunk)
    describe_frames(n, frames)
    n.put("codes", "context")
    plan.at("gather")
    keeps = [
        pltpu.make_async_copy(n.win, n.full_in, n.keep.at[0]),
        pltpu.make_async_copy(n.wout, n.full_out, n.keep.at[1]),
        pltpu.make_async_copy(n.wproject, n.full_project, n.keep.at[2]),
    ]

    def wait_in():
        first_in.end()
        keeps[0].start()

    def wait_out():
        plan.at("out")
        first_out.end()
        keeps[1].start()

    ffn_forward(gather, scatter, n.win, n.wout, n.hidden, n.active, wait_in, wait_out, late=True, at=plan.at)
    for chunk in range(CHUNKS):
        here = scatter.rows(chunk)
        n.first[here, :] = n.values[here, :].astype(F32) + 0.5 * scatter.total(chunk)
        n.rows_two[here, :] = norm_rows(n.first[here, :], n.gains[1:2, :]).astype(BF16)
        gather_two.start(chunk)
        plan.at(f"total{chunk}")
    n.put("rows", "hidden", "first")
    project.end()
    keeps[2].start()
    gather_two.wait_near()

    def send_block(slot):
        place = owner(slot)
        source = n.all_own.at[span(place * height, height), pl.ds(local, 2 * local)]
        upper = lax.div(place, 2)

        def piece(kind):
            if kind == 0:
                peer, row = lax.rem(seq + 1, count), MAXLEN - frames + place * height
            elif kind == 1:
                peer, row = lax.rem(seq + count - 1, count), MAXLEN + frames + place * height
            else:
                peer = lax.rem(seq + count - 2 + 4 * upper, count)
                row = MAXLEN + place * height + 2 * frames * (1 - 2 * upper)
            target = n.window.at[span(row, height), :]
            return remote(source, target, n.halo_send.at[kind, slot], n.halo_receive.at[kind, slot], {SEQ: peer})

        return [piece(kind) for kind in range(3)]

    def there(kind, slot, sending):
        upper = lax.div(owner(slot), 2)
        if kind == 2:
            shift = 4 * upper - 2
        else:
            shift = 1 - 2 * kind
        target = seq + shift if sending else seq - shift
        return (target >= 0) & (target < count)

    def project_rows(slots, low):
        def part(cols):
            product = plain_product(n.rows_two[low, :], n.wproject[:, cols]).astype(BF16)
            for index, slot in enumerate(slots):
                n.all_own[span(owner(slot) * height, height), cols] = product[index * height : (index + 1) * height]

        tiles(3 * local, local, part)
        for slot in slots:
            for kind, copy in enumerate(send_block(slot)):

                @pl.when(there(kind, slot, True))
                def _():
                    copy.start()

    project_rows((0, 1), pl.ds(0, 2 * height))
    for chunk in range(CHUNKS):
        gather_two.pass_on(chunk)
    plan.at("near")
    for chunk in range(CHUNKS):
        gather_two.wait_last(chunk)
    n.put("rows_two")
    project_rows((2, 3), pl.ds(2 * height, 2 * height))
    own = pltpu.make_async_copy(
        n.all_own.at[:, pl.ds(local, 2 * local)], n.window.at[pl.ds(MAXLEN, frames), :], n.keep.at[3]
    )
    own.start()
    asked = pltpu.make_async_copy(n.all_own.at[:, pl.ds(0, local)], n.queries, n.keep.at[4])
    asked.start()
    for slot in range(4):
        for kind, copy in enumerate(send_block(slot)):

            @pl.when(there(kind, slot, False))
            def _():
                copy.wait_recv()

            @pl.when(there(kind, slot, True))
            def _():
                copy.wait_send()

    attend_out.end()
    for keep in keeps:
        keep.wait()
    own.wait()
    asked.wait()
    plan.finish()
    for item in [gather, scatter, gather_two]:
        item.finish()


def run_open(values, gains, shards, segs, pads):
    height, width = values.shape
    frames = 4 * height
    count = lax.axis_size(SEQ)
    inner, local = shards.ffn1_in.shape[1], shards.attend.shape[0] * count
    fulls = dict(
        full_in=shards.ffn1_in, full_out=shards.ffn1_out,
        full_attend=shards.attend,
    )
    return run_kernel(
        open_kernel,
        0,
        dict(
            values=(values, True), gains=(gains, True), shard_in=(shards.ffn1_in, True),
            shard_out=(shards.ffn1_out, True), project_parts=(shards.project, True),
            segs=(segs, True), pads=(pads, True),
            shard_attend=(shards.attend, True),
        ),
        dict(
            first=((height, width), F32, KEEP),
            rows=((frames, width), BF16, KEEP),
            hidden=((frames, inner), F32, KEEP),
            rows_two=((frames, width), BF16, KEEP),
            queries=((frames, local), BF16, False),
            window=((frames + 2 * MAXLEN, 2 * local), BF16, False),
            codes=((frames + 2 * MAXLEN, 128), jnp.int32, KEEP),
            context=((frames, 128), F32, KEEP),
            bounds=((8, 128), jnp.int32, True),
            full_project=((width, 3 * local), BF16, False),
            **{name: ((item.shape[0] * count, item.shape[1]), BF16, False) for name, item in fulls.items()},
        ),
        dict(
            win=pltpu.VMEM((width, inner), BF16),
            wout=pltpu.VMEM((inner, width), BF16),
            wproject=pltpu.VMEM((width, 3 * local), BF16),
            shard_project=pltpu.VMEM((width // count, 3 * local), BF16),
            active=pltpu.VMEM((frames, inner), BF16),
            all_own=pltpu.VMEM((frames, 3 * local), BF16),
            c_in=collect_scratch(), c_out=collect_scratch(), c_project=collect_scratch(),
            c_attend=collect_scratch(),
            g1=gather_scratch(), s1=scatter_scratch(height, width), g2=gather_scratch(),
            halo_send=pltpu.SemaphoreType.DMA((3, 4)), halo_receive=pltpu.SemaphoreType.DMA((3, 4)),
            keep=pltpu.SemaphoreType.DMA((5,)),
        ),
    )


def slot_rows(slots, height):
    return pl.ds(slots[0] * height, 2 * height)


def in_order(swap):
    for place in range(swap.count):
        yield swap.blocks[lax.rem(swap.me + swap.count - place, swap.count)]


def middle_kernel(n):
    height, width = n.first.shape
    frames = 4 * height
    local = n.mixed.shape[1]
    block = 128
    none = jnp.zeros((1, local), F32)
    pair_weight, conv_weight = Collect(n.shard_pair, n.wpair, **n.c_pair), Collect(n.shard_conv, n.wconv, **n.c_conv)
    in_weight, out_weight = Collect(n.shard_in, n.win, **n.c_in), Collect(n.shard_out, n.wout, **n.c_out)
    out_sum, in_sum = Settle(n.grad_out, n.sum_out, **n.t_out), Settle(n.grad_in, n.sum_in, **n.t_in)
    plan = Plan(
        MIDDLE_PLAN,
        (pair_weight, conv_weight, in_weight, out_weight, out_sum, in_sum),
    )
    scatter = Scatter(**n.s1)
    gathers = [
        Gather(n.rows_conv, **n.g1), Gather(n.rows, **n.g2), Gather(n.grads, **n.g3),
        Gather(n.grads_conv, **n.g4), Gather(n.grads, **n.g5),
    ]
    edges, edges_back = Edges(n.gated, **n.edge), Edges(n.back, **n.edge_back)
    swap, swap_back = Swap(**n.swap), Swap(**n.swap_back)
    chunks = [scatter.rows(chunk) for chunk in range(CHUNKS)]
    ready = greet(tp_peers() + seq_peers())
    for slot in range(4):
        n.mixed_low[pl.ds(slot * height, height), :] = n.mixed[span(owner(slot) * height, height), :].astype(BF16)
    for part in range(2):
        n.shard_pair[:, pl.ds(part * local, local)] = n.pair_parts[:, part, :]
    ready()
    plan.at("start")
    scatter.spread(
        lambda slots, cols: plain_product(n.mixed_low[slot_rows(slots, height), :], n.wattend[:, cols]), width
    )
    gather = gathers[0]
    plan.at("spread")
    n.wait("first")
    for chunk, here in enumerate(chunks):
        n.second[here, :] = n.first[here, :] + scatter.total(chunk)
        n.rows_conv[here, :] = norm_rows(n.second[here, :], n.gains[2:3, :]).astype(BF16)
        gather.start(chunk)
        plan.at(f"second{chunk}")
    scatter.finish()
    gather.wait_near()
    pair_weight.end()
    n.wait("context")

    def pair_rows(slots):
        product = plain_product(n.rows_conv[slot_rows(slots, height), :], n.wpair[...])
        for index, slot in enumerate(slots):
            rows = product[index * height : (index + 1) * height]
            place = owner(slot) * height
            n.paired[span(place, height), :] = rows
            real = n.context[span(place, height), KERNEL : KERNEL + 1]
            gated = rows[:, :local] * jax.nn.sigmoid(rows[:, local:]) * real
            n.gated[pl.ds(pl.multiple_of(EDGE + place, EDGE), height), :] = gated.astype(BF16).astype(F32)

    pair_rows((0, 1))
    for chunk in range(CHUNKS):
        gather.pass_on(chunk)
    plan.at("passed")
    for chunk in range(CHUNKS):
        gather.wait_last(chunk)
    pair_rows((2, 3))
    edges.start()
    plan.at("edged")

    def convolve(index, carried):
        total, real_count = carried
        around = n.gated[pl.ds(pl.multiple_of(index * block, block), block + 2 * EDGE), :]
        marks = n.context[span(index * block, block), :]
        conv = jnp.zeros((block, local), F32)
        for tap in range(KERNEL):
            begin = EDGE - KERNEL // 2 + tap
            conv = conv + n.depth[tap : tap + 1, :] * around[begin : begin + block] * marks[:, tap : tap + 1]
        n.normal[span(index * block, block), :] = conv
        real = marks[:, KERNEL : KERNEL + 1]
        return (
            total + jnp.sum(real * conv, axis=0, keepdims=True),
            real_count + jnp.sum(jnp.broadcast_to(real, conv.shape), axis=0, keepdims=True),
        )

    last = frames // block - 1
    carried = lax.fori_loop(1, last, convolve, (none, none))
    edges.wait()
    plan.at("edges")
    total, real_count = convolve(last, convolve(0, carried))
    middle = total / jnp.maximum(real_count, 1.0)

    def deviate(index, carried):
        conv = n.normal[span(index * block, block), :]
        real = n.context[span(index * block, block), KERNEL : KERNEL + 1]
        away = conv - middle
        return carried + jnp.sum(real * away * away, axis=0, keepdims=True)

    squares = lax.fori_loop(0, frames // block, deviate, none)
    swap.blocks[0, 0:1, :] = total
    swap.blocks[0, 1:2, :] = squares
    swap.blocks[0, 2:3, :] = real_count
    swap.start()
    swap.wait()
    plan.at("swapped")
    total_all, real_all = none, none
    for item in in_order(swap):
        total_all = total_all + item[0:1]
        real_all = real_all + item[2:3]
    centre = total_all / real_all
    squares_all = none
    for item in in_order(swap):
        away = item[0:1] / jnp.maximum(item[2:3], 1.0) - centre
        squares_all = squares_all + item[1:2] + item[2:3] * away * away
    inverse = lax.rsqrt(squares_all / real_all + EPSILON)
    for slot in range(4):
        place = span(owner(slot) * height, height)
        normal = (n.normal[place, :] - centre) * inverse
        n.normal[place, :] = normal
        n.alive[pl.ds(slot * height, height), :] = swish(normal * n.bn_gain[...] + n.bn_bias[...]).astype(BF16)
    conv_weight.end()
    scatter.spread(
        lambda slots, cols: plain_product(n.alive[slot_rows(slots, height), :], n.wconv[:, cols]), width
    )
    plan.at("alive")
    gather = gathers[1]
    for chunk, here in enumerate(chunks):
        n.third[here, :] = n.second[here, :] + scatter.total(chunk)
        n.rows[here, :] = norm_rows(n.third[here, :], n.gains[3:4, :]).astype(BF16)
        gather.start(chunk)
        plan.at(f"third{chunk}")
    scatter.finish()
    ffn_forward(gather, scatter, n.win, n.wout, n.hidden, n.active, in_weight.end, out_weight.end, True, plan.at)
    gather = gathers[2]
    n.wait("out_grad")
    gain_four = jnp.zeros((1, width), F32)
    for chunk, here in enumerate(chunks):
        fourth = n.third[here, :] + 0.5 * scatter.total(chunk)
        n.output[here, :] = norm_rows(fourth, n.gains[4:5, :]).astype(BF16)
        grad, gain = norm_back(fourth, n.gains[4:5, :], n.out_grad[here, :].astype(F32))
        gain_four = gain_four + gain
        n.grad_row[here, :] = grad
        n.grads[here, :] = (0.5 * grad).astype(BF16)
        gather.start(chunk)
    scatter.finish()
    n.put("output")

    def nothing():
        return None

    ffn_backward(gather, scatter, n.win, n.wout, n.hidden, None, n.slope, nothing, nothing)
    weight_products(n.grad_out, n.active, n.grads)
    plan.at("grad_out")
    weight_products(n.grad_in, n.rows, n.slope)
    plan.at("grad_in")
    gathers[2].finish()
    gather = gathers[3]
    gain_three = jnp.zeros((1, width), F32)
    for chunk, here in enumerate(chunks):
        grad, gain = norm_back(n.third[here, :], n.gains[3:4, :], scatter.total(chunk))
        gain_three = gain_three + gain
        n.grad_row[here, :] += grad
        n.grads_conv[here, :] = n.grad_row[here, :].astype(BF16)
        gather.start(chunk)
    scatter.finish()
    plan.at("back_start")
    gather.wait_near()
    sums = [none, none]

    def batch_rows(slots):
        product = across_product(n.grads_conv[slot_rows(slots, height), :], n.wconv[...])
        for index, slot in enumerate(slots):
            place = span(owner(slot) * height, height)
            normal = n.normal[place, :]
            batch = normal * n.bn_gain[...] + n.bn_bias[...]
            logistic = jax.nn.sigmoid(batch)
            rows = product[index * height : (index + 1) * height]
            grad = rows * (logistic * (1.0 + batch * (1.0 - logistic)))
            n.grad_batch[place, :] = grad
            sums[0] = sums[0] + jnp.sum(grad * normal, axis=0, keepdims=True)
            sums[1] = sums[1] + jnp.sum(grad, axis=0, keepdims=True)

    batch_rows((0, 1))
    plan.at("back_near")
    for chunk in range(CHUNKS):
        gather.pass_on(chunk)
    plan.at("back_passed")
    for chunk in range(CHUNKS):
        gather.wait_last(chunk)
    batch_rows((2, 3))
    swap_back.blocks[0, 0:1, :] = sums[0]
    swap_back.blocks[0, 1:2, :] = sums[1]
    swap_back.start()
    weight_products(n.grad_conv, n.alive, n.grads_conv)
    n.put("grad_conv")
    plan.at("grad_conv")
    swap_back.wait()
    grad_gain, grad_bias = none, none
    for item in in_order(swap_back):
        grad_gain = grad_gain + item[0:1]
        grad_bias = grad_bias + item[1:2]
    n.sum_gain[...] = grad_gain
    n.sum_bias[...] = grad_bias
    gain = n.bn_gain[...]

    def deconvolve(index, nothing):
        here = span(index * block, block)
        real = n.context[here, KERNEL : KERNEL + 1]
        drift = real * (gain * grad_bias + n.normal[here, :] * gain * grad_gain) / real_all
        n.back[pl.ds(pl.multiple_of(EDGE + index * block, EDGE), block), :] = inverse * (
            n.grad_batch[here, :] * gain - drift
        )
        return nothing

    lax.fori_loop(0, frames // block, deconvolve, 0)
    edges_back.start()
    plan.at("edges_back")
    me = lax.axis_index(TP)

    def part(index, carried):
        here = span(index * block, block)
        around = pl.ds(pl.multiple_of(index * block, block), block + 2 * EDGE)
        back, gated = n.back[around, :], n.gated[around, :]
        marks = n.context[here, :]
        own = back[EDGE : EDGE + block]
        grad = jnp.zeros((block, local), F32)
        result = []
        for tap in range(KERNEL):
            first = EDGE - KERNEL // 2 + tap
            mark = marks[:, tap : tap + 1]
            result.append(
                carried[tap] + jnp.sum(gated[first : first + block] * mark * own, axis=0, keepdims=True)
            )
            mirror = KERNEL - 1 - tap
            grad = grad + n.depth[mirror : mirror + 1, :] * back[first : first + block] * mark
        grad = grad * marks[:, KERNEL : KERNEL + 1]
        both = n.paired[here, :]
        logistic = jax.nn.sigmoid(both[:, local:])
        place = lax.div(index * block, height)
        slot = lax.rem(place + me, 2) + 2 * lax.rem(lax.div(place, 2) + lax.div(me, 2), 2)
        rows = span(slot * height + lax.rem(index * block, height), block)
        n.grad_paired[rows, pl.ds(0, local)] = (grad * logistic).astype(BF16)
        n.grad_paired[rows, pl.ds(local, local)] = (
            grad * both[:, :local] * logistic * (1.0 - logistic)
        ).astype(BF16)
        return tuple(result)

    taps = lax.fori_loop(1, last, part, (none,) * KERNEL)
    edges_back.wait()
    plan.at("parts")
    taps = part(last, part(0, taps))
    for tap in range(KERNEL):
        n.depth_sums[tap : tap + 1, :] = taps[tap]
    plan.at("taps")
    scatter.spread(
        lambda slots, cols: across_product(n.grad_paired[slot_rows(slots, height), :], n.wpair[cols, :]), width
    )
    plan.at("back_spread")
    weight_products(n.grad_pair, n.rows_conv, n.grad_paired)
    n.put("grad_pair")
    plan.at("grad_pair")
    gather = gathers[4]
    gain_two = jnp.zeros((1, width), F32)
    for chunk, here in enumerate(chunks):
        grad, gain = norm_back(n.second[here, :], n.gains[2:3, :], scatter.total(chunk))
        gain_two = gain_two + gain
        n.grad_second[here, :] = n.grad_row[here, :] + grad
        n.grads[here, :] = n.grad_second[here, :].astype(BF16)
        gather.start(chunk)
        plan.at(f"back_second{chunk}")
    scatter.finish()
    n.put("grad_second")
    n.gain_sums[0:1, :] = gain_two
    n.gain_sums[1:2, :] = gain_three
    n.gain_sums[2:3, :] = gain_four
    gather.wait_near()

    def mixed_rows(slots):
        product = across_product(n.grads[slot_rows(slots, height), :], n.wattend[...]).astype(BF16)
        for index, slot in enumerate(slots):
            n.grad_mixed[span(owner(slot) * height, height), :] = product[index * height : (index + 1) * height]

    mixed_rows((0, 1))
    for chunk in range(CHUNKS):
        gather.pass_on(chunk)
    plan.at("last_passed")
    for chunk in range(CHUNKS):
        gather.wait_last(chunk)
    mixed_rows((2, 3))
    n.put("grad_mixed")
    weight_products(n.grad_attend, n.mixed_low, n.grads)
    out_sum.end()
    in_sum.end()
    n.put("sum_out", "sum_in")
    plan.finish()
    for item in gathers[:2] + gathers[3:] + [edges, edges_back, swap, swap_back]:
        item.finish()


MIDDLE_PLAN = dict(
    start=(11, 13, 12, 10, 21, 23, 22, 20,),
    spread=(-11, -13,),
    second0=(-12,),
    second1=(-21, -23, -22, 31, 30, 33, ),
    passed=(-31, ),
    edges=(-33, ),
    swapped=(-32, 41, 40, 43, 42, ),
    alive=(-41, ),
    third0=(-43, ),
    first=(-42, ),
    grad_out=(51, 53, 52, 50, ),
    back_start=(-51, ),
    back_near=(-53, ),
    back_passed=(-52, ),
    edges_back=(-61, 62, 60, ),
    parts=(-63, ),
    back_spread=(-62, ),
    edged=(32, ),
    grad_in=(61, 63, ),
)


def run_middle(mixed, opened, gains, depth, bn_gain, bn_bias, shards, out_grad):
    height, width = opened.first.shape
    frames, local = mixed.shape
    count = lax.axis_size(SEQ)
    inner = shards.ffn2_in.shape[1]
    settled = dict(out=(inner, width), **{"in": (width, inner)})
    weights = ("out", "in", "conv", "pair")
    return run_kernel(
        middle_kernel,
        1,
        dict(
            mixed=(mixed, True), first=(opened.first, LOAD), gains=(gains, True), wattend=(opened.full_attend, True),
            context=(opened.context, LOAD), depth=(depth, True), bn_gain=(bn_gain, True), bn_bias=(bn_bias, True),
            out_grad=(out_grad, LOAD), pair_parts=(shards.pair, True), shard_conv=(shards.conv, True),
            shard_in=(shards.ffn2_in, True), shard_out=(shards.ffn2_out, True),
        ),
        dict(
            output=((height, width), BF16, KEEP),
            grad_second=((height, width), F32, KEEP),
            grad_mixed=((frames, local), BF16, KEEP),
            grad_attend=((local, width), BF16, True),
            grad_conv=((local, width), BF16, KEEP),
            grad_pair=((width, 2 * local), BF16, KEEP),
            depth_sums=((8, local), F32, True),
            sum_gain=((1, local), F32, True),
            sum_bias=((1, local), F32, True),
            gain_sums=((8, width), F32, True),
            **{f"sum_{name}": ((tall // count, wide), F32, KEEP) for name, (tall, wide) in settled.items()},
        ),
        dict(
            shard_pair=pltpu.VMEM((width // count, 2 * local), BF16),
            wpair=pltpu.VMEM((width, 2 * local), BF16), wconv=pltpu.VMEM((local, width), BF16),
            win=pltpu.VMEM((width, inner), BF16), wout=pltpu.VMEM((inner, width), BF16),
            second=pltpu.VMEM((height, width), F32), third=pltpu.VMEM((height, width), F32),
            grad_row=pltpu.VMEM((height, width), F32),
            rows_conv=pltpu.VMEM((frames, width), BF16), rows=pltpu.VMEM((frames, width), BF16),
            grads=pltpu.VMEM((frames, width), BF16), grads_conv=pltpu.VMEM((frames, width), BF16),
            hidden=pltpu.VMEM((frames, inner), F32), active=pltpu.VMEM((frames, inner), BF16),
            slope=pltpu.VMEM((frames, inner), BF16),
            mixed_low=pltpu.VMEM((frames, local), BF16), paired=pltpu.VMEM((frames, 2 * local), F32),
            gated=pltpu.VMEM((frames + 2 * EDGE, local), F32), normal=pltpu.VMEM((frames, local), F32),
            alive=pltpu.VMEM((frames, local), BF16), grad_batch=pltpu.VMEM((frames, local), F32),
            back=pltpu.VMEM((frames + 2 * EDGE, local), F32), grad_paired=pltpu.VMEM((frames, 2 * local), BF16),
            **{f"grad_{name}": pltpu.VMEM((tall, wide), BF16) for name, (tall, wide) in settled.items()},
            **{f"t_{name}": settle_scratch(tall // count, wide) for name, (tall, wide) in settled.items()},
            **{f"c_{name}": collect_scratch() for name in weights},
            **{f"g{place}": gather_scratch() for place in range(1, 6)},
            s1=scatter_scratch(height, width),
            edge=edges_scratch(), edge_back=edges_scratch(), swap=swap_scratch(8, local), swap_back=swap_scratch(8, local),
        ),
    )


def close_kernel(n):
    height, width = n.grad_second.shape
    frames = 4 * height
    local = n.grad_query.shape[1]
    seq, count = lax.axis_index(SEQ), lax.axis_size(SEQ)
    half = MAXLEN - frames
    loads = [
        pltpu.make_async_copy(n.full_out, n.wout, n.load.at[0]),
        pltpu.make_async_copy(n.full_hidden, n.hidden, n.load.at[1]),
        pltpu.make_async_copy(n.full_in, n.win, n.load.at[2]),
        pltpu.make_async_copy(n.grad_key.at[pl.ds(MAXLEN, frames), :], n.own_back.at[0], n.load.at[3]),
        pltpu.make_async_copy(n.grad_value.at[pl.ds(MAXLEN, frames), :], n.own_back.at[1], n.load.at[4]),
    ]
    for load in loads:
        load.start()
    attend_sum = Settle(n.grad_attend, n.sum_attend, **n.t_attend)
    conv_sum = Settle(n.grad_conv, n.sum_conv, **n.t_conv)
    pair_sum = Settle(n.grad_pair, n.sum_pair, **n.t_pair)
    project = Settle(n.grad_project, n.sum_project, **n.t_project)
    last = [Settle(n.grad_out, n.sum_out, **n.t_out), Settle(n.grad_in, n.sum_in, **n.t_in)]
    scatter, gather, scatter_two = Scatter(**n.s1), Gather(n.grads, **n.g1), Scatter(**n.s2)
    swap = Swap(**n.swap)
    plan = Plan(
        CLOSE_PLAN, (attend_sum, conv_sum, pair_sum, project, last[0], last[1])
    )
    ready = greet(tp_peers() + seq_peers())
    shifts = (1, -1, 2, -2)
    sources = ((MAXLEN + frames, frames), (MAXLEN - frames, frames), (MAXLEN + 2 * frames, half), (0, half))
    targets = ((0, 0), (1, 0), (2, 0), (2, frames - half))

    def back(kind, which):
        begin, size = sources[kind]
        place, row = targets[kind]
        source = (n.grad_key, n.grad_value)[which].at[pl.ds(begin, size), :]
        target = n.others_back.at[which, place, pl.ds(row, size), :]
        peer = {SEQ: lax.rem(seq + shifts[kind] + count, count)}
        return remote(source, target, n.back_send.at[which, kind], n.back_receive.at[which, kind], peer)

    def there(kind, sending):
        other = seq + shifts[kind] if sending else seq - shifts[kind]
        return (other >= 0) & (other < count)

    for kind in range(4):
        place, row = targets[kind]

        @pl.when(jnp.logical_not(there(kind, False)))
        def _():
            for which in range(2):
                size = sources[kind][1]
                n.others_back[which, place, pl.ds(row, size), :] = jnp.zeros((size, local), BF16)

    ready()
    for kind in range(4):

        @pl.when(there(kind, True))
        def _():
            for which in range(2):
                back(kind, which).start()

    n.wait("grad_query")
    for slot in range(4):
        n.grad_rows[pl.ds(slot * height, height), pl.ds(0, local)] = n.grad_query[span(owner(slot) * height, height), :]
    for kind in range(4):

        @pl.when(there(kind, False))
        def _():
            for which in range(2):
                back(kind, which).wait_recv()

    plan.at("returned")
    loads[3].wait()
    loads[4].wait()
    for slot in range(4):
        place = span(owner(slot) * height, height)
        for which in range(2):
            total = n.own_back[which, place, :].astype(F32)
            for other in range(3):
                total = total + n.others_back[which, other, place, :].astype(F32)
            n.grad_rows[pl.ds(slot * height, height), pl.ds((which + 1) * local, local)] = total.astype(BF16)
    n.wait("wproject")
    scatter.spread(
        lambda slots, cols: across_product(n.grad_rows[slot_rows(slots, height), :], n.wproject[cols, :]), width
    )
    plan.at("spread")
    n.wait("rows_two")
    weight_products(n.grad_project, n.rows_two, n.grad_rows)
    plan.at("grad_project")
    n.wait("first", "grad_second")
    gain_one = jnp.zeros((1, width), F32)
    for chunk in range(CHUNKS):
        here = scatter.rows(chunk)
        grad, gain = norm_back(n.first[here, :], n.gains[1:2, :], scatter.total(chunk))
        gain_one = gain_one + gain
        n.grad_first[here, :] = n.grad_second[here, :] + grad
        n.grads[here, :] = (0.5 * n.grad_first[here, :]).astype(BF16)
        gather.start(chunk)
        plan.at(f"first{chunk}")

    def wait_out():
        loads[0].wait()
        loads[1].wait()

    def products():
        weight_products(n.grad_out, n.active, n.grads)
        plan.at("grad_out")
        n.wait("rows")
        weight_products(n.grad_in, n.rows, n.slope)
        plan.at("grad_in")

    ffn_backward(
        gather, scatter_two, n.win, n.wout, n.hidden, n.active, n.slope, wait_out, loads[2].wait, products, plan.at
    )
    n.wait("values")
    gain_zero = jnp.zeros((1, width), F32)
    for chunk in range(CHUNKS):
        here = scatter.rows(chunk)
        grad, gain = norm_back(n.values[here, :].astype(F32), n.gains[0:1, :], scatter_two.total(chunk))
        gain_zero = gain_zero + gain
        n.input_grad[here, :] = n.grad_first[here, :] + grad
        plan.at(f"zero{chunk}")
    n.small[0, 0:1, :] = gain_zero
    n.small[0, 1:2, :] = gain_one
    n.small[0, 2:5, :] = n.gain_late[0:3, :]
    n.small[0, 5:8, :] = jnp.zeros((3, width), F32)
    near, far = tp_peers()
    hop = remote(n.small.at[0], n.small.at[1], n.small_sem.at[0], n.small_sem.at[1], near)
    hop.start()
    hop.wait_recv()
    n.small[2] = n.small[0] + n.small[1]
    hop_two = remote(n.small.at[2], n.small.at[3], n.small_sem.at[2], n.small_sem.at[3], far)
    hop_two.start()
    hop_two.wait_recv()
    swap.blocks[0, :, pl.ds(0, width)] = n.small[2] + n.small[3]
    swap.blocks[0, :, pl.ds(width, local)] = n.depth_sums[...]
    swap.start()
    plan.at("small")
    n.put("input_grad")
    attend_sum.end()
    conv_sum.end()
    pair_sum.end()
    project.end()
    n.put("sum_attend", "sum_conv", "sum_pair", "sum_project")
    plan.at("ended")
    swap.wait()
    total = jnp.zeros((8, width + local), F32)
    for item in in_order(swap):
        total = total + item
    n.gain_total[...] = total[:5, :width]
    n.depth_total[...] = total[:KERNEL, width:]
    for name, task in zip(("sum_out", "sum_in"), last):
        task.end()
        n.put(name)
    for kind in range(4):

        @pl.when(there(kind, True))
        def _():
            for which in range(2):
                back(kind, which).wait_send()

    hop.wait_send()
    hop_two.wait_send()
    plan.finish()
    for item in [scatter, gather, scatter_two, swap]:
        item.finish()


CLOSE_PLAN = dict(
    returned=(31, 33, 32, 30, 21, 23, 22, 20, 11, 13, 12, 10,),
    spread=(-31,),
    grad_project=(-33, 41, 43, 42, 40,),
    first0=(-32,),
    first1=(-21, -23, -22,),
    first=(-11, -13, -12,),
    grad_out=(-41, -43, 51, 53, 52, 50,),
    grad_in=(-42, 61, 63, 62, 60,),
    second=(-51, -53,),
    zero0=(-52,),
    small=(-61,),
    ended=(-63, -62,),
)


def run_close(values, gains, opened, middle, grad_query, grad_key, grad_value):
    height, width = values.shape
    frames, local = grad_query.shape
    count = lax.axis_size(SEQ)
    inner = opened.full_in.shape[1]
    settled = dict(
        pair=(width, 2 * local), conv=(local, width), attend=(local, width),
        project=(width, 3 * local), out=(inner, width), **{"in": (width, inner)},
    )
    return run_kernel(
        close_kernel,
        4,
        dict(
            values=(values, LOAD), gains=(gains, True), first=(opened.first, LOAD), rows=(opened.rows, LOAD),
            rows_two=(opened.rows_two, LOAD), full_hidden=(opened.hidden, False),
            full_in=(opened.full_in, False), full_out=(opened.full_out, False),
            wproject=(opened.full_project, LOAD), grad_second=(middle.grad_second, LOAD), grad_query=(grad_query, LOAD),
            grad_key=(grad_key, False), grad_value=(grad_value, False), grad_attend=(middle.grad_attend, False),
            grad_conv=(middle.grad_conv, False), grad_pair=(middle.grad_pair, False),
            depth_sums=(middle.depth_sums, True), gain_late=(middle.gain_sums, True),
        ),
        dict(
            input_grad=((height, width), F32, KEEP),
            gain_total=((5, width), F32, True),
            depth_total=((KERNEL, local), F32, True),
            **{f"sum_{name}": ((tall // count, wide), F32, KEEP) for name, (tall, wide) in settled.items()},
        ),
        dict(
            win=pltpu.VMEM((width, inner), BF16), wout=pltpu.VMEM((inner, width), BF16),
            hidden=pltpu.VMEM((frames, inner), F32), active=pltpu.VMEM((frames, inner), BF16),
            slope=pltpu.VMEM((frames, inner), BF16), grads=pltpu.VMEM((frames, width), BF16),
            grad_first=pltpu.VMEM((height, width), F32),
            own_back=pltpu.VMEM((2, frames, local), BF16), others_back=pltpu.VMEM((2, 3, frames, local), BF16),
            grad_rows=pltpu.VMEM((frames, 3 * local), BF16),
            grad_project=pltpu.VMEM((width, 3 * local), BF16),
            grad_in=pltpu.VMEM((width, inner), BF16), grad_out=pltpu.VMEM((inner, width), BF16),
            **{f"t_{name}": settle_scratch(tall // count, wide, name in ("attend", "conv", "pair")) for name, (tall, wide) in settled.items()},
            g1=gather_scratch(), s1=scatter_scratch(height, width), s2=scatter_scratch(height, width),
            swap=swap_scratch(8, width + local),
            small=pltpu.VMEM((4, 8, width), F32), small_sem=pltpu.SemaphoreType.DMA((4,)),
            back_send=pltpu.SemaphoreType.DMA((2, 4)), back_receive=pltpu.SemaphoreType.DMA((2, 4)),
            load=pltpu.SemaphoreType.DMA((5,)),
        ),
    )


def hand_kernel(names, n):
    taken = [pltpu.make_async_copy(n.source[name], n.buffer[name], n.sems.at[0, place]) for place, name in enumerate(names)]
    given = []
    for copy in taken:
        copy.start()
    for place, name in enumerate(names):
        taken[place].wait()
        buffer, target = n.buffer[name], n.target[name]
        if name == "project":
            wide = target.shape[2]
            copies = [
                pltpu.make_async_copy(buffer.at[:, pl.ds(part * wide, wide)], target.at[part], n.sems.at[1 + part, place])
                for part in range(3)
            ]
        elif name == "pair":
            wide = target.shape[2]
            for part in range(2):
                n.apart[:, part, :] = buffer[:, pl.ds(part * wide, wide)]
            copies = [pltpu.make_async_copy(n.apart, target, n.sems.at[1, place])]
        else:
            copies = [pltpu.make_async_copy(buffer, target, n.sems.at[1, place])]
        for copy in copies:
            copy.start()
        given += copies
    for copy in given:
        copy.wait()


def hand_over(arrays):
    names = list(arrays)

    def shape_of(name):
        tall, wide = arrays[name].shape
        return {"project": (3, tall, wide // 3), "pair": (tall, 2, wide // 2)}.get(name, (tall, wide))

    def kernel(*refs):
        count = len(names)
        hand_kernel(
            names,
            SimpleNamespace(
                source=dict(zip(names, refs)),
                target=dict(zip(names, refs[count:])),
                buffer=dict(zip(names, refs[2 * count :])),
                apart=refs[3 * count],
                sems=refs[3 * count + 1],
            ),
        )

    results = pl.pallas_call(
        kernel,
        out_shape=tuple(jax.ShapeDtypeStruct(shape_of(name), arrays[name].dtype) for name in names),
        in_specs=[IN_PLACE] * len(names),
        out_specs=tuple([IN_PLACE] * len(names)),
        scratch_shapes=[pltpu.VMEM(arrays[name].shape, arrays[name].dtype) for name in names]
        + [pltpu.VMEM(shape_of("pair"), F32), pltpu.SemaphoreType.DMA((4, len(names)))],
        compiler_params=pltpu.CompilerParams(vmem_limit_bytes=VMEM_LIMIT),
    )(*arrays.values())
    return SimpleNamespace(**dict(zip(names, results)))


def allowed_block(codes, seg_row, key_begin, query_begin):
    wide = jnp.concatenate([codes] * (QUERY_BLOCK // 128), axis=1)
    place = lax.broadcasted_iota(jnp.int32, (KEY_BLOCK, QUERY_BLOCK), 0) - lax.broadcasted_iota(
        jnp.int32, (KEY_BLOCK, QUERY_BLOCK), 1
    )
    return (wide == seg_row) | (place == query_begin - key_begin)


def head_cols(local):
    return [pl.ds(head * HEAD_DIM, HEAD_DIM) for head in range(local // HEAD_DIM)]


def attend_kernel(bounds, query, keys, values, seg_row, codes, out, totals):
    step = pl.program_id(0)
    heads = head_cols(query.shape[1])
    segs = seg_row[...]

    def one(index, carried):
        here = span(index * KEY_BLOCK, KEY_BLOCK)
        allowed = allowed_block(codes[here, :], segs, index * KEY_BLOCK, MAXLEN + step * QUERY_BLOCK)
        scores = [across_product(keys[here, cols], query[:, cols]) * (SCORE_SCALE * LOG2E) for cols in heads]
        result = []
        for (highest, total, mixed), score, cols in zip(carried, scores, heads):
            score = jnp.where(allowed, score, -1e30)
            top = jnp.maximum(highest, jnp.max(score, axis=0, keepdims=True))
            fade = jnp.exp2(highest - top)
            weights = jnp.exp2(score - top)
            total = total * fade + jnp.sum(weights, axis=0, keepdims=True)
            mixed = mixed * fade + inner_product(values[here, cols], weights.astype(BF16))
            result.append((top, total, mixed))
        return tuple(result)

    start = (
        jnp.full((1, QUERY_BLOCK), -1e30, F32),
        jnp.zeros((1, QUERY_BLOCK), F32),
        jnp.zeros((HEAD_DIM, QUERY_BLOCK), F32),
    )
    ends = lax.fori_loop(bounds[step, 0], bounds[step, 1], one, (start,) * len(heads))
    for head, ((highest, total, mixed), cols) in enumerate(zip(ends, heads)):
        out[:, cols] = jnp.transpose(mixed / total)
        totals[head] = highest + jnp.log2(total)


def attend_back_kernel(
    bounds, query, keys, values, grad, mixed, totals, seg_row, codes, grad_query, key_out, value_out, grad_key, grad_value
):
    step = pl.program_id(0)
    heads = head_cols(query.shape[1])

    @pl.when(step == 0)
    def _():
        grad_key[...] = jnp.zeros_like(grad_key)
        grad_value[...] = jnp.zeros_like(grad_value)

    segs = seg_row[...]
    centres = [
        jnp.sum(jnp.transpose(grad[:, cols].astype(F32) * mixed[:, cols]), axis=0, keepdims=True) for cols in heads
    ]

    def one(index, carried):
        here = span(index * KEY_BLOCK, KEY_BLOCK)
        allowed = allowed_block(codes[here, :], segs, index * KEY_BLOCK, MAXLEN + step * QUERY_BLOCK)
        scores = [across_product(keys[here, cols], query[:, cols]) * (SCORE_SCALE * LOG2E) for cols in heads]
        slopes = [across_product(values[here, cols], grad[:, cols]) for cols in heads]
        result = []
        for head, (total, score, slope, centre, cols) in enumerate(zip(carried, scores, slopes, centres, heads)):
            probs = jnp.where(allowed, jnp.exp2(score - totals[head]), 0.0)
            grad_scores = (probs * (slope - centre) * SCORE_SCALE).astype(BF16)
            grad_value[here, cols] += plain_product(probs.astype(BF16), grad[:, cols])
            grad_key[here, cols] += plain_product(grad_scores, query[:, cols])
            result.append(total + inner_product(grad_scores, keys[here, cols]))
        return tuple(result)

    ends = lax.fori_loop(
        bounds[step, 0], bounds[step, 1], one, (jnp.zeros((QUERY_BLOCK, HEAD_DIM), F32),) * len(heads)
    )
    for total, cols in zip(ends, heads):
        grad_query[:, cols] = total.astype(BF16)

    @pl.when(step == pl.num_programs(0) - 1)
    def _():
        key_out[...] = grad_key[...].astype(BF16)
        value_out[...] = grad_value[...].astype(BF16)


def attend_specs(frames, local, window):
    heads = local // HEAD_DIM
    return dict(
        bounds=pl.BlockSpec(memory_space=pltpu.SMEM),
        rows=pl.BlockSpec((QUERY_BLOCK, local), lambda i: (i, 0)),
        keys=pl.BlockSpec((window, local), lambda i: (0, 0)),
        values=pl.BlockSpec((window, local), lambda i: (0, 1)),
        segs=pl.BlockSpec((1, QUERY_BLOCK), lambda i: (0, i)),
        codes=pl.BlockSpec((window, 128), lambda i: (0, 0)),
        totals=pl.BlockSpec((heads, 1, QUERY_BLOCK), lambda i: (0, 0, i)),
    )


def attend(queries, both, context):
    bounds, seg_row, codes = context
    frames, local = queries.shape
    specs = attend_specs(frames, local, both.shape[0])
    return pl.pallas_call(
        attend_kernel,
        grid=(frames // QUERY_BLOCK,),
        in_specs=[specs[name] for name in ("bounds", "rows", "keys", "values", "segs", "codes")],
        out_specs=[specs["rows"], specs["totals"]],
        out_shape=(
            jax.ShapeDtypeStruct((frames, local), F32),
            jax.ShapeDtypeStruct((local // HEAD_DIM, 1, frames), F32),
        ),
        compiler_params=pltpu.CompilerParams(vmem_limit_bytes=VMEM_LIMIT),
        cost_estimate=pl.CostEstimate(
            flops=4 * frames * MAXLEN * local, bytes_accessed=8 << 20, transcendentals=0
        ),
    )(bounds, queries, both, both, seg_row, codes)


def attend_back(queries, both, grads, mixed, totals, context):
    bounds, seg_row, codes = context
    frames, local = queries.shape
    window = both.shape[0]
    specs = attend_specs(frames, local, window)
    return pl.pallas_call(
        attend_back_kernel,
        grid=(frames // QUERY_BLOCK,),
        in_specs=[
            specs[name]
            for name in ("bounds", "rows", "keys", "values", "rows", "rows", "totals", "segs", "codes")
        ],
        out_specs=[specs["rows"], specs["keys"], specs["keys"]],
        out_shape=(
            jax.ShapeDtypeStruct((frames, local), BF16),
            jax.ShapeDtypeStruct((window, local), BF16),
            jax.ShapeDtypeStruct((window, local), BF16),
        ),
        scratch_shapes=[pltpu.VMEM((window, local), F32), pltpu.VMEM((window, local), F32)],
        compiler_params=pltpu.CompilerParams(vmem_limit_bytes=VMEM_LIMIT),
        cost_estimate=pl.CostEstimate(
            flops=10 * frames * MAXLEN * local, bytes_accessed=16 << 20, transcendentals=0
        ),
    )(bounds, queries, both, both, grads, mixed, totals, seg_row, codes)


def body(
    inputs,
    ln_gains,
    ffn1_in,
    ffn1_out,
    qkv_weight,
    attn_out,
    conv_in,
    conv_depth,
    bn_gain,
    bn_bias,
    conv_out,
    ffn2_in,
    ffn2_out,
    segment_ids,
    pad_mask,
    out_grad,
):
    frames = inputs.shape[0] * lax.axis_size(TP)
    gain_row, bias_row = bn_gain[None, :], bn_bias[None, :]
    shards = SimpleNamespace(
        ffn1_in=ffn1_in,
        ffn1_out=ffn1_out,
        project=jnp.transpose(qkv_weight, (1, 0, 2)),
        attend=attn_out,
        pair=conv_in,
        conv=conv_out,
        ffn2_in=ffn2_in,
        ffn2_out=ffn2_out,
    )
    opened = run_open(
        inputs, ln_gains, shards, segment_ids.reshape(-1, 128), pad_mask.reshape(-1, 128)
    )
    seg_row = lax.dynamic_slice_in_dim(segment_ids, lax.axis_index(SEQ) * frames, frames)[None, :]
    context = (opened.bounds, seg_row, opened.codes)
    mixed, totals = attend(opened.queries, opened.window, context)
    middle = run_middle(mixed, opened, ln_gains, conv_depth, gain_row, bias_row, shards, out_grad)
    grad_query, grad_key, grad_value = attend_back(
        opened.queries, opened.window, middle.grad_mixed, mixed, totals, context
    )
    closed = run_close(inputs, ln_gains, opened, middle, grad_query, grad_key, grad_value)
    given = hand_over(
        dict(
            output=middle.output,
            input_grad=closed.input_grad,
            gains=closed.gain_total,
            first_in=closed.sum_in,
            first_out=closed.sum_out,
            project=closed.sum_project,
            attend=closed.sum_attend,
            pair=closed.sum_pair,
            depth=closed.depth_total,
            gain=middle.sum_gain,
            bias=middle.sum_bias,
            conv=closed.sum_conv,
            second_in=middle.sum_in,
            second_out=middle.sum_out,
        )
    )
    return (
        given.output,
        given.input_grad,
        given.gains,
        given.first_in,
        given.first_out,
        jnp.transpose(given.project, (1, 0, 2)),
        given.attend,
        given.pair,
        given.depth,
        given.gain[0],
        given.bias[0],
        given.conv,
        given.second_in,
        given.second_out,
    )


def solution(mesh):
    return jax.shard_map(
        body,
        mesh=mesh,
        in_specs=(
            P((SEQ, TP), None),
            P(),
            P(SEQ, TP),
            P((TP, SEQ), None),
            P(SEQ, None, TP),
            P((TP, SEQ), None),
            P(SEQ, None, TP),
            P(None, TP),
            P(TP),
            P(TP),
            P((TP, SEQ), None),
            P(SEQ, TP),
            P((TP, SEQ), None),
            P(),
            P(),
            P((SEQ, TP), None),
        ),
        out_specs=(
            P((SEQ, TP), None),
            P((SEQ, TP), None),
            P(),
            P(SEQ, TP),
            P((TP, SEQ), None),
            P(SEQ, None, TP),
            P((TP, SEQ), None),
            P(SEQ, None, TP),
            P(None, TP),
            P(TP),
            P(TP),
            P((TP, SEQ), None),
            P(SEQ, TP),
            P((TP, SEQ), None),
        ),
        check_vma=False,
    )
```
